512 devices in a mesh: sec: 4 (over x_lo, core), tile: 128 (over x_hi, y, z).
Axes of the slice: x: 4 (x_hi: 2, x_lo: 2; x = x_hi * 2 + x_lo), y: 4, z: 16, core: 2. Of those that a mesh axis runs over, the one named last changes fastest.
Arguments:
- ocean_u: float32 [64, 262144], P(None, ('sec', 'tile')), may hold values from -2 to 2
- ocean_b: float32 [64, 262144], P(None, ('sec', 'tile')), may hold values from -4 to 4
- tracers: bfloat16 [17, 64, 196608], P(None, None, ('sec', 'tile')), may hold values from 0.099609375 to 2
- wet_tiles: int32 [1536], replicated, may hold values from 0 to 2047, as said below
- kinetic_matrix: float32 [17, 17], replicated, may hold values from -0.42 to 1.5
Outputs:
- tracers_out: bfloat16 [17, 64, 196608], P(None, None, ('sec', 'tile'))
- ocean_u_out: float32 [64, 262144], P(None, ('sec', 'tile'))
- ocean_b_out: float32 [64, 262144], P(None, ('sec', 'tile'))
The draws below stay inside these ranges and needn't reach their ends.
Inputs may be any that keep to these rules, and one draw needn't show every extreme that they name: `wet_tiles`: increasing tile numbers. For every k, of the tiles k * 4 to k * 4 + 3 either 2 or 4 are listed, and for every even k the tiles of k and k + 1 hold 6 listed tiles together.
All inputs are finite; a program needn't handle non-finite values.
Results may differ from the reference program's by a relative error of at most 0.001.
Values sent between devices are 32-bit elements; how exact they have to be, the bound alone decides.
A program may use at most 64 MiB of HBM per device.

```python
import jax
import jax.numpy as jnp
from jax import lax

LEVELS = 64
TRACERS = 17
TILE_COLS = 128
STEPS = 2
WET = 1536
TILES = 2048
NCOL = 262144
WCOL = 196608


def draw_wet_tiles(key, part):
    devices = TILES // 4
    pair_key = jax.random.fold_in(key, 11)
    rank_key = jax.random.fold_in(key, 12)
    heavier = jax.random.randint(pair_key, (devices // 2,), 0, 2)
    counts = jnp.stack([2 + 2 * heavier, 4 - 2 * heavier], axis=1).reshape(devices)
    scores = jax.random.randint(rank_key, (devices, 4), 0, 1 << 20) * 4 + jnp.arange(4)[None, :]
    ranking = jnp.argsort(jnp.argsort(scores, axis=1), axis=1)
    wet_flags = (ranking < counts[:, None]).reshape(TILES)
    sort_keys = jnp.where(wet_flags, 0, TILES) + jnp.arange(TILES)
    ordering = jnp.argsort(sort_keys)
    return ordering[:WET].astype(jnp.int32)


def draw_kinetic_matrix(key, part):
    lead_key = jax.random.fold_in(key, 21)
    rest_key = jax.random.fold_in(key, 22)
    lead_row = jax.random.uniform(lead_key, (1, TRACERS), jnp.float32, 1.0, 1.5)
    rest_rows = jax.random.uniform(rest_key, (TRACERS - 1, TRACERS), jnp.float32, -0.42, 0.42)
    return jnp.concatenate([lead_row, rest_rows], axis=0)


def levels(rng, extent, split, low, high):
    def one(axis_at, blocks):
        draws = jax.random.uniform(jax.random.fold_in(jax.random.fold_in(rng, 6), axis_at), (blocks,), jnp.float32, low / len(split), high / len(split))
        return jnp.repeat(jnp.exp(draws), extent[axis_at] // blocks).reshape((-1,) + (1,) * (len(extent) - axis_at - 1))

    factor_of = one(*split[0])
    for cut in split[1:]:
        factor_of = factor_of * one(*cut)
    return factor_of


def centred(rng, shape, width, limit, pieces=(), dtype=jnp.bfloat16):
    result = jax.random.normal(rng, shape, jnp.float32) * width
    if len(pieces) > 0:
        result = levels(rng, shape, pieces, -0.22, 0.18) * result
    return jnp.clip(result, min=-limit, max=limit).astype(dtype)


def setup_inputs(seed: int = 0) -> dict:
    key_of = jax.random.split(jax.random.key(seed), 6)
    ocean_u = centred(key_of[0], (LEVELS, NCOL), 0.5, 2.0, ((1, 512),), jnp.float32)
    ocean_b = centred(key_of[1], (LEVELS, NCOL), 1.0, 4.0, ((1, 512),), jnp.float32)
    tracers = jnp.clip(0.099609375 + 1.9003906 * jax.random.uniform(key_of[2], (TRACERS, LEVELS, WCOL), jnp.float32) ** levels(key_of[2], (TRACERS, LEVELS, WCOL), ((2, 512),), -0.2, 0.2), 0.099609375, 2.0).astype(jnp.bfloat16)
    wet_tiles = draw_wet_tiles(jax.random.fold_in(key_of[5], 71), 0)
    kinetic_matrix = draw_kinetic_matrix(jax.random.fold_in(key_of[5], 71), 0)
    return {"ocean_u": ocean_u, "ocean_b": ocean_b, "tracers": tracers, "wet_tiles": wet_tiles, "kinetic_matrix": kinetic_matrix}


DT_OCEAN = 0.25
PRESSURE = 1.0
HORIZ_VISC = 0.2
VERT_VISC = 0.2
HEATING = 0.2
KAPPA_BASE = 0.05
KAPPA_SPAN = 0.35
DT_TRACER = 0.3
DT_MIX = 1.0
KINETIC_DELTA = 0.5
SURFACE_LIGHT = 10.0
WATER_ATT = 0.04
PIGMENT_ATT = 0.08
GROWTH = 0.05
THERMAL_GAIN = 0.1


def vertical_term(field):
    upper_cells = jnp.concatenate([field[:1], field[:-1]], axis=0)
    lower_cells = jnp.concatenate([field[1:], field[-1:]], axis=0)
    return upper_cells + lower_cells - 2.0 * field


def ocean_core(vel_ext, buoy_ext):
    velocity = vel_ext[:, 1:-1]
    buoyancy = buoy_ext[:, 1:-1]
    horiz_term = vel_ext[:, :-2] + vel_ext[:, 2:] - 2.0 * velocity
    press_term = buoy_ext[:, 2:] - buoyancy
    updated = velocity + DT_OCEAN * (HORIZ_VISC * horiz_term + VERT_VISC * vertical_term(velocity) - PRESSURE * press_term)
    return updated, buoyancy


def diffusivity_of(velocity, buoyancy):
    shear_sq = (velocity[:-1] - velocity[1:]) ** 2
    stratified = buoyancy[:-1] - buoyancy[1:]
    interior = KAPPA_BASE + KAPPA_SPAN * jax.nn.sigmoid(4.0 * (shear_sq - stratified))
    return jnp.concatenate([interior, jnp.zeros_like(interior[:1])], axis=0)


def absorption_of(tracer_state):
    pigment = tracer_state[0]
    attenuation = WATER_ATT + PIGMENT_ATT * pigment * pigment
    optical_depth = jnp.cumsum(attenuation, axis=0)
    return SURFACE_LIGHT * (jnp.exp(attenuation - optical_depth) - jnp.exp(-optical_depth))


def profile_change(transported_solutes, turbulent_spreading, seawater_warmth, captured_radiance, kinetic_matrix):
    lower_cells = jnp.concatenate([transported_solutes[:, 1:], transported_solutes[:, -1:]], axis=1)
    vert_flux = turbulent_spreading[None] * (lower_cells - transported_solutes)
    upper_flux = jnp.concatenate([jnp.zeros_like(vert_flux[:, :1]), vert_flux[:, :-1]], axis=1)
    depth_blended_fields = transported_solutes + DT_MIX * (vert_flux - upper_flux)
    kinetic_drift = jnp.einsum("ij,jlc->ilc", kinetic_matrix, depth_blended_fields, precision=lax.Precision.HIGHEST)
    converted_solutes = depth_blended_fields + KINETIC_DELTA * jnp.exp(THERMAL_GAIN * seawater_warmth)[None] * kinetic_drift
    return jnp.concatenate([converted_solutes[:1] + GROWTH * captured_radiance[None], converted_solutes[1:]], axis=0)


def wrap_columns(field):
    return jnp.concatenate([field[:, -1:], field, field[:, :1]], axis=1)


def reference(ocean_u, ocean_b, tracers, wet_tiles, kinetic_matrix):
    following = jnp.roll(wet_tiles, -1)
    adjacent = (jnp.mod(following - wet_tiles, TILES) == 1).astype(jnp.float32)
    face_open = jnp.ones((WET, TILE_COLS), jnp.float32).at[:, TILE_COLS - 1].set(adjacent).reshape(WCOL)
    tracer_state = tracers.astype(jnp.float32)
    velocity = ocean_u
    buoyancy = ocean_b
    for step_index in range(STEPS):
        captured_radiance = absorption_of(tracer_state)
        heating_term = jnp.zeros((LEVELS, TILES, TILE_COLS), jnp.float32).at[:, wet_tiles].set(captured_radiance.reshape(LEVELS, WET, TILE_COLS)).reshape(LEVELS, NCOL)
        buoyancy = buoyancy + HEATING * heating_term
        velocity, buoyancy = ocean_core(wrap_columns(velocity), wrap_columns(buoyancy))
        turbulent_spreading = diffusivity_of(velocity, buoyancy)
        stacked = jnp.stack([velocity, turbulent_spreading, buoyancy]).reshape(3, LEVELS, TILES, TILE_COLS)
        coupled = stacked[:, :, wet_tiles].reshape(3, LEVELS, WCOL)
        face_u = coupled[0]
        following_state = jnp.roll(tracer_state, -1, axis=2)
        face_flux = (jnp.maximum(face_u, 0.0) * tracer_state + jnp.minimum(face_u, 0.0) * following_state) * face_open
        transported_solutes = tracer_state - DT_TRACER * (face_flux - jnp.roll(face_flux, 1, axis=2))
        tracer_state = profile_change(transported_solutes, coupled[1], coupled[2], captured_radiance, kinetic_matrix)
    return tracer_state.astype(jnp.bfloat16), velocity, buoyancy
```

```python
import functools

import jax
import jax.numpy as jnp
from jax import lax
from jax.experimental import pallas as pl
from jax.experimental.pallas import tpu as pltpu
from jax.sharding import PartitionSpec as P

MESH = pl.DeviceIdType.MESH
LANES = 128
STEPS = 2
WET_DEV = 3
OCEAN_DEV = 4
HALO = 3

DT_OCEAN = 0.25
PRESSURE = 1.0
HORIZ_VISC = 0.2
VERT_VISC = 0.2
HEATING = 0.2
KAPPA_BASE = 0.05
KAPPA_SPAN = 0.35
DT_TRACER = 0.3
DT_MIX = 1.0
KINETIC_DELTA = 0.5
SURFACE_LIGHT = 10.0
WATER_ATT = 0.04
PIGMENT_ATT = 0.08
GROWTH = 0.05
THERMAL_GAIN = 0.1


def roll(x, shift, axis):
    size = x.shape[axis]
    shift = shift % size
    return x if shift == 0 else pltpu.roll(x, shift, axis)


def iota(shape, axis):
    return lax.broadcasted_iota(jnp.int32, shape, axis)


def pick(position, options):
    value = None
    for where, option in options:
        value = option if value is None else jnp.where(position == where, option, value)
    return value


def kernel(
    secs, tiles, u_in, b_in, t_in, wet_in, k_in,
    t_out, u_out, b_out,
    u_v, b_v, t_v, k_v, wet_s, to_left, to_right, from_left, from_right, far_in, far_back,
    s_v, mix_v, abs_v, coef, out_v, ub_out, load_sem, wet_sem, send_sem, recv_sem, store_sem,
):
    levels = u_in.shape[0]
    tracers = t_in.shape[0]
    padded = mix_v.shape[0]
    total_wet = WET_DEV * secs * tiles
    total_tiles = OCEAN_DEV * secs * tiles
    own = OCEAN_DEV * LANES
    slots = WET_DEV * LANES
    sec = lax.axis_index("sec")
    tile = lax.axis_index("tile")
    device = sec * tiles + tile
    right_flat = lax.rem(device + 1, secs * tiles)
    left_flat = lax.rem(device + secs * tiles - 1, secs * tiles)
    right = (right_flat // tiles, lax.rem(right_flat, tiles))
    left = (left_flat // tiles, lax.rem(left_flat, tiles))
    odd = lax.rem(tile, 2)
    partner = (sec, tile + 1 - 2 * odd)
    even_lane = odd == 0

    barrier = pltpu.get_barrier_semaphore()
    for neighbour in (left, right):
        pl.semaphore_signal(barrier, inc=1, device_id=neighbour, device_id_type=MESH)

    loads = [
        pltpu.make_async_copy(t_in, t_v, load_sem.at[0]),
        pltpu.make_async_copy(u_in, u_v.at[:, pl.ds(0, own)], load_sem.at[1]),
        pltpu.make_async_copy(b_in, b_v.at[:, pl.ds(0, own)], load_sem.at[2]),
        pltpu.make_async_copy(k_in, k_v, load_sem.at[3]),
        pltpu.make_async_copy(wet_in, wet_s, wet_sem),
    ]
    for load in loads:
        load.start()

    def remote(src, dst, index, target):
        return pltpu.make_async_remote_copy(
            src_ref=src, dst_ref=dst, send_sem=send_sem.at[index], recv_sem=recv_sem.at[index],
            device_id=target, device_id_type=MESH,
        )

    edge = pl.ds(pl.multiple_of((own - LANES) * (1 - odd), LANES), LANES)
    far_u = remote(u_in.at[:, edge], far_in.at[0], 2, partner)
    far_b = remote(b_in.at[:, edge], far_in.at[1], 3, partner)

    lane = iota((levels, LANES), 1)
    loads[0].wait()
    first = jnp.zeros((levels, LANES), jnp.float32)
    last = jnp.zeros((levels, LANES), jnp.float32)
    for t in range(tracers):
        here = (lane >= 2 * t) & (lane < 2 * t + 2)
        head = t_v[t, :, :LANES].astype(jnp.float32)
        tail = t_v[t, :, slots - LANES :].astype(jnp.float32)
        first = jnp.where(here, roll(head, 2 * t, 1), first)
        last = jnp.where(here, roll(tail, 2 * t + 2, 1), last)
    loads[1].wait()
    loads[2].wait()
    base = 2 * tracers
    for field, offset in ((u_v, base), (b_v, base + HALO)):
        here = (lane >= offset) & (lane < offset + HALO)
        head = jnp.where(even_lane, field[:, :LANES], field[:, LANES : 2 * LANES])
        tail = jnp.where(even_lane, field[:, 2 * LANES : 3 * LANES], field[:, 3 * LANES : own])
        first = jnp.where(here, roll(head, offset, 1), first)
        last = jnp.where(here, roll(tail, offset + HALO, 1), last)
    to_left[...] = first
    to_right[...] = last

    pl.semaphore_wait(barrier, 2)
    near_left = remote(to_left, from_right, 0, left)
    near_right = remote(to_right, from_left, 1, right)
    near_left.start()
    near_right.start()
    far_u.start()
    far_b.start()

    loads[3].wait()
    rows = 8 * padded
    spread = ((iota((rows, tracers), 0) >> 3) == iota((rows, tracers), 1)).astype(jnp.float32)
    wide = 3 * rows
    column = iota((tracers, wide), 1)
    column = jnp.where(column >= 2 * rows, column - 2 * rows, jnp.where(column >= rows, column - rows, column))
    gather = ((column >> 3) == iota((tracers, wide), 0)).astype(jnp.float32)
    exact = functools.partial(
        jnp.dot, precision=lax.Precision.HIGHEST, preferred_element_type=jnp.float32
    )
    matrix = exact(exact(spread, k_v[...]), gather)
    same = (iota((rows, wide), 0) & 7) == (iota((rows, wide), 1) & 7)
    matrix = jnp.where(same, matrix, 0.0)
    coarse = matrix.astype(jnp.bfloat16)
    fine = (matrix - coarse.astype(jnp.float32)).astype(jnp.bfloat16)
    matrix = jnp.where(iota((rows, wide), 1) < 2 * rows, coarse.astype(jnp.float32), fine.astype(jnp.float32)).astype(jnp.bfloat16)
    mix_v[tracers, :, :] = jnp.zeros(mix_v.shape[1:], jnp.float32)

    for t in range(tracers):
        s_v[t, :, :slots] = t_v[t].astype(jnp.float32)

    loads[4].wait()
    listed = [
        wet_s[lax.rem(device * WET_DEV + total_wet + j, total_wet)] for j in range(-1, WET_DEV + 1)
    ]
    ring = OCEAN_DEV + 2
    relative = [lax.rem(w - device * OCEAN_DEV + total_tiles + 2, total_tiles) - 2 for w in listed]
    position = [
        jnp.where(r < 0, r + ring, jnp.where(r < ring, r, ring)) for r in relative
    ]
    is_open = [
        lax.rem(listed[j + 1] - listed[j] + total_tiles, total_tiles) == 1 for j in range(WET_DEV + 1)
    ]
    spot_left, spot, spot_right = position[0], position[1 : WET_DEV + 1], position[WET_DEV + 1]

    tri = (iota((levels, levels), 0) >= iota((levels, levels), 1)).astype(jnp.float32)

    def absorb(width, start):
        pigment = s_v[0, :, start : start + width]
        attenuation = WATER_ATT + PIGMENT_ATT * pigment * pigment
        depth = exact(tri, attenuation)
        below = jnp.exp(-depth)
        above = jnp.where(iota((levels, width), 0) == 0, 1.0, roll(below, 1, 0))
        abs_v[:, start : start + width] = SURFACE_LIGHT * (above - below)

    absorb(slots, 0)

    near_left.wait()
    near_right.wait()
    for t in range(tracers):
        after = roll(from_right[...], -2 * t, 1)
        before = roll(from_left[...], -2 - 2 * t, 1)
        s_v[t, :, slots:] = jnp.where(lane < 2, after, jnp.where(lane >= LANES - 2, before, 0.0))
    absorb(LANES, slots)
    far_u.wait()
    far_b.wait()
    for field, offset, far in ((u_v, base, far_in[0]), (b_v, base + HALO, far_in[1])):
        after = roll(from_right[...], -offset, 1)
        before = roll(from_left[...], -HALO - offset, 1)
        near = jnp.where(lane < HALO, after, jnp.where(lane >= LANES - HALO, before, 0.0))
        field[:, own : own + LANES] = jnp.where(even_lane, far, near)
        field[:, own + LANES :] = jnp.where(even_lane, near, far)

    final = None
    for step in range(STEPS):
        width = slots + LANES if step < STEPS - 1 else slots
        light = [abs_v[:, j * LANES : (j + 1) * LANES] for j in range(WET_DEV + 1)]
        heat = []
        for q in range(ring):
            at_halo = jnp.where(lane < LANES // 2, spot_right, spot_left) == q
            term = jnp.where(at_halo, light[WET_DEV], 0.0)
            for j in range(WET_DEV):
                term = jnp.where(spot[j] == q, light[j], term)
            heat.append(term)
        buoyancy = b_v[...] + HEATING * jnp.concatenate(heat, axis=1)
        b_v[...] = buoyancy
        velocity = u_v[...]
        level = iota(velocity.shape, 0)
        horiz = roll(velocity, 1, 1) + roll(velocity, -1, 1) - 2.0 * velocity
        press = roll(buoyancy, -1, 1) - buoyancy
        upper = jnp.where(level == 0, velocity, roll(velocity, 1, 0))
        lower = jnp.where(level == levels - 1, velocity, roll(velocity, -1, 0))
        vert = upper + lower - 2.0 * velocity
        u_v[...] = velocity + DT_OCEAN * (
            HORIZ_VISC * horiz + VERT_VISC * vert - PRESSURE * press
        )
        if step == STEPS - 1:
            place = pl.ds(pl.multiple_of(own + LANES * odd, LANES), LANES)
            final = (
                remote(u_v.at[:, place], far_back.at[0], 4, partner),
                remote(b_v.at[:, place], far_back.at[1], 5, partner),
            )
            for copy in final:
                copy.start()
        taken = []
        for field in (u_v, b_v):
            part = [field[:, q * LANES : (q + 1) * LANES] for q in range(ring)]
            chosen = [
                pick(spot[0], [(0, part[0]), (1, part[1]), (2, part[2]), (5, part[5])]),
                pick(spot[1], [(0, part[0]), (1, part[1]), (2, part[2]), (3, part[3])]),
                pick(spot[2], [(1, part[1]), (2, part[2]), (3, part[3]), (4, part[4])]),
            ]
            ahead = pick(spot_right, [(3, part[3]), (4, part[4]), (5, part[5])])
            behind = pick(spot_left, [(0, part[0]), (4, part[4]), (5, part[5])])
            chosen.append(jnp.where(lane < LANES // 2, ahead, behind))
            taken.append(jnp.concatenate(chosen, axis=1))
        face_u, warmth = taken
        level = iota(face_u.shape, 0)
        shear = face_u - roll(face_u, -1, 0)
        stratified = warmth - roll(warmth, -1, 0)
        steep = 4.0 * (shear * shear - stratified)
        spreading = KAPPA_BASE + KAPPA_SPAN / (1.0 + jnp.exp(-steep))
        spreading = jnp.where(level == levels - 1, 0.0, spreading)
        spreading_up = jnp.where(level == 0, 0.0, roll(spreading, 1, 0))
        gates = []
        for j in range(WET_DEV + 1):
            ends = is_open[(j + 1) % (WET_DEV + 1)].astype(jnp.float32)
            gates.append(jnp.where(lane == LANES - 1, ends, 1.0))
        gate = DT_TRACER * jnp.concatenate(gates, axis=1)
        forward = jnp.maximum(face_u, 0.0) * gate
        backward = jnp.minimum(face_u, 0.0) * gate
        forward_in = roll(forward, 1, 1)
        coef[0] = 1.0 - forward + roll(backward, 1, 1)
        coef[1] = -backward
        coef[2] = forward_in
        coef[3] = 1.0 - DT_MIX * (spreading + spreading_up)
        coef[4] = DT_MIX * spreading
        coef[5] = DT_MIX * spreading_up
        coef[6] = KINETIC_DELTA * jnp.exp(THERMAL_GAIN * warmth)

        for t in range(tracers):
            state = s_v[t]
            moved = (
                coef[0] * state + coef[1] * roll(state, -1, 1) + coef[2] * roll(state, 1, 1)
            )[:, :width]
            mixed = (
                coef[3][:, :width] * moved
                + coef[4][:, :width] * roll(moved, -1, 0)
                + coef[5][:, :width] * roll(moved, 1, 0)
            )
            mix_v[t, :, :width] = mixed

        for group in range(levels // 16):
            halves = []
            for half in range(2):
                level = slice(group * 16 + half * 8, group * 16 + half * 8 + 8)
                mixed = mix_v[:, level, :width]
                flat = mixed.reshape(rows, width)
                high = flat.astype(jnp.bfloat16)
                low = (flat - high.astype(jnp.float32)).astype(jnp.bfloat16)
                drift = jnp.dot(
                    matrix, jnp.concatenate([high, low, high], axis=0),
                    preferred_element_type=jnp.float32,
                ).reshape(padded, 8, width)
                grown = mixed + coef[6, level, :width][None] * drift
                grown_first = grown[0] + GROWTH * abs_v[level, :width]
                grown = jnp.concatenate([grown_first[None], grown[1:tracers]], axis=0)
                if step < STEPS - 1:
                    s_v[:, level, :width] = grown
                halves.append(grown)
            if step == STEPS - 1:
                level = slice(group * 16, group * 16 + 16)
                out_v[:, level, :] = jnp.concatenate(halves, axis=1).astype(jnp.bfloat16)
        if step < STEPS - 1:
            absorb(width, 0)

    store_t = pltpu.make_async_copy(out_v, t_out, store_sem.at[0])
    store_t.start()
    for copy in final:
        copy.wait()
    for field, index in ((u_v, 0), (b_v, 1)):
        back = far_back[index]
        low_given = jnp.logical_and(odd == 1, spot_left == 0)
        high_given = jnp.logical_and(odd == 0, spot_right == OCEAN_DEV - 1)
        ub_out[index, :, :LANES] = jnp.where(low_given, back, field[:, :LANES])
        ub_out[index, :, LANES : own - LANES] = field[:, LANES : own - LANES]
        ub_out[index, :, own - LANES :] = jnp.where(high_given, back, field[:, own - LANES : own])
    store_u = pltpu.make_async_copy(ub_out.at[0], u_out, store_sem.at[1])
    store_b = pltpu.make_async_copy(ub_out.at[1], b_out, store_sem.at[2])
    store_u.start()
    store_b.start()
    store_t.wait()
    store_u.wait()
    store_b.wait()


def on_device(ocean_u, ocean_b, tracers, wet_tiles, kinetic_matrix):
    levels, own = ocean_u.shape
    count, _, slots = tracers.shape
    padded = count + count % 2
    wide = slots + LANES
    domain = own + 2 * LANES
    f32 = jnp.float32
    anywhere = pl.BlockSpec(memory_space=pl.ANY)
    return pl.pallas_call(
        functools.partial(kernel, lax.axis_size("sec"), lax.axis_size("tile")),
        out_shape=(
            jax.ShapeDtypeStruct(tracers.shape, jnp.bfloat16),
            jax.ShapeDtypeStruct(ocean_u.shape, f32),
            jax.ShapeDtypeStruct(ocean_b.shape, f32),
        ),
        in_specs=[anywhere] * 5,
        out_specs=(anywhere,) * 3,
        scratch_shapes=[
            pltpu.VMEM((levels, domain), f32),
            pltpu.VMEM((levels, domain), f32),
            pltpu.VMEM(tracers.shape, jnp.bfloat16),
            pltpu.VMEM(kinetic_matrix.shape, f32),
            pltpu.SMEM(wet_tiles.shape, jnp.int32),
            pltpu.VMEM((levels, LANES), f32),
            pltpu.VMEM((levels, LANES), f32),
            pltpu.VMEM((levels, LANES), f32),
            pltpu.VMEM((levels, LANES), f32),
            pltpu.VMEM((2, levels, LANES), f32),
            pltpu.VMEM((2, levels, LANES), f32),
            pltpu.VMEM((count, levels, wide), f32),
            pltpu.VMEM((padded, levels, wide), f32),
            pltpu.VMEM((levels, wide), f32),
            pltpu.VMEM((7, levels, wide), f32),
            pltpu.VMEM(tracers.shape, jnp.bfloat16),
            pltpu.VMEM((2, levels, own), f32),
            pltpu.SemaphoreType.DMA((4,)),
            pltpu.SemaphoreType.DMA,
            pltpu.SemaphoreType.DMA((6,)),
            pltpu.SemaphoreType.DMA((6,)),
            pltpu.SemaphoreType.DMA((3,)),
        ],
        compiler_params=pltpu.CompilerParams(
            collective_id=0, has_side_effects=True, vmem_limit_bytes=48 * 2**20
        ),
    )(ocean_u, ocean_b, tracers, wet_tiles, kinetic_matrix)


def solution(mesh):
    flat = ("sec", "tile")
    placed = (P(None, flat), P(None, flat), P(None, None, flat), P(), P())
    return jax.shard_map(
        on_device,
        mesh=mesh,
        in_specs=placed,
        out_specs=(P(None, None, flat), P(None, flat), P(None, flat)),
        check_vma=False,
    )
```

```python
import functools

import jax
import jax.numpy as jnp
from jax import lax
from jax.experimental import pallas as pl
from jax.experimental.pallas import tpu as pltpu
from jax.sharding import PartitionSpec as P

MESH = pl.DeviceIdType.MESH
LANES = 128
STEPS = 2
WET_DEV = 3
OCEAN_DEV = 4
HALO = 3

DT_OCEAN = 0.25
PRESSURE = 1.0
HORIZ_VISC = 0.2
VERT_VISC = 0.2
HEATING = 0.2
KAPPA_BASE = 0.05
KAPPA_SPAN = 0.35
DT_TRACER = 0.3
DT_MIX = 1.0
KINETIC_DELTA = 0.5
SURFACE_LIGHT = 10.0
WATER_ATT = 0.04
PIGMENT_ATT = 0.08
GROWTH = 0.05
THERMAL_GAIN = 0.1


def roll(x, shift, axis):
    size = x.shape[axis]
    shift = shift % size
    return x if shift == 0 else pltpu.roll(x, shift, axis)


def iota(shape, axis):
    return lax.broadcasted_iota(jnp.int32, shape, axis)


def pick(position, options):
    value = None
    for where, option in options:
        value = option if value is None else jnp.where(position == where, option, value)
    return value


def exact(a, b):
    return jnp.dot(a, b, precision=lax.Precision.HIGHEST, preferred_element_type=jnp.float32)


def absorbed_light(pigment, tri):
    attenuation = WATER_ATT + PIGMENT_ATT * pigment * pigment
    below = jnp.exp(-exact(tri, attenuation))
    above = jnp.where(iota(pigment.shape, 0) == 0, 1.0, roll(below, 1, 0))
    return SURFACE_LIGHT * (above - below)


def advance_velocity(velocity, buoyancy):
    level = iota(velocity.shape, 0)
    horiz = roll(velocity, 1, 1) + roll(velocity, -1, 1) - 2.0 * velocity
    press = roll(buoyancy, -1, 1) - buoyancy
    upper = jnp.where(level == 0, velocity, roll(velocity, 1, 0))
    lower = jnp.where(level == velocity.shape[0] - 1, velocity, roll(velocity, -1, 0))
    vert = upper + lower - 2.0 * velocity
    return velocity + DT_OCEAN * (HORIZ_VISC * horiz + VERT_VISC * vert - PRESSURE * press)


def set_coefficients(coef, face_u, warmth, gate):
    level = iota(face_u.shape, 0)
    shear = face_u - roll(face_u, -1, 0)
    stratified = warmth - roll(warmth, -1, 0)
    steep = 4.0 * (shear * shear - stratified)
    spreading = KAPPA_BASE + KAPPA_SPAN / (1.0 + jnp.exp(-steep))
    spreading = jnp.where(level == face_u.shape[0] - 1, 0.0, spreading)
    spreading_up = jnp.where(level == 0, 0.0, roll(spreading, 1, 0))
    gate = DT_TRACER * gate
    forward = jnp.maximum(face_u, 0.0) * gate
    backward = jnp.minimum(face_u, 0.0) * gate
    coef[0] = 1.0 - forward + roll(backward, 1, 1)
    coef[1] = -backward
    coef[2] = roll(forward, 1, 1)
    coef[3] = 1.0 - DT_MIX * (spreading + spreading_up)
    coef[4] = DT_MIX * spreading
    coef[5] = DT_MIX * spreading_up
    coef[6] = KINETIC_DELTA * jnp.exp(THERMAL_GAIN * warmth)


def transport(state, coef, width):
    moved = (coef[0] * state + coef[1] * roll(state, -1, 1) + coef[2] * roll(state, 1, 1))[:, :width]
    return (
        coef[3][:, :width] * moved
        + coef[4][:, :width] * roll(moved, -1, 0)
        + coef[5][:, :width] * roll(moved, 1, 0)
    )


def react(mixed, warm, light, matrix, tracers):
    padded, rows, width = mixed.shape
    flat = mixed.reshape(padded * rows, width)
    high = flat.astype(jnp.bfloat16)
    low = (flat - high.astype(jnp.float32)).astype(jnp.bfloat16)
    drift = jnp.dot(
        matrix, jnp.concatenate([high, low, high], axis=0), preferred_element_type=jnp.float32
    ).reshape(padded, rows, width)
    grown = mixed + warm[None] * drift
    return jnp.concatenate([(grown[0] + GROWTH * light)[None], grown[1:tracers]], axis=0)


def kernel(
    secs, tiles, u_in, b_in, t_in, wet_in, k_in,
    out_v, ub_out,
    u_v, b_v, t_v, k_v, wet_s, edge_t, edge_ub, to_near, to_far, from_near, from_far, tile_in, tile_back,
    s_v, mix_v, abs_v, coef, strip_v, strip_mix, strip_coef,
    load_sem, wet_sem, send_sem, recv_sem, ready_sem,
):
    levels = u_in.shape[0]
    tracers = t_in.shape[0]
    padded = mix_v.shape[0]
    total_wet = WET_DEV * secs * tiles
    total_tiles = OCEAN_DEV * secs * tiles
    own = OCEAN_DEV * LANES
    slots = WET_DEV * LANES
    sec = lax.axis_index("sec")
    tile = lax.axis_index("tile")
    device = sec * tiles + tile
    odd = lax.rem(tile, 2)
    even_lane = odd == 0
    partner = (sec, tile + 1 - 2 * odd)
    far_flat = lax.rem(device + 2 * odd - 1 + secs * tiles, secs * tiles)
    far = (far_flat // tiles, lax.rem(far_flat, tiles))

    barrier = pltpu.get_barrier_semaphore()
    pl.semaphore_signal(barrier, inc=1, device_id=partner, device_id_type=MESH)

    @pl.when(odd == 0)
    def _():
        pl.semaphore_signal(barrier, inc=1, device_id=far, device_id_type=MESH)

    slot_edge = pl.ds(pl.multiple_of((slots - LANES) * odd, LANES), LANES)
    far_edge = pl.ds(pl.multiple_of((own - LANES) * odd, LANES), LANES)
    near_edge = pl.ds(pl.multiple_of((own - LANES) * (1 - odd), LANES), LANES)
    loads = [
        pltpu.make_async_copy(t_in.at[:, :, slot_edge], edge_t, load_sem.at[0]),
        pltpu.make_async_copy(u_in.at[:, far_edge], edge_ub.at[0], load_sem.at[1]),
        pltpu.make_async_copy(b_in.at[:, far_edge], edge_ub.at[1], load_sem.at[2]),
        pltpu.make_async_copy(t_in, t_v, load_sem.at[3]),
        pltpu.make_async_copy(u_in, u_v.at[:, pl.ds(0, own)], load_sem.at[4]),
        pltpu.make_async_copy(b_in, b_v.at[:, pl.ds(0, own)], load_sem.at[5]),
        pltpu.make_async_copy(k_in, k_v, load_sem.at[6]),
        pltpu.make_async_copy(wet_in, wet_s, wet_sem),
    ]
    for load in loads:
        load.start()

    def remote(src, dst, index, target):
        return pltpu.make_async_remote_copy(
            src_ref=src, dst_ref=dst, send_sem=send_sem.at[index], recv_sem=recv_sem.at[index],
            device_id=target, device_id_type=MESH,
        )

    lane = iota((levels, LANES), 1)
    base = 2 * tracers
    for load in loads[:3]:
        load.wait()
    message = jnp.zeros((levels, LANES), jnp.float32)
    for t in range(tracers):
        here = (lane >= 2 * t) & (lane < 2 * t + 2)
        message = jnp.where(here, pltpu.roll(edge_t[t].astype(jnp.float32), 2 * t + 2 * odd, 1), message)
    for field in range(2):
        offset = base + HALO * field
        here = (lane >= offset) & (lane < offset + HALO)
        message = jnp.where(here, pltpu.roll(edge_ub[field], offset + HALO * odd, 1), message)
    to_far[...] = message

    pl.semaphore_wait(barrier, 1 + odd)
    send_far = remote(to_far, from_far, 0, far)

    @pl.when(odd == 1)
    def _():
        pl.semaphore_signal(ready_sem, inc=1, device_id=far, device_id_type=MESH)
        send_far.start()

    tile_u = remote(u_in.at[:, near_edge], tile_in.at[0], 2, partner)
    tile_b = remote(b_in.at[:, near_edge], tile_in.at[1], 3, partner)
    tile_u.start()
    tile_b.start()

    for load in loads[3:6]:
        load.wait()
    message = jnp.zeros((levels, LANES), jnp.float32)
    for t in range(tracers):
        here = (lane >= 2 * t) & (lane < 2 * t + 2)
        near = jnp.where(even_lane, t_v[t, :, slots - LANES :], t_v[t, :, :LANES]).astype(jnp.float32)
        message = jnp.where(here, pltpu.roll(near, 2 * t + 2 - 2 * odd, 1), message)
    for field, offset in ((u_v, base), (b_v, base + HALO)):
        here = (lane >= offset) & (lane < offset + HALO)
        near = jnp.where(even_lane, field[:, 2 * LANES : 3 * LANES], field[:, LANES : 2 * LANES])
        message = jnp.where(here, pltpu.roll(near, offset + HALO - HALO * odd, 1), message)
    to_near[...] = message
    send_near = remote(to_near, from_near, 1, partner)
    send_near.start()

    loads[6].wait()
    rows = 8 * padded
    wide = 3 * rows
    spread = ((iota((rows, tracers), 0) >> 3) == iota((rows, tracers), 1)).astype(jnp.float32)
    column = iota((tracers, wide), 1)
    column = jnp.where(column >= 2 * rows, column - 2 * rows, jnp.where(column >= rows, column - rows, column))
    gather = ((column >> 3) == iota((tracers, wide), 0)).astype(jnp.float32)
    matrix = exact(exact(spread, k_v[...]), gather)
    same = (iota((rows, wide), 0) & 7) == (iota((rows, wide), 1) & 7)
    matrix = jnp.where(same, matrix, 0.0)
    coarse = matrix.astype(jnp.bfloat16).astype(jnp.float32)
    matrix = jnp.where(iota((rows, wide), 1) < 2 * rows, coarse, matrix - coarse).astype(jnp.bfloat16)
    mix_v[tracers, :, :] = jnp.zeros(mix_v.shape[1:], jnp.float32)
    strip_mix[tracers, :, :] = jnp.zeros(strip_mix.shape[1:], jnp.float32)

    for t in range(tracers):
        s_v[t, :, :slots] = t_v[t].astype(jnp.float32)

    loads[7].wait()
    listed = [
        wet_s[lax.rem(device * WET_DEV + total_wet + j, total_wet)] for j in range(-1, WET_DEV + 1)
    ]
    ring = OCEAN_DEV + 2
    relative = [lax.rem(w - device * OCEAN_DEV + total_tiles + 2, total_tiles) - 2 for w in listed]
    position = [jnp.where(r < 0, r + ring, jnp.where(r < ring, r, ring)) for r in relative]
    is_open = [
        lax.rem(listed[j + 1] - listed[j] + total_tiles, total_tiles) == 1 for j in range(WET_DEV + 1)
    ]
    spot_left, spot, spot_right = position[0], position[1 : WET_DEV + 1], position[WET_DEV + 1]

    tri = (iota((levels, levels), 0) >= iota((levels, levels), 1)).astype(jnp.float32)
    abs_v[:, :slots] = absorbed_light(s_v[0, :, :slots], tri)

    send_near.wait()
    halo_two = jnp.where(even_lane, lane, LANES - 1 - lane) < 2
    halo_three = jnp.where(even_lane, lane, LANES - 1 - lane) < HALO
    for t in range(tracers):
        came = pltpu.roll(from_near[...], 2 * LANES - 2 * t - 2 * odd, 1)
        s_v[t, :, slots:] = jnp.where(halo_two, came, 0.0)
    abs_v[:, slots:] = absorbed_light(s_v[0, :, slots:], tri)
    tile_u.wait()
    tile_b.wait()
    for field, offset, whole in ((u_v, base, tile_in[0]), (b_v, base + HALO, tile_in[1])):
        came = pltpu.roll(from_near[...], 2 * LANES - offset - HALO * odd, 1)
        near = jnp.where(halo_three, came, 0.0)
        field[:, own : own + LANES] = jnp.where(even_lane, whole, near)
        field[:, own + LANES :] = jnp.where(even_lane, near, whole)

    final = None
    for step in range(STEPS):
        width = slots + LANES if step < STEPS - 1 else slots
        light = [abs_v[:, j * LANES : (j + 1) * LANES] for j in range(WET_DEV + 1)]
        heat = []
        for q in range(ring):
            at_halo = jnp.where(lane < LANES // 2, spot_right, spot_left) == q
            term = jnp.where(at_halo, light[WET_DEV], 0.0)
            for j in range(WET_DEV):
                term = jnp.where(spot[j] == q, light[j], term)
            heat.append(term)
        buoyancy = b_v[...] + HEATING * jnp.concatenate(heat, axis=1)
        b_v[...] = buoyancy
        u_v[...] = advance_velocity(u_v[...], buoyancy)
        if step == STEPS - 1:
            place = pl.ds(pl.multiple_of(own + LANES * odd, LANES), LANES)
            final = (
                remote(u_v.at[:, place], tile_back.at[0], 4, partner),
                remote(b_v.at[:, place], tile_back.at[1], 5, partner),
            )
            for copy in final:
                copy.start()
        taken = []
        for field in (u_v, b_v):
            part = [field[:, q * LANES : (q + 1) * LANES] for q in range(ring)]
            chosen = [
                pick(spot[0], [(0, part[0]), (1, part[1]), (2, part[2]), (5, part[5])]),
                pick(spot[1], [(0, part[0]), (1, part[1]), (2, part[2]), (3, part[3])]),
                pick(spot[2], [(1, part[1]), (2, part[2]), (3, part[3]), (4, part[4])]),
            ]
            ahead = pick(spot_right, [(3, part[3]), (4, part[4]), (5, part[5])])
            behind = pick(spot_left, [(0, part[0]), (4, part[4]), (5, part[5])])
            chosen.append(jnp.where(lane < LANES // 2, ahead, behind))
            taken.append(jnp.concatenate(chosen, axis=1))
        gates = []
        for j in range(WET_DEV + 1):
            ends = is_open[(j + 1) % (WET_DEV + 1)].astype(jnp.float32)
            gates.append(jnp.where(lane == LANES - 1, ends, 1.0))
        set_coefficients(coef, taken[0], taken[1], jnp.concatenate(gates, axis=1))
        for t in range(tracers):
            mix_v[t, :, :width] = transport(s_v[t], coef, width)
        for group in range(levels // 16):
            halves = []
            for half in range(2):
                level = slice(group * 16 + half * 8, group * 16 + half * 8 + 8)
                grown = react(
                    mix_v[:, level, :width], coef[6, level, :width], abs_v[level, :width], matrix, tracers
                )
                if step < STEPS - 1:
                    s_v[:, level, :width] = grown
                halves.append(grown)
            if step == STEPS - 1:
                level = slice(group * 16, group * 16 + 16)
                out_v[:, level, :] = jnp.concatenate(halves, axis=1).astype(jnp.bfloat16)
        if step < STEPS - 1:
            abs_v[:, :width] = absorbed_light(s_v[0, :, :width], tri)

    @pl.when(odd == 0)
    def _():
        pl.semaphore_wait(ready_sem, 1)
        send_far.start()

    for copy in final:
        copy.wait()
    for field, index in ((u_v, 0), (b_v, 1)):
        back = tile_back[index]
        low_given = jnp.logical_and(odd == 1, spot_left == 0)
        high_given = jnp.logical_and(odd == 0, spot_right == OCEAN_DEV - 1)
        ub_out[index, :, :LANES] = jnp.where(low_given, back, field[:, :LANES])
        ub_out[index, :, LANES : own - LANES] = field[:, LANES : own - LANES]
        ub_out[index, :, own - LANES :] = jnp.where(high_given, back, field[:, own - LANES : own])

    edge_wet = jnp.where(even_lane, relative[1] == 0, relative[WET_DEV] == OCEAN_DEV - 1)
    halo_wet = jnp.where(even_lane, relative[0] == -1, relative[WET_DEV + 1] == OCEAN_DEV)
    own_side = jnp.where(even_lane, lane, LANES - 1 - lane) < LANES // 2
    lit = jnp.where(own_side, edge_wet.astype(jnp.int32), halo_wet.astype(jnp.int32)) == 1
    ends = jnp.logical_and(edge_wet, halo_wet).astype(jnp.float32)
    gate = jnp.where(lane == LANES - 1, ends, 1.0)
    halo_two = jnp.where(even_lane, LANES - 1 - lane, lane) < 2
    halo_three = jnp.where(even_lane, LANES - 1 - lane, lane) < HALO
    result = jnp.where(even_lane, lane, LANES - 1 - lane) < 4
    send_far.wait()
    for t in range(tracers):
        came = pltpu.roll(from_far[...], 2 * LANES - 2 - 2 * t + 2 * odd, 1)
        strip_v[t] = jnp.where(halo_two, came, edge_t[t].astype(jnp.float32))
    strip = []
    for field in range(2):
        came = pltpu.roll(from_far[...], 2 * LANES - HALO - base - HALO * field + HALO * odd, 1)
        strip.append(jnp.where(halo_three, came, edge_ub[field]))
    velocity, buoyancy = strip
    for step in range(STEPS):
        light = absorbed_light(strip_v[0], tri)
        buoyancy = buoyancy + HEATING * jnp.where(lit, light, 0.0)
        velocity = advance_velocity(velocity, buoyancy)
        set_coefficients(strip_coef, velocity, buoyancy, gate)
        for t in range(tracers):
            strip_mix[t] = transport(strip_v[t], strip_coef, LANES)
        for group in range(levels // 8):
            level = slice(group * 8, group * 8 + 8)
            strip_v[:, level, :] = react(
                strip_mix[:, level, :], strip_coef[6, level], light[level], matrix, tracers
            )
    for index, field in enumerate((velocity, buoyancy)):
        low = jnp.logical_and(result, even_lane)
        high = jnp.logical_and(result, odd == 1)
        ub_out[index, :, :LANES] = jnp.where(low, field, ub_out[index, :, :LANES])
        ub_out[index, :, own - LANES :] = jnp.where(high, field, ub_out[index, :, own - LANES :])
    fresh = jnp.logical_and(result, edge_wet)
    for t in range(tracers):
        kept = out_v[t, :, slot_edge].astype(jnp.float32)
        out_v[t, :, slot_edge] = jnp.where(fresh, strip_v[t], kept).astype(jnp.bfloat16)


def finish(t_v, ub_v, t_out, u_out, b_out, sems):
    copies = [
        pltpu.make_async_copy(t_v, t_out, sems.at[0]),
        pltpu.make_async_copy(ub_v.at[0], u_out, sems.at[1]),
        pltpu.make_async_copy(ub_v.at[1], b_out, sems.at[2]),
    ]
    for copy in copies:
        copy.start()
    for copy in copies:
        copy.wait()


def on_device(ocean_u, ocean_b, tracers, wet_tiles, kinetic_matrix):
    levels, own = ocean_u.shape
    count, _, slots = tracers.shape
    padded = count + count % 2
    wide = slots + LANES
    domain = own + 2 * LANES
    f32, bf16 = jnp.float32, jnp.bfloat16
    hbm = pl.BlockSpec(memory_space=pltpu.HBM)
    vmem = pl.BlockSpec(memory_space=pltpu.VMEM)
    operands = [
        pltpu.with_memory_space_constraint(x, pltpu.HBM)
        for x in (ocean_u, ocean_b, tracers, wet_tiles, kinetic_matrix)
    ]
    main, ub = pl.pallas_call(
        functools.partial(kernel, lax.axis_size("sec"), lax.axis_size("tile")),
        out_shape=(
            jax.ShapeDtypeStruct(tracers.shape, bf16),
            jax.ShapeDtypeStruct((2, levels, own), f32),
        ),
        in_specs=[hbm] * 5,
        out_specs=(vmem, vmem),
        scratch_shapes=[
            pltpu.VMEM((levels, domain), f32),
            pltpu.VMEM((levels, domain), f32),
            pltpu.VMEM(tracers.shape, bf16),
            pltpu.VMEM(kinetic_matrix.shape, f32),
            pltpu.SMEM(wet_tiles.shape, jnp.int32),
            pltpu.VMEM((count, levels, LANES), bf16),
            pltpu.VMEM((2, levels, LANES), f32),
            pltpu.VMEM((levels, LANES), f32),
            pltpu.VMEM((levels, LANES), f32),
            pltpu.VMEM((levels, LANES), f32),
            pltpu.VMEM((levels, LANES), f32),
            pltpu.VMEM((2, levels, LANES), f32),
            pltpu.VMEM((2, levels, LANES), f32),
            pltpu.VMEM((count, levels, wide), f32),
            pltpu.VMEM((padded, levels, wide), f32),
            pltpu.VMEM((levels, wide), f32),
            pltpu.VMEM((7, levels, wide), f32),
            pltpu.VMEM((count, levels, LANES), f32),
            pltpu.VMEM((padded, levels, LANES), f32),
            pltpu.VMEM((7, levels, LANES), f32),
            pltpu.SemaphoreType.DMA((7,)),
            pltpu.SemaphoreType.DMA,
            pltpu.SemaphoreType.DMA((6,)),
            pltpu.SemaphoreType.DMA((6,)),
            pltpu.SemaphoreType.REGULAR,
        ],
        compiler_params=pltpu.CompilerParams(
            collective_id=0, has_side_effects=True, vmem_limit_bytes=40 * 2**20
        ),
    )(*operands)
    return pl.pallas_call(
        finish,
        out_shape=(
            jax.ShapeDtypeStruct(tracers.shape, bf16),
            jax.ShapeDtypeStruct(ocean_u.shape, f32),
            jax.ShapeDtypeStruct(ocean_b.shape, f32),
        ),
        in_specs=[vmem, vmem],
        out_specs=(hbm, hbm, hbm),
        scratch_shapes=[pltpu.SemaphoreType.DMA((3,))],
        compiler_params=pltpu.CompilerParams(vmem_limit_bytes=2**20),
    )(main, ub)


def solution(mesh):
    flat = ("sec", "tile")
    placed = (P(None, flat), P(None, flat), P(None, None, flat), P(), P())
    return jax.shard_map(
        on_device,
        mesh=mesh,
        in_specs=placed,
        out_specs=(P(None, None, flat), P(None, flat), P(None, flat)),
        check_vma=False,
    )
```

```python
import functools

import jax
import jax.numpy as jnp
from jax import lax
from jax.experimental import pallas as pl
from jax.experimental.pallas import tpu as pltpu
from jax.sharding import PartitionSpec as P

MESH = pl.DeviceIdType.MESH
LANES = 128
STEPS = 2
WET_DEV = 3
OCEAN_DEV = 4
HALO = 3

DT_OCEAN = 0.25
PRESSURE = 1.0
HORIZ_VISC = 0.2
VERT_VISC = 0.2
HEATING = 0.2
KAPPA_BASE = 0.05
KAPPA_SPAN = 0.35
DT_TRACER = 0.3
DT_MIX = 1.0
KINETIC_DELTA = 0.5
SURFACE_LIGHT = 10.0
WATER_ATT = 0.04
PIGMENT_ATT = 0.08
GROWTH = 0.05
THERMAL_GAIN = 0.1


def roll(x, shift, axis):
    size = x.shape[axis]
    shift = shift % size
    return x if shift == 0 else pltpu.roll(x, shift, axis)


def iota(shape, axis):
    return lax.broadcasted_iota(jnp.int32, shape, axis)


def pick(position, options):
    value = None
    for where, option in options:
        value = option if value is None else jnp.where(position == where, option, value)
    return value


def exact(a, b):
    return jnp.dot(a, b, precision=lax.Precision.HIGHEST, preferred_element_type=jnp.float32)


def absorbed_light(pigment, tri):
    attenuation = WATER_ATT + PIGMENT_ATT * pigment * pigment
    below = jnp.exp(-exact(tri, attenuation))
    above = jnp.where(iota(pigment.shape, 0) == 0, 1.0, roll(below, 1, 0))
    return SURFACE_LIGHT * (above - below)


def advance_velocity(velocity, buoyancy):
    level = iota(velocity.shape, 0)
    horiz = roll(velocity, 1, 1) + roll(velocity, -1, 1) - 2.0 * velocity
    press = roll(buoyancy, -1, 1) - buoyancy
    upper = jnp.where(level == 0, velocity, roll(velocity, 1, 0))
    lower = jnp.where(level == velocity.shape[0] - 1, velocity, roll(velocity, -1, 0))
    vert = upper + lower - 2.0 * velocity
    return velocity + DT_OCEAN * (HORIZ_VISC * horiz + VERT_VISC * vert - PRESSURE * press)


def set_coefficients(coef, face_u, warmth, gate):
    level = iota(face_u.shape, 0)
    shear = face_u - roll(face_u, -1, 0)
    stratified = warmth - roll(warmth, -1, 0)
    steep = 4.0 * (shear * shear - stratified)
    spreading = KAPPA_BASE + KAPPA_SPAN / (1.0 + jnp.exp(-steep))
    spreading = jnp.where(level == face_u.shape[0] - 1, 0.0, spreading)
    spreading_up = jnp.where(level == 0, 0.0, roll(spreading, 1, 0))
    gate = DT_TRACER * gate
    forward = jnp.maximum(face_u, 0.0) * gate
    backward = jnp.minimum(face_u, 0.0) * gate
    coef[0] = 1.0 - forward + roll(backward, 1, 1)
    coef[1] = -backward
    coef[2] = roll(forward, 1, 1)
    coef[3] = 1.0 - DT_MIX * (spreading + spreading_up)
    coef[4] = DT_MIX * spreading
    coef[5] = DT_MIX * spreading_up
    coef[6] = KINETIC_DELTA * jnp.exp(THERMAL_GAIN * warmth)


def transport(state, coef, width):
    moved = (coef[0] * state + coef[1] * roll(state, -1, 1) + coef[2] * roll(state, 1, 1))[:, :width]
    return (
        coef[3][:, :width] * moved
        + coef[4][:, :width] * roll(moved, -1, 0)
        + coef[5][:, :width] * roll(moved, 1, 0)
    )


def react(mixed, warm, light, matrix, tracers):
    padded, rows, width = mixed.shape
    flat = mixed.reshape(padded * rows, width)
    high = flat.astype(jnp.bfloat16)
    low = (flat - high.astype(jnp.float32)).astype(jnp.bfloat16)
    drift = jnp.dot(
        matrix, jnp.concatenate([high, low, high], axis=0), preferred_element_type=jnp.float32
    ).reshape(padded, rows, width)
    grown = mixed + warm[None] * drift
    return jnp.concatenate([(grown[0] + GROWTH * light)[None], grown[1:tracers]], axis=0)


def kernel(
    secs, tiles, u_in, b_in, t_in, wet_in, k_in,
    out_v, ub_out, pack_out, far_out, mask_out, matrix_out,
    u_v, b_v, t_v, k_v, wet_s, edge_t, edge_ub, to_near, to_far, from_near, from_far, tile_in, tile_back,
    s_v, mix_v, abs_v, coef,
    load_sem, wet_sem, send_sem, recv_sem, far_ready, near_ready,
):
    levels = u_in.shape[0]
    tracers = t_in.shape[0]
    padded = mix_v.shape[0]
    total_wet = WET_DEV * secs * tiles
    total_tiles = OCEAN_DEV * secs * tiles
    own = OCEAN_DEV * LANES
    slots = WET_DEV * LANES
    sec = lax.axis_index("sec")
    tile = lax.axis_index("tile")
    device = sec * tiles + tile
    odd = lax.rem(tile, 2)
    even_lane = odd == 0
    partner = (sec, tile + 1 - 2 * odd)
    far_flat = lax.rem(device + 2 * odd - 1 + secs * tiles, secs * tiles)
    far = (far_flat // tiles, lax.rem(far_flat, tiles))

    slot_edge = pl.ds(pl.multiple_of((slots - LANES) * odd, LANES), LANES)
    far_edge = pl.ds(pl.multiple_of((own - LANES) * odd, LANES), LANES)
    near_edge = pl.ds(pl.multiple_of((own - LANES) * (1 - odd), LANES), LANES)
    loads = [
        pltpu.make_async_copy(t_in.at[:, :, slot_edge], edge_t, load_sem.at[0]),
        pltpu.make_async_copy(u_in.at[:, far_edge], edge_ub.at[0], load_sem.at[1]),
        pltpu.make_async_copy(b_in.at[:, far_edge], edge_ub.at[1], load_sem.at[2]),
        pltpu.make_async_copy(t_in, t_v, load_sem.at[3]),
        pltpu.make_async_copy(u_in, u_v.at[:, pl.ds(0, own)], load_sem.at[4]),
        pltpu.make_async_copy(b_in, b_v.at[:, pl.ds(0, own)], load_sem.at[5]),
        pltpu.make_async_copy(k_in, k_v, load_sem.at[6]),
        pltpu.make_async_copy(wet_in, wet_s, wet_sem),
    ]
    for load in loads[:3]:
        load.start()

    barrier = pltpu.get_barrier_semaphore()
    greeted = (jnp.where(even_lane, far[0], partner[0]), jnp.where(even_lane, far[1], partner[1]))
    pl.semaphore_signal(barrier, inc=1, device_id=greeted, device_id_type=MESH)
    for load in loads[3:]:
        load.start()

    def remote(src, dst, index, target):
        return pltpu.make_async_remote_copy(
            src_ref=src, dst_ref=dst, send_sem=send_sem.at[index], recv_sem=recv_sem.at[index],
            device_id=target, device_id_type=MESH,
        )

    lane = iota((levels, LANES), 1)
    base = 2 * tracers
    for load in loads[:3]:
        load.wait()
    thin = iota((8, LANES), 1)
    groups = levels // 8
    for part in range(3):
        members = range(8 * part, min(8 * part + 8, tracers))
        value = None
        for g in range(groups):
            level = slice(8 * g, 8 * g + 8)
            chunk = None
            for t in members:
                shift = (16 * g + 2 * (t - 8 * part) + 2 * odd) & (LANES - 1)
                moved = pltpu.roll(edge_t[t, level, :].astype(jnp.float32), shift, 1)
                chunk = moved if chunk is None else jnp.where((thin & 15) >= 2 * (t - 8 * part), moved, chunk)
            if part == 2:
                for field in range(2):
                    offset = 2 + HALO * field
                    moved = pltpu.roll(edge_ub[field, level, :], (16 * g + offset + HALO * odd) & (LANES - 1), 1)
                    chunk = jnp.where((thin & 15) >= offset, moved, chunk)
            value = chunk if value is None else jnp.where((thin >> 4) == g, chunk, value)
        to_far[8 * part : 8 * part + 8, :] = value

    pl.semaphore_wait(barrier, 1)
    send_far = remote(to_far, from_far, 0, far)

    @pl.when(odd == 1)
    def _():
        pl.semaphore_signal(far_ready, inc=1, device_id=far, device_id_type=MESH)
        send_far.start()
        pl.semaphore_wait(near_ready, 1)

    @pl.when(odd == 0)
    def _():
        pl.semaphore_signal(near_ready, inc=1, device_id=partner, device_id_type=MESH)

    tile_u = remote(u_in.at[:, near_edge], tile_in.at[0], 2, partner)
    tile_b = remote(b_in.at[:, near_edge], tile_in.at[1], 3, partner)
    tile_u.start()
    tile_b.start()

    for load in loads[3:6]:
        load.wait()
    message = jnp.zeros((levels, LANES), jnp.float32)
    for t in range(tracers):
        here = (lane >= 2 * t) & (lane < 2 * t + 2)
        near = jnp.where(even_lane, t_v[t, :, slots - LANES :], t_v[t, :, :LANES]).astype(jnp.float32)
        message = jnp.where(here, pltpu.roll(near, 2 * t + 2 - 2 * odd, 1), message)
    for field, offset in ((u_v, base), (b_v, base + HALO)):
        here = (lane >= offset) & (lane < offset + HALO)
        near = jnp.where(even_lane, field[:, 2 * LANES : 3 * LANES], field[:, LANES : 2 * LANES])
        message = jnp.where(here, pltpu.roll(near, offset + HALO - HALO * odd, 1), message)
    to_near[...] = message
    send_near = remote(to_near, from_near, 1, partner)
    send_near.start()

    loads[6].wait()
    rows = 8 * padded
    wide = 3 * rows
    spread = ((iota((rows, tracers), 0) >> 3) == iota((rows, tracers), 1)).astype(jnp.float32)
    column = iota((tracers, wide), 1)
    column = jnp.where(column >= 2 * rows, column - 2 * rows, jnp.where(column >= rows, column - rows, column))
    gather = ((column >> 3) == iota((tracers, wide), 0)).astype(jnp.float32)
    matrix = exact(exact(spread, k_v[...]), gather)
    same = (iota((rows, wide), 0) & 7) == (iota((rows, wide), 1) & 7)
    matrix = jnp.where(same, matrix, 0.0)
    coarse = matrix.astype(jnp.bfloat16).astype(jnp.float32)
    matrix = jnp.where(iota((rows, wide), 1) < 2 * rows, coarse, matrix - coarse).astype(jnp.bfloat16)
    mix_v[tracers, :, :] = jnp.zeros(mix_v.shape[1:], jnp.float32)
    matrix_out[...] = matrix

    for f in range(tracers + 2):
        value = None
        for g in range(groups):
            level = slice(8 * g, 8 * g + 8)
            part = edge_t[f, level, :].astype(jnp.float32) if f < tracers else edge_ub[f - tracers, level, :]
            moved = roll(part, 16 * g + 8, 1)
            value = moved if value is None else jnp.where((thin >> 4) == g, moved, value)
        pack_out[f] = value

    for t in range(tracers):
        s_v[t, :, :slots] = t_v[t].astype(jnp.float32)

    loads[7].wait()
    listed = [
        wet_s[lax.rem(device * WET_DEV + total_wet + j, total_wet)] for j in range(-1, WET_DEV + 1)
    ]
    ring = OCEAN_DEV + 2
    relative = [lax.rem(w - device * OCEAN_DEV + total_tiles + 2, total_tiles) - 2 for w in listed]
    position = [jnp.where(r < 0, r + ring, jnp.where(r < ring, r, ring)) for r in relative]
    is_open = [
        lax.rem(listed[j + 1] - listed[j] + total_tiles, total_tiles) == 1 for j in range(WET_DEV + 1)
    ]
    spot_left, spot, spot_right = position[0], position[1 : WET_DEV + 1], position[WET_DEV + 1]

    tri = (iota((levels, levels), 0) >= iota((levels, levels), 1)).astype(jnp.float32)
    abs_v[:, :slots] = absorbed_light(s_v[0, :, :slots], tri)

    send_near.wait()
    halo_two = jnp.where(even_lane, lane, LANES - 1 - lane) < 2
    halo_three = jnp.where(even_lane, lane, LANES - 1 - lane) < HALO
    for t in range(tracers):
        came = pltpu.roll(from_near[...], 2 * LANES - 2 * t - 2 * odd, 1)
        s_v[t, :, slots:] = jnp.where(halo_two, came, 0.0)
    abs_v[:, slots:] = absorbed_light(s_v[0, :, slots:], tri)
    tile_u.wait()
    tile_b.wait()
    for field, offset, whole in ((u_v, base, tile_in[0]), (b_v, base + HALO, tile_in[1])):
        came = pltpu.roll(from_near[...], 2 * LANES - offset - HALO * odd, 1)
        near = jnp.where(halo_three, came, 0.0)
        field[:, own : own + LANES] = jnp.where(even_lane, whole, near)
        field[:, own + LANES :] = jnp.where(even_lane, near, whole)

    final = None
    for step in range(STEPS):
        width = slots + LANES if step < STEPS - 1 else slots
        light = [abs_v[:, j * LANES : (j + 1) * LANES] for j in range(WET_DEV + 1)]
        heat = []
        for q in range(ring):
            at_halo = jnp.where(lane < LANES // 2, spot_right, spot_left) == q
            term = jnp.where(at_halo, light[WET_DEV], 0.0)
            for j in range(WET_DEV):
                term = jnp.where(spot[j] == q, light[j], term)
            heat.append(term)
        buoyancy = b_v[...] + HEATING * jnp.concatenate(heat, axis=1)
        b_v[...] = buoyancy
        u_v[...] = advance_velocity(u_v[...], buoyancy)
        if step == STEPS - 1:
            place = pl.ds(pl.multiple_of(own + LANES * odd, LANES), LANES)
            final = (
                remote(u_v.at[:, place], tile_back.at[0], 4, partner),
                remote(b_v.at[:, place], tile_back.at[1], 5, partner),
            )
            for copy in final:
                copy.start()
        taken = []
        for field in (u_v, b_v):
            part = [field[:, q * LANES : (q + 1) * LANES] for q in range(ring)]
            chosen = [
                pick(spot[0], [(0, part[0]), (1, part[1]), (2, part[2]), (5, part[5])]),
                pick(spot[1], [(0, part[0]), (1, part[1]), (2, part[2]), (3, part[3])]),
                pick(spot[2], [(1, part[1]), (2, part[2]), (3, part[3]), (4, part[4])]),
            ]
            ahead = pick(spot_right, [(3, part[3]), (4, part[4]), (5, part[5])])
            behind = pick(spot_left, [(0, part[0]), (4, part[4]), (5, part[5])])
            chosen.append(jnp.where(lane < LANES // 2, ahead, behind))
            taken.append(jnp.concatenate(chosen, axis=1))
        gates = []
        for j in range(WET_DEV + 1):
            ends = is_open[(j + 1) % (WET_DEV + 1)].astype(jnp.float32)
            gates.append(jnp.where(lane == LANES - 1, ends, 1.0))
        set_coefficients(coef, taken[0], taken[1], jnp.concatenate(gates, axis=1))
        for t in range(tracers):
            mix_v[t, :, :width] = transport(s_v[t], coef, width)
        for group in range(levels // 16):
            halves = []
            for half in range(2):
                level = slice(group * 16 + half * 8, group * 16 + half * 8 + 8)
                grown = react(
                    mix_v[:, level, :width], coef[6, level, :width], abs_v[level, :width], matrix, tracers
                )
                if step < STEPS - 1:
                    s_v[:, level, :width] = grown
                halves.append(grown)
            if step == STEPS - 1:
                level = slice(group * 16, group * 16 + 16)
                out_v[:, level, :] = jnp.concatenate(halves, axis=1).astype(jnp.bfloat16)
        if step < STEPS - 1:
            abs_v[:, :width] = absorbed_light(s_v[0, :, :width], tri)

    @pl.when(odd == 0)
    def _():
        pl.semaphore_wait(far_ready, 1)
        send_far.start()

    for copy in final:
        copy.wait()
    for field, index in ((u_v, 0), (b_v, 1)):
        back = tile_back[index]
        low_given = jnp.logical_and(odd == 1, spot_left == 0)
        high_given = jnp.logical_and(odd == 0, spot_right == OCEAN_DEV - 1)
        ub_out[index, :, :LANES] = jnp.where(low_given, back, field[:, :LANES])
        ub_out[index, :, LANES : own - LANES] = field[:, LANES : own - LANES]
        ub_out[index, :, own - LANES :] = jnp.where(high_given, back, field[:, own - LANES : own])

    edge_wet = jnp.where(even_lane, relative[1] == 0, relative[WET_DEV] == OCEAN_DEV - 1)
    halo_wet = jnp.where(even_lane, relative[0] == -1, relative[WET_DEV + 1] == OCEAN_DEV)
    column = thin & 15
    distance = jnp.where(even_lane, column - 8, 7 - column)
    edge_wet, halo_wet = edge_wet.astype(jnp.float32), halo_wet.astype(jnp.float32)
    mask_out[0] = jnp.where(distance >= 0, edge_wet, halo_wet)
    mask_out[1] = jnp.where(column == 7, edge_wet * halo_wet, 1.0)
    mask_out[2] = jnp.zeros((8, LANES), jnp.float32) + edge_wet
    send_far.wait()
    far_out[...] = from_far[...]


def finish(
    t_v, ub_v, pack_v, far_v, mask_v, matrix_v, t_out, u_out, b_out, mix_v, sems,
):
    tracers, levels, slots = t_out.shape
    own = u_out.shape[1]
    odd = lax.rem(lax.axis_index("tile"), 2)
    even_lane = odd == 0
    slot_rest = pl.ds(pl.multiple_of(LANES * (1 - odd), LANES), slots - LANES)
    own_rest = pl.ds(pl.multiple_of(LANES * (1 - odd), LANES), own - LANES)
    slot_edge = pl.ds(pl.multiple_of((slots - LANES) * odd, LANES), LANES)
    far_edge = pl.ds(pl.multiple_of((own - LANES) * odd, LANES), LANES)
    outs = (u_out, b_out)
    copies = [pltpu.make_async_copy(t_v.at[:, :, slot_rest], t_out.at[:, :, slot_rest], sems.at[0])]
    for f in range(2):
        copies.append(
            pltpu.make_async_copy(ub_v.at[f, :, own_rest], outs[f].at[:, own_rest], sems.at[1 + f])
        )
    for copy in copies:
        copy.start()

    shape = (8, LANES)
    lane = iota(shape, 1)
    row = iota(shape, 0)
    column = lane & 15
    level = 8 * (lane >> 4) + row
    inside = jnp.where(even_lane, 7 - column, column - 8)
    halo_two = (inside >= 0) & (inside < 2)
    halo_three = (inside >= 0) & (inside < HALO)

    def above(x):
        turned = roll(x, 1, 0)
        return jnp.where(row == 0, roll(turned, 16, 1), turned)

    def below(x):
        turned = roll(x, -1, 0)
        return jnp.where(row == 7, roll(turned, -16, 1), turned)

    def total_from_top(x):
        for shift in (1, 2, 4):
            x = x + jnp.where(row >= shift, roll(x, shift, 0), 0.0)
        groups = jnp.where(lane >= 16, roll(jnp.broadcast_to(x[7:8], shape), 16, 1), 0.0)
        for shift in (16, 32, 64):
            groups = groups + jnp.where(lane >= shift, roll(groups, shift, 1), 0.0)
        return x + groups

    state = []
    for t in range(tracers):
        part = far_v[8 * (t // 8) : 8 * (t // 8) + 8, :]
        came = pltpu.roll(part, (6 - 2 * (t % 8) + 2 * odd) & (LANES - 1), 1)
        state.append(jnp.where(halo_two, came, pack_v[t]))
    fields = []
    for f in range(2):
        came = pltpu.roll(far_v[16:24, :], 3 - HALO * f + HALO * odd, 1)
        fields.append(jnp.where(halo_three, came, pack_v[tracers + f]))
    velocity, buoyancy = fields
    lit, gate = mask_v[0], DT_TRACER * mask_v[1]
    mix_v[8 * tracers :, :] = jnp.zeros((8, LANES), jnp.float32)
    matrix = matrix_v[...]
    for step in range(STEPS):
        attenuation = WATER_ATT + PIGMENT_ATT * state[0] * state[0]
        depth = total_from_top(attenuation)
        light = SURFACE_LIGHT * (jnp.exp(attenuation - depth) - jnp.exp(-depth))
        buoyancy = buoyancy + HEATING * lit * light
        horiz = roll(velocity, 1, 1) + roll(velocity, -1, 1) - 2.0 * velocity
        upper = jnp.where(level == 0, velocity, above(velocity))
        lower = jnp.where(level == levels - 1, velocity, below(velocity))
        press = roll(buoyancy, -1, 1) - buoyancy
        velocity = velocity + DT_OCEAN * (
            HORIZ_VISC * horiz + VERT_VISC * (upper + lower - 2.0 * velocity) - PRESSURE * press
        )
        shear = velocity - below(velocity)
        steep = 4.0 * (shear * shear - (buoyancy - below(buoyancy)))
        spreading = KAPPA_BASE + KAPPA_SPAN / (1.0 + jnp.exp(-steep))
        spreading = jnp.where(level == levels - 1, 0.0, spreading)
        spreading_up = jnp.where(level == 0, 0.0, above(spreading))
        forward = jnp.maximum(velocity, 0.0) * gate
        backward = jnp.minimum(velocity, 0.0) * gate
        stay = 1.0 - forward + roll(backward, 1, 1)
        from_left = roll(forward, 1, 1)
        keep = 1.0 - DT_MIX * (spreading + spreading_up)
        warm = KINETIC_DELTA * jnp.exp(THERMAL_GAIN * buoyancy)
        mixed = []
        for t in range(tracers):
            moved = stay * state[t] - backward * roll(state[t], -1, 1) + from_left * roll(state[t], 1, 1)
            mixed.append(
                keep * moved + DT_MIX * (spreading * below(moved) + spreading_up * above(moved))
            )
            mix_v[8 * t : 8 * t + 8, :] = mixed[t]
        flat = mix_v[...]
        high = flat.astype(jnp.bfloat16)
        low = (flat - high.astype(jnp.float32)).astype(jnp.bfloat16)
        drift = jnp.dot(
            matrix, jnp.concatenate([high, low, high], axis=0), preferred_element_type=jnp.float32
        )
        state = [mixed[t] + warm * drift[8 * t : 8 * t + 8] for t in range(tracers)]
        state[0] = state[0] + GROWTH * light

    near_edge = jnp.where(even_lane, lane, LANES - 1 - lane) < 4
    near_wet = near_edge & (mask_v[2] > 0.5)
    for f, field in enumerate((velocity, buoyancy)):
        for g in range(levels // 8):
            rows = slice(8 * g, 8 * g + 8)
            kept = ub_v[f, rows, far_edge]
            ub_v[f, rows, far_edge] = jnp.where(near_edge, roll(field, -16 * g - 8, 1), kept)
        copies.append(
            pltpu.make_async_copy(ub_v.at[f, :, far_edge], outs[f].at[:, far_edge], sems.at[3 + f])
        )
        copies[-1].start()
    near_wet = jnp.concatenate([near_wet.astype(jnp.float32)] * 2, axis=0) > 0.5
    for t in range(tracers):
        for g in range(levels // 16):
            rows = slice(16 * g, 16 * g + 16)
            fresh = jnp.concatenate(
                [roll(state[t], -32 * g - 8, 1), roll(state[t], -32 * g - 24, 1)], axis=0
            )
            kept = t_v[t, rows, slot_edge].astype(jnp.float32)
            t_v[t, rows, slot_edge] = jnp.where(near_wet, fresh, kept).astype(jnp.bfloat16)
    copies.append(
        pltpu.make_async_copy(t_v.at[:, :, slot_edge], t_out.at[:, :, slot_edge], sems.at[5])
    )
    copies[-1].start()
    for copy in copies:
        copy.wait()


def on_device(ocean_u, ocean_b, tracers, wet_tiles, kinetic_matrix):
    levels, own = ocean_u.shape
    count, _, slots = tracers.shape
    padded = count + count % 2
    wide = slots + LANES
    domain = own + 2 * LANES
    f32, bf16 = jnp.float32, jnp.bfloat16
    hbm = pl.BlockSpec(memory_space=pltpu.HBM)
    vmem = pl.BlockSpec(memory_space=pltpu.VMEM)
    operands = [
        pltpu.with_memory_space_constraint(x, pltpu.HBM)
        for x in (ocean_u, ocean_b, tracers, wet_tiles, kinetic_matrix)
    ]
    rows = 8 * padded
    parts = pl.pallas_call(
        functools.partial(kernel, lax.axis_size("sec"), lax.axis_size("tile")),
        out_shape=(
            jax.ShapeDtypeStruct(tracers.shape, bf16),
            jax.ShapeDtypeStruct((2, levels, own), f32),
            jax.ShapeDtypeStruct((count + 2, 8, LANES), f32),
            jax.ShapeDtypeStruct((24, LANES), f32),
            jax.ShapeDtypeStruct((3, 8, LANES), f32),
            jax.ShapeDtypeStruct((rows, 3 * rows), bf16),
        ),
        in_specs=[hbm] * 5,
        out_specs=(vmem,) * 6,
        scratch_shapes=[
            pltpu.VMEM((levels, domain), f32),
            pltpu.VMEM((levels, domain), f32),
            pltpu.VMEM(tracers.shape, bf16),
            pltpu.VMEM(kinetic_matrix.shape, f32),
            pltpu.SMEM(wet_tiles.shape, jnp.int32),
            pltpu.VMEM((count, levels, LANES), bf16),
            pltpu.VMEM((2, levels, LANES), f32),
            pltpu.VMEM((levels, LANES), f32),
            pltpu.VMEM((24, LANES), f32),
            pltpu.VMEM((levels, LANES), f32),
            pltpu.VMEM((24, LANES), f32),
            pltpu.VMEM((2, levels, LANES), f32),
            pltpu.VMEM((2, levels, LANES), f32),
            pltpu.VMEM((count, levels, wide), f32),
            pltpu.VMEM((padded, levels, wide), f32),
            pltpu.VMEM((levels, wide), f32),
            pltpu.VMEM((7, levels, wide), f32),
            pltpu.SemaphoreType.DMA((7,)),
            pltpu.SemaphoreType.DMA,
            pltpu.SemaphoreType.DMA((6,)),
            pltpu.SemaphoreType.DMA((6,)),
            pltpu.SemaphoreType.REGULAR,
            pltpu.SemaphoreType.REGULAR,
        ],
        compiler_params=pltpu.CompilerParams(
            collective_id=0, has_side_effects=True, vmem_limit_bytes=40 * 2**20
        ),
    )(*operands)
    return pl.pallas_call(
        finish,
        out_shape=(
            jax.ShapeDtypeStruct(tracers.shape, bf16),
            jax.ShapeDtypeStruct(ocean_u.shape, f32),
            jax.ShapeDtypeStruct(ocean_b.shape, f32),
        ),
        in_specs=[vmem] * 6,
        out_specs=(hbm, hbm, hbm),
        scratch_shapes=[pltpu.VMEM((rows, LANES), f32), pltpu.SemaphoreType.DMA((6,))],
        compiler_params=pltpu.CompilerParams(vmem_limit_bytes=4 * 2**20),
    )(*parts)


def solution(mesh):
    flat = ("sec", "tile")
    placed = (P(None, flat), P(None, flat), P(None, None, flat), P(), P())
    return jax.shard_map(
        on_device,
        mesh=mesh,
        in_specs=placed,
        out_specs=(P(None, None, flat), P(None, flat), P(None, flat)),
        check_vma=False,
    )
```

```python
import functools

import jax
import jax.numpy as jnp
from jax import lax
from jax.experimental import pallas as pl
from jax.experimental.pallas import tpu as pltpu
from jax.sharding import PartitionSpec as P

MESH = pl.DeviceIdType.MESH
LANES = 128
STEPS = 2
WET_DEV = 3
OCEAN_DEV = 4
HALO = 3

DT_OCEAN = 0.25
PRESSURE = 1.0
HORIZ_VISC = 0.2
VERT_VISC = 0.2
HEATING = 0.2
KAPPA_BASE = 0.05
KAPPA_SPAN = 0.35
DT_TRACER = 0.3
DT_MIX = 1.0
KINETIC_DELTA = 0.5
SURFACE_LIGHT = 10.0
WATER_ATT = 0.04
PIGMENT_ATT = 0.08
GROWTH = 0.05
THERMAL_GAIN = 0.1


def roll(x, shift, axis):
    size = x.shape[axis]
    shift = shift % size
    return x if shift == 0 else pltpu.roll(x, shift, axis)


def iota(shape, axis):
    return lax.broadcasted_iota(jnp.int32, shape, axis)


def pick(position, options):
    value = None
    for where, option in options:
        value = option if value is None else jnp.where(position == where, option, value)
    return value


def exact(a, b):
    return jnp.dot(a, b, precision=lax.Precision.HIGHEST, preferred_element_type=jnp.float32)


def absorbed_light(pigment, tri):
    attenuation = WATER_ATT + PIGMENT_ATT * pigment * pigment
    below = jnp.exp(-exact(tri, attenuation))
    above = jnp.where(iota(pigment.shape, 0) == 0, 1.0, roll(below, 1, 0))
    return SURFACE_LIGHT * (above - below)


def advance_velocity(velocity, buoyancy):
    level = iota(velocity.shape, 0)
    horiz = roll(velocity, 1, 1) + roll(velocity, -1, 1) - 2.0 * velocity
    press = roll(buoyancy, -1, 1) - buoyancy
    upper = jnp.where(level == 0, velocity, roll(velocity, 1, 0))
    lower = jnp.where(level == velocity.shape[0] - 1, velocity, roll(velocity, -1, 0))
    vert = upper + lower - 2.0 * velocity
    return velocity + DT_OCEAN * (HORIZ_VISC * horiz + VERT_VISC * vert - PRESSURE * press)


def set_coefficients(coef, face_u, warmth, gate):
    level = iota(face_u.shape, 0)
    shear = face_u - roll(face_u, -1, 0)
    stratified = warmth - roll(warmth, -1, 0)
    steep = 4.0 * (shear * shear - stratified)
    spreading = KAPPA_BASE + KAPPA_SPAN / (1.0 + jnp.exp(-steep))
    spreading = jnp.where(level == face_u.shape[0] - 1, 0.0, spreading)
    spreading_up = jnp.where(level == 0, 0.0, roll(spreading, 1, 0))
    gate = DT_TRACER * gate
    forward = jnp.maximum(face_u, 0.0) * gate
    backward = jnp.minimum(face_u, 0.0) * gate
    coef[0] = 1.0 - forward + roll(backward, 1, 1)
    coef[1] = -backward
    coef[2] = roll(forward, 1, 1)
    coef[3] = 1.0 - DT_MIX * (spreading + spreading_up)
    coef[4] = DT_MIX * spreading
    coef[5] = DT_MIX * spreading_up
    coef[6] = KINETIC_DELTA * jnp.exp(THERMAL_GAIN * warmth)


def transport(state, coef, width):
    moved = (coef[0] * state + coef[1] * roll(state, -1, 1) + coef[2] * roll(state, 1, 1))[:, :width]
    return (
        coef[3][:, :width] * moved
        + coef[4][:, :width] * roll(moved, -1, 0)
        + coef[5][:, :width] * roll(moved, 1, 0)
    )


def react(mixed, warm, light, matrix, tracers):
    padded, rows, width = mixed.shape
    flat = mixed.reshape(padded * rows, width)
    high = flat.astype(jnp.bfloat16)
    low = (flat - high.astype(jnp.float32)).astype(jnp.bfloat16)
    drift = jnp.dot(
        matrix, jnp.concatenate([high, low, high], axis=0), preferred_element_type=jnp.float32
    ).reshape(padded, rows, width)
    grown = mixed + warm[None] * drift
    return jnp.concatenate([(grown[0] + GROWTH * light)[None], grown[1:tracers]], axis=0)


def kernel(
    secs, tiles, u_in, b_in, t_in, wet_in, k_in,
    out_v, ub_out,
    u_v, b_v, t_v, k_v, wet_s, edge_t, edge_ub, to_near, to_far, from_near, from_far, tile_in, tile_back,
    s_v, mix_v, abs_v, coef, pack_v, thin_mix,
    load_sem, wet_sem, send_sem, recv_sem, far_ready, near_ready,
):
    levels = u_in.shape[0]
    tracers = t_in.shape[0]
    padded = mix_v.shape[0]
    total_wet = WET_DEV * secs * tiles
    total_tiles = OCEAN_DEV * secs * tiles
    own = OCEAN_DEV * LANES
    slots = WET_DEV * LANES
    sec = lax.axis_index("sec")
    tile = lax.axis_index("tile")
    device = sec * tiles + tile
    odd = lax.rem(tile, 2)
    even_lane = odd == 0
    partner = (sec, tile + 1 - 2 * odd)
    far_flat = lax.rem(device + 2 * odd - 1 + secs * tiles, secs * tiles)
    far = (far_flat // tiles, lax.rem(far_flat, tiles))

    slot_edge = pl.ds(pl.multiple_of((slots - LANES) * odd, LANES), LANES)
    far_edge = pl.ds(pl.multiple_of((own - LANES) * odd, LANES), LANES)
    near_edge = pl.ds(pl.multiple_of((own - LANES) * (1 - odd), LANES), LANES)
    loads = [
        pltpu.make_async_copy(t_in.at[:, :, slot_edge], edge_t, load_sem.at[0]),
        pltpu.make_async_copy(u_in.at[:, far_edge], edge_ub.at[0], load_sem.at[1]),
        pltpu.make_async_copy(b_in.at[:, far_edge], edge_ub.at[1], load_sem.at[2]),
        pltpu.make_async_copy(t_in, t_v, load_sem.at[3]),
        pltpu.make_async_copy(u_in, u_v.at[:, pl.ds(0, own)], load_sem.at[4]),
        pltpu.make_async_copy(b_in, b_v.at[:, pl.ds(0, own)], load_sem.at[5]),
        pltpu.make_async_copy(k_in, k_v, load_sem.at[6]),
        pltpu.make_async_copy(wet_in, wet_s, wet_sem),
    ]
    for load in loads[:3]:
        load.start()

    barrier = pltpu.get_barrier_semaphore()
    greeted = (jnp.where(even_lane, far[0], partner[0]), jnp.where(even_lane, far[1], partner[1]))
    pl.semaphore_signal(barrier, inc=1, device_id=greeted, device_id_type=MESH)
    for load in loads[3:]:
        load.start()

    def remote(src, dst, index, target):
        return pltpu.make_async_remote_copy(
            src_ref=src, dst_ref=dst, send_sem=send_sem.at[index], recv_sem=recv_sem.at[index],
            device_id=target, device_id_type=MESH,
        )

    lane = iota((levels, LANES), 1)
    base = 2 * tracers
    for load in loads[:3]:
        load.wait()
    thin = iota((8, LANES), 1)
    groups = levels // 8
    for part in range(3):
        members = range(8 * part, min(8 * part + 8, tracers))
        value = None
        for g in range(groups):
            level = slice(8 * g, 8 * g + 8)
            chunk = None
            for t in members:
                shift = (16 * g + 2 * (t - 8 * part) + 2 * odd) & (LANES - 1)
                moved = pltpu.roll(edge_t[t, level, :].astype(jnp.float32), shift, 1)
                chunk = moved if chunk is None else jnp.where((thin & 15) >= 2 * (t - 8 * part), moved, chunk)
            if part == 2:
                for field in range(2):
                    offset = 2 + HALO * field
                    moved = pltpu.roll(edge_ub[field, level, :], (16 * g + offset + HALO * odd) & (LANES - 1), 1)
                    chunk = jnp.where((thin & 15) >= offset, moved, chunk)
            value = chunk if value is None else jnp.where((thin >> 4) == g, chunk, value)
        to_far[8 * part : 8 * part + 8, :] = value

    pl.semaphore_wait(barrier, 1)
    send_far = remote(to_far, from_far, 0, far)

    @pl.when(odd == 1)
    def _():
        pl.semaphore_signal(far_ready, inc=1, device_id=far, device_id_type=MESH)
        send_far.start()
        pl.semaphore_wait(near_ready, 1)

    @pl.when(odd == 0)
    def _():
        pl.semaphore_signal(near_ready, inc=1, device_id=partner, device_id_type=MESH)

    tile_u = remote(u_in.at[:, near_edge], tile_in.at[0], 2, partner)
    tile_b = remote(b_in.at[:, near_edge], tile_in.at[1], 3, partner)
    tile_u.start()
    tile_b.start()

    for load in loads[3:6]:
        load.wait()
    message = jnp.zeros((levels, LANES), jnp.float32)
    for t in range(tracers):
        here = (lane >= 2 * t) & (lane < 2 * t + 2)
        near = jnp.where(even_lane, t_v[t, :, slots - LANES :], t_v[t, :, :LANES]).astype(jnp.float32)
        message = jnp.where(here, pltpu.roll(near, 2 * t + 2 - 2 * odd, 1), message)
    for field, offset in ((u_v, base), (b_v, base + HALO)):
        here = (lane >= offset) & (lane < offset + HALO)
        near = jnp.where(even_lane, field[:, 2 * LANES : 3 * LANES], field[:, LANES : 2 * LANES])
        message = jnp.where(here, pltpu.roll(near, offset + HALO - HALO * odd, 1), message)
    to_near[...] = message
    send_near = remote(to_near, from_near, 1, partner)
    send_near.start()

    loads[6].wait()
    rows = 8 * padded
    wide = 3 * rows
    spread = ((iota((rows, tracers), 0) >> 3) == iota((rows, tracers), 1)).astype(jnp.float32)
    column = iota((tracers, wide), 1)
    column = jnp.where(column >= 2 * rows, column - 2 * rows, jnp.where(column >= rows, column - rows, column))
    gather = ((column >> 3) == iota((tracers, wide), 0)).astype(jnp.float32)
    matrix = exact(exact(spread, k_v[...]), gather)
    same = (iota((rows, wide), 0) & 7) == (iota((rows, wide), 1) & 7)
    matrix = jnp.where(same, matrix, 0.0)
    coarse = matrix.astype(jnp.bfloat16).astype(jnp.float32)
    matrix = jnp.where(iota((rows, wide), 1) < 2 * rows, coarse, matrix - coarse).astype(jnp.bfloat16)
    mix_v[tracers, :, :] = jnp.zeros(mix_v.shape[1:], jnp.float32)
    thin_mix[8 * tracers :, :] = jnp.zeros((8, LANES), jnp.float32)

    for f in range(tracers + 2):
        value = None
        for g in range(groups):
            level = slice(8 * g, 8 * g + 8)
            part = edge_t[f, level, :].astype(jnp.float32) if f < tracers else edge_ub[f - tracers, level, :]
            moved = roll(part, 16 * g + 8, 1)
            value = moved if value is None else jnp.where((thin >> 4) == g, moved, value)
        pack_v[f] = value

    for t in range(tracers):
        s_v[t, :, :slots] = t_v[t].astype(jnp.float32)

    loads[7].wait()
    listed = [
        wet_s[lax.rem(device * WET_DEV + total_wet + j, total_wet)] for j in range(-1, WET_DEV + 1)
    ]
    ring = OCEAN_DEV + 2
    relative = [lax.rem(w - device * OCEAN_DEV + total_tiles + 2, total_tiles) - 2 for w in listed]
    position = [jnp.where(r < 0, r + ring, jnp.where(r < ring, r, ring)) for r in relative]
    is_open = [
        lax.rem(listed[j + 1] - listed[j] + total_tiles, total_tiles) == 1 for j in range(WET_DEV + 1)
    ]
    spot_left, spot, spot_right = position[0], position[1 : WET_DEV + 1], position[WET_DEV + 1]

    tri = (iota((levels, levels), 0) >= iota((levels, levels), 1)).astype(jnp.float32)
    abs_v[:, :slots] = absorbed_light(s_v[0, :, :slots], tri)

    send_near.wait()
    halo_two = jnp.where(even_lane, lane, LANES - 1 - lane) < 2
    halo_three = jnp.where(even_lane, lane, LANES - 1 - lane) < HALO
    for t in range(tracers):
        came = pltpu.roll(from_near[...], 2 * LANES - 2 * t - 2 * odd, 1)
        s_v[t, :, slots:] = jnp.where(halo_two, came, 0.0)
    abs_v[:, slots:] = absorbed_light(s_v[0, :, slots:], tri)
    tile_u.wait()
    tile_b.wait()
    for field, offset, whole in ((u_v, base, tile_in[0]), (b_v, base + HALO, tile_in[1])):
        came = pltpu.roll(from_near[...], 2 * LANES - offset - HALO * odd, 1)
        near = jnp.where(halo_three, came, 0.0)
        field[:, own : own + LANES] = jnp.where(even_lane, whole, near)
        field[:, own + LANES :] = jnp.where(even_lane, near, whole)

    final = None
    for step in range(STEPS):
        width = slots + LANES if step < STEPS - 1 else slots
        light = [abs_v[:, j * LANES : (j + 1) * LANES] for j in range(WET_DEV + 1)]
        heat = []
        for q in range(ring):
            at_halo = jnp.where(lane < LANES // 2, spot_right, spot_left) == q
            term = jnp.where(at_halo, light[WET_DEV], 0.0)
            for j in range(WET_DEV):
                term = jnp.where(spot[j] == q, light[j], term)
            heat.append(term)
        buoyancy = b_v[...] + HEATING * jnp.concatenate(heat, axis=1)
        b_v[...] = buoyancy
        u_v[...] = advance_velocity(u_v[...], buoyancy)
        if step == STEPS - 1:
            place = pl.ds(pl.multiple_of(own + LANES * odd, LANES), LANES)
            final = (
                remote(u_v.at[:, place], tile_back.at[0], 4, partner),
                remote(b_v.at[:, place], tile_back.at[1], 5, partner),
            )
            for copy in final:
                copy.start()
        taken = []
        for field in (u_v, b_v):
            part = [field[:, q * LANES : (q + 1) * LANES] for q in range(ring)]
            chosen = [
                pick(spot[0], [(0, part[0]), (1, part[1]), (2, part[2]), (5, part[5])]),
                pick(spot[1], [(0, part[0]), (1, part[1]), (2, part[2]), (3, part[3])]),
                pick(spot[2], [(1, part[1]), (2, part[2]), (3, part[3]), (4, part[4])]),
            ]
            ahead = pick(spot_right, [(3, part[3]), (4, part[4]), (5, part[5])])
            behind = pick(spot_left, [(0, part[0]), (4, part[4]), (5, part[5])])
            chosen.append(jnp.where(lane < LANES // 2, ahead, behind))
            taken.append(jnp.concatenate(chosen, axis=1))
        gates = []
        for j in range(WET_DEV + 1):
            ends = is_open[(j + 1) % (WET_DEV + 1)].astype(jnp.float32)
            gates.append(jnp.where(lane == LANES - 1, ends, 1.0))
        set_coefficients(coef, taken[0], taken[1], jnp.concatenate(gates, axis=1))
        for t in range(tracers):
            mix_v[t, :, :width] = transport(s_v[t], coef, width)
        for group in range(levels // 16):
            halves = []
            for half in range(2):
                level = slice(group * 16 + half * 8, group * 16 + half * 8 + 8)
                grown = react(
                    mix_v[:, level, :width], coef[6, level, :width], abs_v[level, :width], matrix, tracers
                )
                if step < STEPS - 1:
                    s_v[:, level, :width] = grown
                halves.append(grown)
            if step == STEPS - 1:
                level = slice(group * 16, group * 16 + 16)
                out_v[:, level, :] = jnp.concatenate(halves, axis=1).astype(jnp.bfloat16)
        if step < STEPS - 1:
            abs_v[:, :width] = absorbed_light(s_v[0, :, :width], tri)

    @pl.when(odd == 0)
    def _():
        pl.semaphore_wait(far_ready, 1)
        send_far.start()

    for copy in final:
        copy.wait()
    for field, index in ((u_v, 0), (b_v, 1)):
        back = tile_back[index]
        low_given = jnp.logical_and(odd == 1, spot_left == 0)
        high_given = jnp.logical_and(odd == 0, spot_right == OCEAN_DEV - 1)
        ub_out[index, :, :LANES] = jnp.where(low_given, back, field[:, :LANES])
        ub_out[index, :, LANES : own - LANES] = field[:, LANES : own - LANES]
        ub_out[index, :, own - LANES :] = jnp.where(high_given, back, field[:, own - LANES : own])

    edge_wet = jnp.where(even_lane, relative[1] == 0, relative[WET_DEV] == OCEAN_DEV - 1)
    halo_wet = jnp.where(even_lane, relative[0] == -1, relative[WET_DEV + 1] == OCEAN_DEV)
    column = thin & 15
    distance = jnp.where(even_lane, column - 8, 7 - column)
    edge_wet, halo_wet = edge_wet.astype(jnp.float32), halo_wet.astype(jnp.float32)
    shape = (8, LANES)
    lane = thin
    row = iota(shape, 0)
    level = 8 * (lane >> 4) + row
    inside = jnp.where(even_lane, 7 - column, column - 8)
    halo_two = (inside >= 0) & (inside < 2)
    halo_three = (inside >= 0) & (inside < HALO)

    def above(x):
        turned = roll(x, 1, 0)
        return jnp.where(row == 0, roll(turned, 16, 1), turned)

    def below(x):
        turned = roll(x, -1, 0)
        return jnp.where(row == 7, roll(turned, -16, 1), turned)

    def total_from_top(x):
        for shift in (1, 2, 4):
            x = x + jnp.where(row >= shift, roll(x, shift, 0), 0.0)
        groups = jnp.where(lane >= 16, roll(jnp.broadcast_to(x[7:8], shape), 16, 1), 0.0)
        for shift in (16, 32, 64):
            groups = groups + jnp.where(lane >= shift, roll(groups, shift, 1), 0.0)
        return x + groups

    lit = jnp.where(distance >= 0, edge_wet, halo_wet)
    gate = DT_TRACER * jnp.where(column == 7, edge_wet * halo_wet, 1.0)
    near_side = jnp.where(even_lane, lane, LANES - 1 - lane) < 4
    near_wet = jnp.concatenate([jnp.where(near_side, edge_wet, 0.0)] * 2, axis=0) > 0.5

    send_far.wait()
    state = []
    for t in range(tracers):
        part = from_far[8 * (t // 8) : 8 * (t // 8) + 8, :]
        came = pltpu.roll(part, (6 - 2 * (t % 8) + 2 * odd) & (LANES - 1), 1)
        state.append(jnp.where(halo_two, came, pack_v[t]))
    fields = []
    for f in range(2):
        came = pltpu.roll(from_far[16:24, :], 3 - HALO * f + HALO * odd, 1)
        fields.append(jnp.where(halo_three, came, pack_v[tracers + f]))
    velocity, buoyancy = fields
    for step in range(STEPS):
        attenuation = WATER_ATT + PIGMENT_ATT * state[0] * state[0]
        depth = total_from_top(attenuation)
        light = SURFACE_LIGHT * (jnp.exp(attenuation - depth) - jnp.exp(-depth))
        buoyancy = buoyancy + HEATING * lit * light
        horiz = roll(velocity, 1, 1) + roll(velocity, -1, 1) - 2.0 * velocity
        upper = jnp.where(level == 0, velocity, above(velocity))
        lower = jnp.where(level == levels - 1, velocity, below(velocity))
        press = roll(buoyancy, -1, 1) - buoyancy
        velocity = velocity + DT_OCEAN * (
            HORIZ_VISC * horiz + VERT_VISC * (upper + lower - 2.0 * velocity) - PRESSURE * press
        )
        shear = velocity - below(velocity)
        steep = 4.0 * (shear * shear - (buoyancy - below(buoyancy)))
        spreading = KAPPA_BASE + KAPPA_SPAN / (1.0 + jnp.exp(-steep))
        spreading = jnp.where(level == levels - 1, 0.0, spreading)
        spreading_up = jnp.where(level == 0, 0.0, above(spreading))
        forward = jnp.maximum(velocity, 0.0) * gate
        backward = jnp.minimum(velocity, 0.0) * gate
        stay = 1.0 - forward + roll(backward, 1, 1)
        from_left = roll(forward, 1, 1)
        keep = 1.0 - DT_MIX * (spreading + spreading_up)
        warm = KINETIC_DELTA * jnp.exp(THERMAL_GAIN * buoyancy)
        mixed = []
        for t in range(tracers):
            moved = stay * state[t] - backward * roll(state[t], -1, 1) + from_left * roll(state[t], 1, 1)
            mixed.append(
                keep * moved + DT_MIX * (spreading * below(moved) + spreading_up * above(moved))
            )
            thin_mix[8 * t : 8 * t + 8, :] = mixed[t]
        flat = thin_mix[...]
        high = flat.astype(jnp.bfloat16)
        low = (flat - high.astype(jnp.float32)).astype(jnp.bfloat16)
        drift = jnp.dot(
            matrix, jnp.concatenate([high, low, high], axis=0), preferred_element_type=jnp.float32
        )
        state = [mixed[t] + warm * drift[8 * t : 8 * t + 8] for t in range(tracers)]
        state[0] = state[0] + GROWTH * light

    for f, field in enumerate((velocity, buoyancy)):
        for g in range(groups):
            rows = slice(8 * g, 8 * g + 8)
            kept = ub_out[f, rows, far_edge]
            ub_out[f, rows, far_edge] = jnp.where(near_side, roll(field, -16 * g - 8, 1), kept)
    for t in range(tracers):
        for g in range(levels // 16):
            rows = slice(16 * g, 16 * g + 16)
            fresh = jnp.concatenate(
                [roll(state[t], -32 * g - 8, 1), roll(state[t], -32 * g - 24, 1)], axis=0
            )
            kept = out_v[t, rows, slot_edge].astype(jnp.float32)
            out_v[t, rows, slot_edge] = jnp.where(near_wet, fresh, kept).astype(jnp.bfloat16)


def finish(t_v, ub_v, t_out, u_out, b_out, sems):
    copies = [
        pltpu.make_async_copy(t_v, t_out, sems.at[0]),
        pltpu.make_async_copy(ub_v.at[0], u_out, sems.at[1]),
        pltpu.make_async_copy(ub_v.at[1], b_out, sems.at[2]),
    ]
    for copy in copies:
        copy.start()
    for copy in copies:
        copy.wait()


def on_device(ocean_u, ocean_b, tracers, wet_tiles, kinetic_matrix):
    levels, own = ocean_u.shape
    count, _, slots = tracers.shape
    padded = count + count % 2
    wide = slots + LANES
    domain = own + 2 * LANES
    f32, bf16 = jnp.float32, jnp.bfloat16
    hbm = pl.BlockSpec(memory_space=pltpu.HBM)
    vmem = pl.BlockSpec(memory_space=pltpu.VMEM)
    operands = [
        pltpu.with_memory_space_constraint(x, pltpu.HBM)
        for x in (ocean_u, ocean_b, tracers, wet_tiles, kinetic_matrix)
    ]
    rows = 8 * padded
    parts = pl.pallas_call(
        functools.partial(kernel, lax.axis_size("sec"), lax.axis_size("tile")),
        out_shape=(
            jax.ShapeDtypeStruct(tracers.shape, bf16),
            jax.ShapeDtypeStruct((2, levels, own), f32),
        ),
        in_specs=[hbm] * 5,
        out_specs=(vmem,) * 2,
        scratch_shapes=[
            pltpu.VMEM((levels, domain), f32),
            pltpu.VMEM((levels, domain), f32),
            pltpu.VMEM(tracers.shape, bf16),
            pltpu.VMEM(kinetic_matrix.shape, f32),
            pltpu.SMEM(wet_tiles.shape, jnp.int32),
            pltpu.VMEM((count, levels, LANES), bf16),
            pltpu.VMEM((2, levels, LANES), f32),
            pltpu.VMEM((levels, LANES), f32),
            pltpu.VMEM((24, LANES), f32),
            pltpu.VMEM((levels, LANES), f32),
            pltpu.VMEM((24, LANES), f32),
            pltpu.VMEM((2, levels, LANES), f32),
            pltpu.VMEM((2, levels, LANES), f32),
            pltpu.VMEM((count, levels, wide), f32),
            pltpu.VMEM((padded, levels, wide), f32),
            pltpu.VMEM((levels, wide), f32),
            pltpu.VMEM((7, levels, wide), f32),
            pltpu.VMEM((count + 2, 8, LANES), f32),
            pltpu.VMEM((rows, LANES), f32),
            pltpu.SemaphoreType.DMA((7,)),
            pltpu.SemaphoreType.DMA,
            pltpu.SemaphoreType.DMA((6,)),
            pltpu.SemaphoreType.DMA((6,)),
            pltpu.SemaphoreType.REGULAR,
            pltpu.SemaphoreType.REGULAR,
        ],
        compiler_params=pltpu.CompilerParams(
            collective_id=0, has_side_effects=True, vmem_limit_bytes=40 * 2**20
        ),
    )(*operands)
    return pl.pallas_call(
        finish,
        out_shape=(
            jax.ShapeDtypeStruct(tracers.shape, bf16),
            jax.ShapeDtypeStruct(ocean_u.shape, f32),
            jax.ShapeDtypeStruct(ocean_b.shape, f32),
        ),
        in_specs=[vmem] * 2,
        out_specs=(hbm, hbm, hbm),
        scratch_shapes=[pltpu.SemaphoreType.DMA((3,))],
        compiler_params=pltpu.CompilerParams(vmem_limit_bytes=2**20),
    )(*parts)


def solution(mesh):
    flat = ("sec", "tile")
    placed = (P(None, flat), P(None, flat), P(None, None, flat), P(), P())
    return jax.shard_map(
        on_device,
        mesh=mesh,
        in_specs=placed,
        out_specs=(P(None, None, flat), P(None, flat), P(None, flat)),
        check_vma=False,
    )
```

```python
import functools

import jax
import jax.numpy as jnp
from jax import lax
from jax.experimental import pallas as pl
from jax.experimental.pallas import tpu as pltpu
from jax.sharding import PartitionSpec as P

MESH = pl.DeviceIdType.MESH
LANES = 128
STEPS = 2
WET_DEV = 3
OCEAN_DEV = 4
HALO = 3

DT_OCEAN = 0.25
PRESSURE = 1.0
HORIZ_VISC = 0.2
VERT_VISC = 0.2
HEATING = 0.2
KAPPA_BASE = 0.05
KAPPA_SPAN = 0.35
DT_TRACER = 0.3
DT_MIX = 1.0
KINETIC_DELTA = 0.5
SURFACE_LIGHT = 10.0
WATER_ATT = 0.04
PIGMENT_ATT = 0.08
GROWTH = 0.05
THERMAL_GAIN = 0.1


def roll(x, shift, axis):
    size = x.shape[axis]
    shift = shift % size
    return x if shift == 0 else pltpu.roll(x, shift, axis)


def iota(shape, axis):
    return lax.broadcasted_iota(jnp.int32, shape, axis)


def pick(position, options):
    value = None
    for where, option in options:
        value = option if value is None else jnp.where(position == where, option, value)
    return value


def exact(a, b):
    return jnp.dot(a, b, precision=lax.Precision.HIGHEST, preferred_element_type=jnp.float32)


def absorbed_light(pigment, tri):
    attenuation = WATER_ATT + PIGMENT_ATT * pigment * pigment
    below = jnp.exp(-exact(tri, attenuation))
    above = jnp.where(iota(pigment.shape, 0) == 0, 1.0, roll(below, 1, 0))
    return SURFACE_LIGHT * (above - below)


def advance_velocity(velocity, buoyancy):
    level = iota(velocity.shape, 0)
    horiz = roll(velocity, 1, 1) + roll(velocity, -1, 1) - 2.0 * velocity
    press = roll(buoyancy, -1, 1) - buoyancy
    upper = jnp.where(level == 0, velocity, roll(velocity, 1, 0))
    lower = jnp.where(level == velocity.shape[0] - 1, velocity, roll(velocity, -1, 0))
    vert = upper + lower - 2.0 * velocity
    return velocity + DT_OCEAN * (HORIZ_VISC * horiz + VERT_VISC * vert - PRESSURE * press)


def diffusivity(shear, settled):
    steep = 4.0 * (shear * shear - settled)
    return KAPPA_BASE + KAPPA_SPAN / (1.0 + jnp.exp(-steep))


def set_coefficients(coef, face_u, warmth, gate):
    level = iota(face_u.shape, 0)
    shear = face_u - roll(face_u, -1, 0)
    stratified = warmth - roll(warmth, -1, 0)
    spreading = diffusivity(shear, stratified)
    spreading = jnp.where(level == face_u.shape[0] - 1, 0.0, spreading)
    spreading_up = jnp.where(level == 0, 0.0, roll(spreading, 1, 0))
    gate = DT_TRACER * gate
    forward = jnp.maximum(face_u, 0.0) * gate
    backward = jnp.minimum(face_u, 0.0) * gate
    coef[0] = 1.0 - forward + roll(backward, 1, 1)
    coef[1] = -backward
    coef[2] = roll(forward, 1, 1)
    coef[3] = 1.0 - DT_MIX * (spreading + spreading_up)
    coef[4] = DT_MIX * spreading
    coef[5] = DT_MIX * spreading_up
    coef[6] = KINETIC_DELTA * jnp.exp(THERMAL_GAIN * warmth)


def transport(state, coef, width):
    moved = (coef[0] * state + coef[1] * roll(state, -1, 1) + coef[2] * roll(state, 1, 1))[:, :width]
    return (
        coef[3][:, :width] * moved
        + coef[4][:, :width] * roll(moved, -1, 0)
        + coef[5][:, :width] * roll(moved, 1, 0)
    )


def react(mixed, warm, light, matrix, tracers):
    padded, rows, width = mixed.shape
    flat = mixed.reshape(padded * rows, width)
    high = flat.astype(jnp.bfloat16)
    low = (flat - high.astype(jnp.float32)).astype(jnp.bfloat16)
    drift = jnp.dot(
        matrix, jnp.concatenate([high, low, high], axis=0), preferred_element_type=jnp.float32
    ).reshape(padded, rows, width)
    grown = mixed + warm[None] * drift
    return jnp.concatenate([(grown[0] + GROWTH * light)[None], grown[1:tracers]], axis=0)


def kernel(
    secs, tiles, u_in, b_in, t_in, wet_in, k_in,
    out_v, ub_out,
    u_v, b_v, t_v, k_v, wet_s, edge_t, edge_ub, to_near, to_far, from_near, from_far, tile_in, tile_back,
    s_v, mix_v, abs_v, coef, pack_v, thin_mix,
    load_sem, wet_sem, send_sem, recv_sem, far_ready, near_ready,
):
    levels = u_in.shape[0]
    tracers = t_in.shape[0]
    padded = mix_v.shape[0]
    total_wet = WET_DEV * secs * tiles
    total_tiles = OCEAN_DEV * secs * tiles
    own = OCEAN_DEV * LANES
    slots = WET_DEV * LANES
    sec = lax.axis_index("sec")
    tile = lax.axis_index("tile")
    device = sec * tiles + tile
    odd = lax.rem(tile, 2)
    even_lane = odd == 0
    partner = (sec, tile + 1 - 2 * odd)
    far_flat = lax.rem(device + 2 * odd - 1 + secs * tiles, secs * tiles)
    far = (far_flat // tiles, lax.rem(far_flat, tiles))

    slot_edge = pl.ds(pl.multiple_of((slots - LANES) * odd, LANES), LANES)
    far_edge = pl.ds(pl.multiple_of((own - LANES) * odd, LANES), LANES)
    near_edge = pl.ds(pl.multiple_of((own - LANES) * (1 - odd), LANES), LANES)
    loads = [
        pltpu.make_async_copy(t_in.at[:, :, slot_edge], edge_t, load_sem.at[0]),
        pltpu.make_async_copy(u_in.at[:, far_edge], edge_ub.at[0], load_sem.at[1]),
        pltpu.make_async_copy(b_in.at[:, far_edge], edge_ub.at[1], load_sem.at[2]),
        pltpu.make_async_copy(t_in, t_v, load_sem.at[3]),
        pltpu.make_async_copy(u_in, u_v.at[:, pl.ds(0, own)], load_sem.at[4]),
        pltpu.make_async_copy(b_in, b_v.at[:, pl.ds(0, own)], load_sem.at[5]),
        pltpu.make_async_copy(k_in, k_v, load_sem.at[6]),
        pltpu.make_async_copy(wet_in, wet_s, wet_sem),
    ]
    for load in loads[:3]:
        load.start()

    barrier = pltpu.get_barrier_semaphore()
    greeted = (jnp.where(even_lane, far[0], partner[0]), jnp.where(even_lane, far[1], partner[1]))
    pl.semaphore_signal(barrier, inc=1, device_id=greeted, device_id_type=MESH)
    for load in loads[3:]:
        load.start()

    def remote(src, dst, index, target):
        return pltpu.make_async_remote_copy(
            src_ref=src, dst_ref=dst, send_sem=send_sem.at[index], recv_sem=recv_sem.at[index],
            device_id=target, device_id_type=MESH,
        )

    lane = iota((levels, LANES), 1)
    base = 2 * tracers
    for load in loads[:3]:
        load.wait()
    thin = iota((8, LANES), 1)
    groups = levels // 8
    frame = (thin + (LANES - 8 + 2 * odd)) & (LANES - 1)
    last_frame = (thin + (LANES - 8 + HALO * odd)) & (LANES - 1)
    for part in range(3):
        spots = frame if part < 2 else last_frame
        within = spots & 15
        value = None
        for g in range(groups):
            level = slice(8 * g, 8 * g + 8)
            natural = 16 * g + 8
            if part < 2:
                chunk = None
                for k in range(8):
                    moved = roll(edge_t[8 * part + k, level, :].astype(jnp.float32), natural + 2 * k, 1)
                    chunk = moved if chunk is None else jnp.where(within >= 2 * k, moved, chunk)
            else:
                chunk = roll(edge_ub[0, level, :], natural, 1)
                chunk = jnp.where(within >= HALO, roll(edge_ub[1, level, :], natural + HALO, 1), chunk)
                moved = roll(edge_t[tracers - 1, level, :].astype(jnp.float32), natural + 2 * HALO, 1)
                chunk = jnp.where(within >= 2 * HALO, moved, chunk)
            value = chunk if value is None else jnp.where((spots >> 4) == g, chunk, value)
        to_far[8 * part : 8 * part + 8, :] = value

    pl.semaphore_wait(barrier, 1)
    send_far = remote(to_far, from_far, 0, far)

    @pl.when(odd == 1)
    def _():
        pl.semaphore_signal(far_ready, inc=1, device_id=far, device_id_type=MESH)
        send_far.start()
        pl.semaphore_wait(near_ready, 1)

    @pl.when(odd == 0)
    def _():
        pl.semaphore_signal(near_ready, inc=1, device_id=partner, device_id_type=MESH)

    tile_u = remote(u_in.at[:, near_edge], tile_in.at[0], 2, partner)
    tile_b = remote(b_in.at[:, near_edge], tile_in.at[1], 3, partner)
    tile_u.start()
    tile_b.start()

    for load in loads[3:6]:
        load.wait()
    message = jnp.zeros((levels, LANES), jnp.float32)
    for t in range(tracers):
        here = (lane >= 2 * t) & (lane < 2 * t + 2)
        near = jnp.where(even_lane, t_v[t, :, slots - LANES :], t_v[t, :, :LANES]).astype(jnp.float32)
        message = jnp.where(here, pltpu.roll(near, 2 * t + 2 - 2 * odd, 1), message)
    for field, offset in ((u_v, base), (b_v, base + HALO)):
        here = (lane >= offset) & (lane < offset + HALO)
        near = jnp.where(even_lane, field[:, 2 * LANES : 3 * LANES], field[:, LANES : 2 * LANES])
        message = jnp.where(here, pltpu.roll(near, offset + HALO - HALO * odd, 1), message)
    to_near[...] = message
    send_near = remote(to_near, from_near, 1, partner)
    send_near.start()

    loads[6].wait()
    rows = 8 * padded
    wide = 3 * rows
    spread = ((iota((rows, tracers), 0) >> 3) == iota((rows, tracers), 1)).astype(jnp.float32)
    column = iota((tracers, wide), 1)
    column = jnp.where(column >= 2 * rows, column - 2 * rows, jnp.where(column >= rows, column - rows, column))
    gather = ((column >> 3) == iota((tracers, wide), 0)).astype(jnp.float32)
    matrix = exact(exact(spread, k_v[...]), gather)
    same = (iota((rows, wide), 0) & 7) == (iota((rows, wide), 1) & 7)
    matrix = jnp.where(same, matrix, 0.0)
    coarse = matrix.astype(jnp.bfloat16).astype(jnp.float32)
    matrix = jnp.where(iota((rows, wide), 1) < 2 * rows, coarse, matrix - coarse).astype(jnp.bfloat16)
    mix_v[tracers, :, :] = jnp.zeros(mix_v.shape[1:], jnp.float32)
    thin_mix[8 * tracers :, :] = jnp.zeros((8, LANES), jnp.float32)

    for f in range(tracers + 2):
        value = None
        for g in range(groups):
            level = slice(8 * g, 8 * g + 8)
            part = edge_t[f, level, :].astype(jnp.float32) if f < tracers else edge_ub[f - tracers, level, :]
            moved = roll(part, 16 * g + 8, 1)
            value = moved if value is None else jnp.where((thin >> 4) == g, moved, value)
        pack_v[f] = value

    for t in range(tracers):
        s_v[t, :, :slots] = t_v[t].astype(jnp.float32)

    loads[7].wait()
    listed = [
        wet_s[lax.rem(device * WET_DEV + total_wet + j, total_wet)] for j in range(-1, WET_DEV + 1)
    ]
    ring = OCEAN_DEV + 2
    relative = [lax.rem(w - device * OCEAN_DEV + total_tiles + 2, total_tiles) - 2 for w in listed]
    position = [jnp.where(r < 0, r + ring, jnp.where(r < ring, r, ring)) for r in relative]
    is_open = [
        lax.rem(listed[j + 1] - listed[j] + total_tiles, total_tiles) == 1 for j in range(WET_DEV + 1)
    ]
    spot_left, spot, spot_right = position[0], position[1 : WET_DEV + 1], position[WET_DEV + 1]

    tri = (iota((levels, levels), 0) >= iota((levels, levels), 1)).astype(jnp.float32)
    abs_v[:, :slots] = absorbed_light(s_v[0, :, :slots], tri)

    send_near.wait()
    halo_two = jnp.where(even_lane, lane, LANES - 1 - lane) < 2
    halo_three = jnp.where(even_lane, lane, LANES - 1 - lane) < HALO
    for t in range(tracers):
        came = pltpu.roll(from_near[...], 2 * LANES - 2 * t - 2 * odd, 1)
        s_v[t, :, slots:] = jnp.where(halo_two, came, 0.0)
    abs_v[:, slots:] = absorbed_light(s_v[0, :, slots:], tri)
    tile_u.wait()
    tile_b.wait()
    for field, offset, whole in ((u_v, base, tile_in[0]), (b_v, base + HALO, tile_in[1])):
        came = pltpu.roll(from_near[...], 2 * LANES - offset - HALO * odd, 1)
        near = jnp.where(halo_three, came, 0.0)
        field[:, own : own + LANES] = jnp.where(even_lane, whole, near)
        field[:, own + LANES :] = jnp.where(even_lane, near, whole)

    final = None
    for step in range(STEPS):
        width = slots + LANES if step < STEPS - 1 else slots
        light = [abs_v[:, j * LANES : (j + 1) * LANES] for j in range(WET_DEV + 1)]
        heat = []
        for q in range(ring):
            at_halo = jnp.where(lane < LANES // 2, spot_right, spot_left) == q
            term = jnp.where(at_halo, light[WET_DEV], 0.0)
            for j in range(WET_DEV):
                term = jnp.where(spot[j] == q, light[j], term)
            heat.append(term)
        buoyancy = b_v[...] + HEATING * jnp.concatenate(heat, axis=1)
        b_v[...] = buoyancy
        u_v[...] = advance_velocity(u_v[...], buoyancy)
        if step == STEPS - 1:
            place = pl.ds(pl.multiple_of(own + LANES * odd, LANES), LANES)
            final = (
                remote(u_v.at[:, place], tile_back.at[0], 4, partner),
                remote(b_v.at[:, place], tile_back.at[1], 5, partner),
            )
            for copy in final:
                copy.start()
        taken = []
        for field in (u_v, b_v):
            part = [field[:, q * LANES : (q + 1) * LANES] for q in range(ring)]
            chosen = [
                pick(spot[0], [(0, part[0]), (1, part[1]), (2, part[2]), (5, part[5])]),
                pick(spot[1], [(0, part[0]), (1, part[1]), (2, part[2]), (3, part[3])]),
                pick(spot[2], [(1, part[1]), (2, part[2]), (3, part[3]), (4, part[4])]),
            ]
            ahead = pick(spot_right, [(3, part[3]), (4, part[4]), (5, part[5])])
            behind = pick(spot_left, [(0, part[0]), (4, part[4]), (5, part[5])])
            chosen.append(jnp.where(lane < LANES // 2, ahead, behind))
            taken.append(jnp.concatenate(chosen, axis=1))
        gates = []
        for j in range(WET_DEV + 1):
            ends = is_open[(j + 1) % (WET_DEV + 1)].astype(jnp.float32)
            gates.append(jnp.where(lane == LANES - 1, ends, 1.0))
        set_coefficients(coef, taken[0], taken[1], jnp.concatenate(gates, axis=1))
        for t in range(tracers):
            mix_v[t, :, :width] = transport(s_v[t], coef, width)
        for group in range(levels // 16):
            halves = []
            for half in range(2):
                level = slice(group * 16 + half * 8, group * 16 + half * 8 + 8)
                grown = react(
                    mix_v[:, level, :width], coef[6, level, :width], abs_v[level, :width], matrix, tracers
                )
                if step < STEPS - 1:
                    s_v[:, level, :width] = grown
                halves.append(grown)
            if step == STEPS - 1:
                level = slice(group * 16, group * 16 + 16)
                out_v[:, level, :] = jnp.concatenate(halves, axis=1).astype(jnp.bfloat16)
        if step < STEPS - 1:
            abs_v[:, :width] = absorbed_light(s_v[0, :, :width], tri)

    @pl.when(odd == 0)
    def _():
        pl.semaphore_wait(far_ready, 1)
        send_far.start()

    for copy in final:
        copy.wait()
    for field, index in ((u_v, 0), (b_v, 1)):
        back = tile_back[index]
        low_given = jnp.logical_and(odd == 1, spot_left == 0)
        high_given = jnp.logical_and(odd == 0, spot_right == OCEAN_DEV - 1)
        ub_out[index, :, :LANES] = jnp.where(low_given, back, field[:, :LANES])
        ub_out[index, :, LANES : own - LANES] = field[:, LANES : own - LANES]
        ub_out[index, :, own - LANES :] = jnp.where(high_given, back, field[:, own - LANES : own])

    edge_wet = jnp.where(even_lane, relative[1] == 0, relative[WET_DEV] == OCEAN_DEV - 1)
    halo_wet = jnp.where(even_lane, relative[0] == -1, relative[WET_DEV + 1] == OCEAN_DEV)
    column = thin & 15
    distance = jnp.where(even_lane, column - 8, 7 - column)
    edge_wet, halo_wet = edge_wet.astype(jnp.float32), halo_wet.astype(jnp.float32)
    shape = (8, LANES)
    lane = thin
    row = iota(shape, 0)
    level = 8 * (lane >> 4) + row
    inside = jnp.where(even_lane, 7 - column, column - 8)
    halo_two = (inside >= 0) & (inside < 2)
    halo_three = (inside >= 0) & (inside < HALO)

    def above(x):
        turned = roll(x, 1, 0)
        return jnp.where(row == 0, roll(turned, 16, 1), turned)

    def below(x):
        turned = roll(x, -1, 0)
        return jnp.where(row == 7, roll(turned, -16, 1), turned)

    def total_from_top(x):
        for shift in (1, 2, 4):
            x = x + jnp.where(row >= shift, roll(x, shift, 0), 0.0)
        whole = jnp.broadcast_to(x[7:8], shape)
        parts = [jnp.where(lane >= 16 * k, roll(whole, 16 * k, 1), 0.0) for k in range(1, levels // 8)]
        while len(parts) > 1:
            parts = [sum(parts[k : k + 2]) for k in range(0, len(parts), 2)]
        return x + parts[0]

    lit = jnp.where(distance >= 0, edge_wet, halo_wet)
    gate = DT_TRACER * jnp.where(column == 7, edge_wet * halo_wet, 1.0)
    near_side = jnp.where(even_lane, lane, LANES - 1 - lane) < 4
    near_wet = jnp.concatenate([jnp.where(near_side, edge_wet, 0.0)] * 2, axis=0) > 0.5

    send_far.wait()
    state = []
    for t in range(tracers):
        part = from_far[8 * (t // 8) : 8 * (t // 8) + 8, :]
        came = roll(part, -2 * (t % 8) if t < 16 else -2 * HALO, 1)
        state.append(jnp.where(halo_two, came, pack_v[t]))
    fields = []
    for f in range(2):
        came = roll(from_far[16:24, :], -HALO * f, 1)
        fields.append(jnp.where(halo_three, came, pack_v[tracers + f]))
    velocity, buoyancy = fields
    for step in range(STEPS):
        attenuation = WATER_ATT + PIGMENT_ATT * state[0] * state[0]
        depth = total_from_top(attenuation)
        light = SURFACE_LIGHT * (jnp.exp(attenuation - depth) - jnp.exp(-depth))
        buoyancy = buoyancy + HEATING * lit * light
        horiz = roll(velocity, 1, 1) + roll(velocity, -1, 1) - 2.0 * velocity
        upper = jnp.where(level == 0, velocity, above(velocity))
        lower = jnp.where(level == levels - 1, velocity, below(velocity))
        press = roll(buoyancy, -1, 1) - buoyancy
        velocity = velocity + DT_OCEAN * (
            HORIZ_VISC * horiz + VERT_VISC * (upper + lower - 2.0 * velocity) - PRESSURE * press
        )
        shear, settled = velocity - below(velocity), buoyancy - below(buoyancy)
        spreading = jnp.where(level == levels - 1, 0.0, diffusivity(shear, settled))
        shear, settled = above(velocity) - velocity, above(buoyancy) - buoyancy
        spreading_up = jnp.where(level == 0, 0.0, diffusivity(shear, settled))
        forward = jnp.maximum(velocity, 0.0) * gate
        backward = jnp.minimum(velocity, 0.0) * gate
        stay = 1.0 - forward + roll(backward, 1, 1)
        from_left = roll(forward, 1, 1)
        keep = 1.0 - DT_MIX * (spreading + spreading_up)
        warm = KINETIC_DELTA * jnp.exp(THERMAL_GAIN * buoyancy)
        mixed = []
        for t in range(tracers):
            moved = stay * state[t] - backward * roll(state[t], -1, 1) + from_left * roll(state[t], 1, 1)
            mixed.append(
                keep * moved + DT_MIX * (spreading * below(moved) + spreading_up * above(moved))
            )
            thin_mix[8 * t : 8 * t + 8, :] = mixed[t]
        flat = thin_mix[...]
        high = flat.astype(jnp.bfloat16)
        low = (flat - high.astype(jnp.float32)).astype(jnp.bfloat16)
        drift = jnp.dot(
            matrix, jnp.concatenate([high, low, high], axis=0), preferred_element_type=jnp.float32
        )
        state = [mixed[t] + warm * drift[8 * t : 8 * t + 8] for t in range(tracers)]
        state[0] = state[0] + GROWTH * light

    for f, field in enumerate((velocity, buoyancy)):
        for g in range(groups):
            rows = slice(8 * g, 8 * g + 8)
            kept = ub_out[f, rows, far_edge]
            ub_out[f, rows, far_edge] = jnp.where(near_side, roll(field, -16 * g - 8, 1), kept)
    for t in range(tracers):
        for g in range(levels // 16):
            rows = slice(16 * g, 16 * g + 16)
            fresh = jnp.concatenate(
                [roll(state[t], -32 * g - 8, 1), roll(state[t], -32 * g - 24, 1)], axis=0
            )
            kept = out_v[t, rows, slot_edge].astype(jnp.float32)
            out_v[t, rows, slot_edge] = jnp.where(near_wet, fresh, kept).astype(jnp.bfloat16)


def finish(t_v, ub_v, t_out, u_out, b_out, sems):
    copies = [
        pltpu.make_async_copy(t_v, t_out, sems.at[0]),
        pltpu.make_async_copy(ub_v.at[0], u_out, sems.at[1]),
        pltpu.make_async_copy(ub_v.at[1], b_out, sems.at[2]),
    ]
    for copy in copies:
        copy.start()
    for copy in copies:
        copy.wait()


def on_device(ocean_u, ocean_b, tracers, wet_tiles, kinetic_matrix):
    levels, own = ocean_u.shape
    count, _, slots = tracers.shape
    padded = count + count % 2
    wide = slots + LANES
    domain = own + 2 * LANES
    f32, bf16 = jnp.float32, jnp.bfloat16
    hbm = pl.BlockSpec(memory_space=pltpu.HBM)
    vmem = pl.BlockSpec(memory_space=pltpu.VMEM)
    operands = [
        pltpu.with_memory_space_constraint(x, pltpu.HBM)
        for x in (ocean_u, ocean_b, tracers, wet_tiles, kinetic_matrix)
    ]
    rows = 8 * padded
    parts = pl.pallas_call(
        functools.partial(kernel, lax.axis_size("sec"), lax.axis_size("tile")),
        out_shape=(
            jax.ShapeDtypeStruct(tracers.shape, bf16),
            jax.ShapeDtypeStruct((2, levels, own), f32),
        ),
        in_specs=[hbm] * 5,
        out_specs=(vmem,) * 2,
        scratch_shapes=[
            pltpu.VMEM((levels, domain), f32),
            pltpu.VMEM((levels, domain), f32),
            pltpu.VMEM(tracers.shape, bf16),
            pltpu.VMEM(kinetic_matrix.shape, f32),
            pltpu.SMEM(wet_tiles.shape, jnp.int32),
            pltpu.VMEM((count, levels, LANES), bf16),
            pltpu.VMEM((2, levels, LANES), f32),
            pltpu.VMEM((levels, LANES), f32),
            pltpu.VMEM((24, LANES), f32),
            pltpu.VMEM((levels, LANES), f32),
            pltpu.VMEM((24, LANES), f32),
            pltpu.VMEM((2, levels, LANES), f32),
            pltpu.VMEM((2, levels, LANES), f32),
            pltpu.VMEM((count, levels, wide), f32),
            pltpu.VMEM((padded, levels, wide), f32),
            pltpu.VMEM((levels, wide), f32),
            pltpu.VMEM((7, levels, wide), f32),
            pltpu.VMEM((count + 2, 8, LANES), f32),
            pltpu.VMEM((rows, LANES), f32),
            pltpu.SemaphoreType.DMA((7,)),
            pltpu.SemaphoreType.DMA,
            pltpu.SemaphoreType.DMA((6,)),
            pltpu.SemaphoreType.DMA((6,)),
            pltpu.SemaphoreType.REGULAR,
            pltpu.SemaphoreType.REGULAR,
        ],
        compiler_params=pltpu.CompilerParams(
            collective_id=0, has_side_effects=True, vmem_limit_bytes=40 * 2**20
        ),
    )(*operands)
    return pl.pallas_call(
        finish,
        out_shape=(
            jax.ShapeDtypeStruct(tracers.shape, bf16),
            jax.ShapeDtypeStruct(ocean_u.shape, f32),
            jax.ShapeDtypeStruct(ocean_b.shape, f32),
        ),
        in_specs=[vmem] * 2,
        out_specs=(hbm, hbm, hbm),
        scratch_shapes=[pltpu.SemaphoreType.DMA((3,))],
        compiler_params=pltpu.CompilerParams(vmem_limit_bytes=2**20),
    )(*parts)


def solution(mesh):
    flat = ("sec", "tile")
    placed = (P(None, flat), P(None, flat), P(None, None, flat), P(), P())
    return jax.shard_map(
        on_device,
        mesh=mesh,
        in_specs=placed,
        out_specs=(P(None, None, flat), P(None, flat), P(None, flat)),
        check_vma=False,
    )
```

```python
import functools

import jax
import jax.numpy as jnp
from jax import lax
from jax.experimental import pallas as pl
from jax.experimental.pallas import tpu as pltpu
from jax.sharding import PartitionSpec as P

MESH = pl.DeviceIdType.MESH
LANES = 128
STEPS = 2
WET_DEV = 3
OCEAN_DEV = 4
HALO = 3

DT_OCEAN = 0.25
PRESSURE = 1.0
HORIZ_VISC = 0.2
VERT_VISC = 0.2
HEATING = 0.2
KAPPA_BASE = 0.05
KAPPA_SPAN = 0.35
DT_TRACER = 0.3
DT_MIX = 1.0
KINETIC_DELTA = 0.5
SURFACE_LIGHT = 10.0
WATER_ATT = 0.04
PIGMENT_ATT = 0.08
GROWTH = 0.05
THERMAL_GAIN = 0.1


def roll(x, shift, axis):
    size = x.shape[axis]
    shift = shift % size
    return x if shift == 0 else pltpu.roll(x, shift, axis)


def iota(shape, axis):
    return lax.broadcasted_iota(jnp.int32, shape, axis)


def pick(position, options):
    value = None
    for where, option in options:
        value = option if value is None else jnp.where(position == where, option, value)
    return value


def exact(a, b):
    return jnp.dot(a, b, precision=lax.Precision.HIGHEST, preferred_element_type=jnp.float32)


def absorbed_light(pigment, tri):
    attenuation = WATER_ATT + PIGMENT_ATT * pigment * pigment
    below = jnp.exp(-exact(tri, attenuation))
    above = jnp.where(iota(pigment.shape, 0) == 0, 1.0, roll(below, 1, 0))
    return SURFACE_LIGHT * (above - below)


def advance_velocity(velocity, buoyancy):
    level = iota(velocity.shape, 0)
    horiz = roll(velocity, 1, 1) + roll(velocity, -1, 1) - 2.0 * velocity
    press = roll(buoyancy, -1, 1) - buoyancy
    upper = jnp.where(level == 0, velocity, roll(velocity, 1, 0))
    lower = jnp.where(level == velocity.shape[0] - 1, velocity, roll(velocity, -1, 0))
    vert = upper + lower - 2.0 * velocity
    return velocity + DT_OCEAN * (HORIZ_VISC * horiz + VERT_VISC * vert - PRESSURE * press)


def diffusivity(shear, settled):
    steep = 4.0 * (shear * shear - settled)
    return KAPPA_BASE + KAPPA_SPAN / (1.0 + jnp.exp(-steep))


def set_coefficients(coef, face_u, warmth, gate):
    level = iota(face_u.shape, 0)
    shear = face_u - roll(face_u, -1, 0)
    stratified = warmth - roll(warmth, -1, 0)
    spreading = diffusivity(shear, stratified)
    spreading = jnp.where(level == face_u.shape[0] - 1, 0.0, spreading)
    spreading_up = jnp.where(level == 0, 0.0, roll(spreading, 1, 0))
    gate = DT_TRACER * gate
    forward = jnp.maximum(face_u, 0.0) * gate
    backward = jnp.minimum(face_u, 0.0) * gate
    coef[0] = 1.0 - forward + roll(backward, 1, 1)
    coef[1] = -backward
    coef[2] = roll(forward, 1, 1)
    coef[3] = 1.0 - DT_MIX * (spreading + spreading_up)
    coef[4] = DT_MIX * spreading
    coef[5] = DT_MIX * spreading_up
    coef[6] = KINETIC_DELTA * jnp.exp(THERMAL_GAIN * warmth)


def transport(state, coef, width):
    moved = (coef[0] * state + coef[1] * roll(state, -1, 1) + coef[2] * roll(state, 1, 1))[:, :width]
    return (
        coef[3][:, :width] * moved
        + coef[4][:, :width] * roll(moved, -1, 0)
        + coef[5][:, :width] * roll(moved, 1, 0)
    )


def react(mixed, warm, light, matrix, tracers):
    padded, rows, width = mixed.shape
    flat = mixed.reshape(padded * rows, width)
    high = flat.astype(jnp.bfloat16)
    low = (flat - high.astype(jnp.float32)).astype(jnp.bfloat16)
    drift = jnp.dot(
        matrix, jnp.concatenate([high, low, high], axis=0), preferred_element_type=jnp.float32
    ).reshape(padded, rows, width)
    grown = mixed + warm[None] * drift
    return jnp.concatenate([(grown[0] + GROWTH * light)[None], grown[1:tracers]], axis=0)


def kernel(
    secs, tiles, u_in, b_in, t_in, wet_in, k_in,
    out_v, ub_out,
    u_v, b_v, t_v, k_v, wet_s, edge_t, edge_ub, to_near, to_far, from_near, from_far, tile_in, tile_back,
    s_v, mix_v, abs_v, coef, pack_v, thin_mix,
    load_sem, wet_sem, send_sem, recv_sem, far_ready, near_ready,
):
    levels = u_in.shape[0]
    tracers = t_in.shape[0]
    padded = mix_v.shape[0]
    total_wet = WET_DEV * secs * tiles
    total_tiles = OCEAN_DEV * secs * tiles
    own = OCEAN_DEV * LANES
    slots = WET_DEV * LANES
    sec = lax.axis_index("sec")
    tile = lax.axis_index("tile")
    device = sec * tiles + tile
    odd = lax.rem(tile, 2)
    even_lane = odd == 0
    partner = (sec, tile + 1 - 2 * odd)
    far_flat = lax.rem(device + 2 * odd - 1 + secs * tiles, secs * tiles)
    far = (far_flat // tiles, lax.rem(far_flat, tiles))

    slot_edge = pl.ds(pl.multiple_of((slots - LANES) * odd, LANES), LANES)
    far_edge = pl.ds(pl.multiple_of((own - LANES) * odd, LANES), LANES)
    near_edge = pl.ds(pl.multiple_of((own - LANES) * (1 - odd), LANES), LANES)
    loads = [
        pltpu.make_async_copy(t_in.at[:, :, slot_edge], edge_t, load_sem.at[0]),
        pltpu.make_async_copy(u_in.at[:, far_edge], edge_ub.at[0], load_sem.at[1]),
        pltpu.make_async_copy(b_in.at[:, far_edge], edge_ub.at[1], load_sem.at[2]),
        pltpu.make_async_copy(t_in, t_v, load_sem.at[0]),
        pltpu.make_async_copy(u_in, u_v.at[:, pl.ds(0, own)], load_sem.at[1]),
        pltpu.make_async_copy(b_in, b_v.at[:, pl.ds(0, own)], load_sem.at[2]),
        pltpu.make_async_copy(k_in, k_v, load_sem.at[3]),
        pltpu.make_async_copy(wet_in, wet_s, wet_sem),
    ]
    for load in loads[:3]:
        load.start()

    barrier = pltpu.get_barrier_semaphore()
    greeted = (jnp.where(even_lane, far[0], partner[0]), jnp.where(even_lane, far[1], partner[1]))
    pl.semaphore_signal(barrier, inc=1, device_id=greeted, device_id_type=MESH)

    def remote(src, dst, index, target):
        return pltpu.make_async_remote_copy(
            src_ref=src, dst_ref=dst, send_sem=send_sem.at[index], recv_sem=recv_sem.at[index],
            device_id=target, device_id_type=MESH,
        )

    lane = iota((levels, LANES), 1)
    base = 2 * tracers
    for load in loads[:3]:
        load.wait()
    for load in loads[3:]:
        load.start()
    thin = iota((8, LANES), 1)
    groups = levels // 8
    frame = (thin + (LANES - 8 + 2 * odd)) & (LANES - 1)
    last_frame = (thin + (LANES - 8 + HALO * odd)) & (LANES - 1)
    for part in range(3):
        spots = frame if part < 2 else last_frame
        within = spots & 15
        value = None
        for g in range(groups):
            level = slice(8 * g, 8 * g + 8)
            natural = 16 * g + 8
            if part < 2:
                chunk = None
                for k in range(8):
                    moved = roll(edge_t[8 * part + k, level, :].astype(jnp.float32), natural + 2 * k, 1)
                    chunk = moved if chunk is None else jnp.where(within >= 2 * k, moved, chunk)
            else:
                chunk = roll(edge_ub[0, level, :], natural, 1)
                chunk = jnp.where(within >= HALO, roll(edge_ub[1, level, :], natural + HALO, 1), chunk)
                moved = roll(edge_t[tracers - 1, level, :].astype(jnp.float32), natural + 2 * HALO, 1)
                chunk = jnp.where(within >= 2 * HALO, moved, chunk)
            value = chunk if value is None else jnp.where((spots >> 4) == g, chunk, value)
        to_far[8 * part : 8 * part + 8, :] = value

    pl.semaphore_wait(barrier, 1)
    send_far = remote(to_far, from_far, 0, far)

    @pl.when(odd == 1)
    def _():
        pl.semaphore_signal(far_ready, inc=1, device_id=far, device_id_type=MESH)
        send_far.start()
        pl.semaphore_wait(near_ready, 1)

    @pl.when(odd == 0)
    def _():
        pl.semaphore_signal(near_ready, inc=1, device_id=partner, device_id_type=MESH)

    tile_u = remote(u_in.at[:, near_edge], tile_in.at[0], 2, partner)
    tile_b = remote(b_in.at[:, near_edge], tile_in.at[1], 3, partner)
    tile_u.start()
    tile_b.start()

    for load in loads[3:6]:
        load.wait()
    message = jnp.zeros((levels, LANES), jnp.float32)
    for t in range(tracers):
        here = (lane >= 2 * t) & (lane < 2 * t + 2)
        near = jnp.where(even_lane, t_v[t, :, slots - LANES :], t_v[t, :, :LANES]).astype(jnp.float32)
        message = jnp.where(here, pltpu.roll(near, 2 * t + 2 - 2 * odd, 1), message)
    for field, offset in ((u_v, base), (b_v, base + HALO)):
        here = (lane >= offset) & (lane < offset + HALO)
        near = jnp.where(even_lane, field[:, 2 * LANES : 3 * LANES], field[:, LANES : 2 * LANES])
        message = jnp.where(here, pltpu.roll(near, offset + HALO - HALO * odd, 1), message)
    to_near[...] = message
    send_near = remote(to_near, from_near, 1, partner)
    send_near.start()

    loads[6].wait()
    rows = 8 * padded
    wide = 3 * rows
    spread = ((iota((rows, tracers), 0) >> 3) == iota((rows, tracers), 1)).astype(jnp.float32)
    column = iota((tracers, wide), 1)
    column = jnp.where(column >= 2 * rows, column - 2 * rows, jnp.where(column >= rows, column - rows, column))
    gather = ((column >> 3) == iota((tracers, wide), 0)).astype(jnp.float32)
    matrix = exact(exact(spread, k_v[...]), gather)
    same = (iota((rows, wide), 0) & 7) == (iota((rows, wide), 1) & 7)
    matrix = jnp.where(same, matrix, 0.0)
    coarse = matrix.astype(jnp.bfloat16).astype(jnp.float32)
    matrix = jnp.where(iota((rows, wide), 1) < 2 * rows, coarse, matrix - coarse).astype(jnp.bfloat16)
    mix_v[tracers, :, :] = jnp.zeros(mix_v.shape[1:], jnp.float32)
    thin_mix[8 * tracers :, :] = jnp.zeros((8, LANES), jnp.float32)

    for f in range(tracers + 2):
        value = None
        for g in range(groups):
            level = slice(8 * g, 8 * g + 8)
            part = edge_t[f, level, :].astype(jnp.float32) if f < tracers else edge_ub[f - tracers, level, :]
            moved = roll(part, 16 * g + 8, 1)
            value = moved if value is None else jnp.where((thin >> 4) == g, moved, value)
        pack_v[f] = value

    for t in range(tracers):
        s_v[t, :, :slots] = t_v[t].astype(jnp.float32)

    loads[7].wait()
    listed = [
        wet_s[lax.rem(device * WET_DEV + total_wet + j, total_wet)] for j in range(-1, WET_DEV + 1)
    ]
    ring = OCEAN_DEV + 2
    relative = [lax.rem(w - device * OCEAN_DEV + total_tiles + 2, total_tiles) - 2 for w in listed]
    position = [jnp.where(r < 0, r + ring, jnp.where(r < ring, r, ring)) for r in relative]
    is_open = [
        lax.rem(listed[j + 1] - listed[j] + total_tiles, total_tiles) == 1 for j in range(WET_DEV + 1)
    ]
    spot_left, spot, spot_right = position[0], position[1 : WET_DEV + 1], position[WET_DEV + 1]

    tri = (iota((levels, levels), 0) >= iota((levels, levels), 1)).astype(jnp.float32)
    abs_v[:, :slots] = absorbed_light(s_v[0, :, :slots], tri)

    send_near.wait()
    halo_two = jnp.where(even_lane, lane, LANES - 1 - lane) < 2
    halo_three = jnp.where(even_lane, lane, LANES - 1 - lane) < HALO
    for t in range(tracers):
        came = pltpu.roll(from_near[...], 2 * LANES - 2 * t - 2 * odd, 1)
        s_v[t, :, slots:] = jnp.where(halo_two, came, 0.0)
    abs_v[:, slots:] = absorbed_light(s_v[0, :, slots:], tri)
    tile_u.wait()
    tile_b.wait()
    for field, offset, whole in ((u_v, base, tile_in[0]), (b_v, base + HALO, tile_in[1])):
        came = pltpu.roll(from_near[...], 2 * LANES - offset - HALO * odd, 1)
        near = jnp.where(halo_three, came, 0.0)
        field[:, own : own + LANES] = jnp.where(even_lane, whole, near)
        field[:, own + LANES :] = jnp.where(even_lane, near, whole)

    final = None
    for step in range(STEPS):
        width = slots + LANES if step < STEPS - 1 else slots
        light = [abs_v[:, j * LANES : (j + 1) * LANES] for j in range(WET_DEV + 1)]
        heat = []
        for q in range(ring):
            at_halo = jnp.where(lane < LANES // 2, spot_right, spot_left) == q
            term = jnp.where(at_halo, light[WET_DEV], 0.0)
            for j in range(WET_DEV):
                term = jnp.where(spot[j] == q, light[j], term)
            heat.append(term)
        buoyancy = b_v[...] + HEATING * jnp.concatenate(heat, axis=1)
        b_v[...] = buoyancy
        u_v[...] = advance_velocity(u_v[...], buoyancy)
        if step == STEPS - 1:
            place = pl.ds(pl.multiple_of(own + LANES * odd, LANES), LANES)
            final = (
                remote(u_v.at[:, place], tile_back.at[0], 4, partner),
                remote(b_v.at[:, place], tile_back.at[1], 5, partner),
            )
            for copy in final:
                copy.start()
        taken = []
        for field in (u_v, b_v):
            part = [field[:, q * LANES : (q + 1) * LANES] for q in range(ring)]
            chosen = [
                pick(spot[0], [(0, part[0]), (1, part[1]), (2, part[2]), (5, part[5])]),
                pick(spot[1], [(0, part[0]), (1, part[1]), (2, part[2]), (3, part[3])]),
                pick(spot[2], [(1, part[1]), (2, part[2]), (3, part[3]), (4, part[4])]),
            ]
            ahead = pick(spot_right, [(3, part[3]), (4, part[4]), (5, part[5])])
            behind = pick(spot_left, [(0, part[0]), (4, part[4]), (5, part[5])])
            chosen.append(jnp.where(lane < LANES // 2, ahead, behind))
            taken.append(jnp.concatenate(chosen, axis=1))
        gates = []
        for j in range(WET_DEV + 1):
            ends = is_open[(j + 1) % (WET_DEV + 1)].astype(jnp.float32)
            gates.append(jnp.where(lane == LANES - 1, ends, 1.0))
        set_coefficients(coef, taken[0], taken[1], jnp.concatenate(gates, axis=1))
        for t in range(tracers):
            mix_v[t, :, :width] = transport(s_v[t], coef, width)
        for group in range(levels // 16):
            halves = []
            for half in range(2):
                level = slice(group * 16 + half * 8, group * 16 + half * 8 + 8)
                grown = react(
                    mix_v[:, level, :width], coef[6, level, :width], abs_v[level, :width], matrix, tracers
                )
                if step < STEPS - 1:
                    s_v[:, level, :width] = grown
                halves.append(grown)
            if step == STEPS - 1:
                level = slice(group * 16, group * 16 + 16)
                out_v[:, level, :] = jnp.concatenate(halves, axis=1).astype(jnp.bfloat16)
        if step < STEPS - 1:
            abs_v[:, :width] = absorbed_light(s_v[0, :, :width], tri)

    @pl.when(odd == 0)
    def _():
        pl.semaphore_wait(far_ready, 1)
        send_far.start()

    for copy in final:
        copy.wait()
    for field, index in ((u_v, 0), (b_v, 1)):
        back = tile_back[index]
        low_given = jnp.logical_and(odd == 1, spot_left == 0)
        high_given = jnp.logical_and(odd == 0, spot_right == OCEAN_DEV - 1)
        ub_out[index, :, :LANES] = jnp.where(low_given, back, field[:, :LANES])
        ub_out[index, :, LANES : own - LANES] = field[:, LANES : own - LANES]
        ub_out[index, :, own - LANES :] = jnp.where(high_given, back, field[:, own - LANES : own])

    edge_wet = jnp.where(even_lane, relative[1] == 0, relative[WET_DEV] == OCEAN_DEV - 1)
    halo_wet = jnp.where(even_lane, relative[0] == -1, relative[WET_DEV + 1] == OCEAN_DEV)
    column = thin & 15
    distance = jnp.where(even_lane, column - 8, 7 - column)
    edge_wet, halo_wet = edge_wet.astype(jnp.float32), halo_wet.astype(jnp.float32)
    shape = (8, LANES)
    lane = thin
    row = iota(shape, 0)
    level = 8 * (lane >> 4) + row
    inside = jnp.where(even_lane, 7 - column, column - 8)
    halo_two = (inside >= 0) & (inside < 2)
    halo_three = (inside >= 0) & (inside < HALO)

    def above(x):
        turned = roll(x, 1, 0)
        return jnp.where(row == 0, roll(turned, 16, 1), turned)

    def below(x):
        turned = roll(x, -1, 0)
        return jnp.where(row == 7, roll(turned, -16, 1), turned)

    def total_from_top(x):
        for shift in (1, 2, 4):
            x = x + jnp.where(row >= shift, roll(x, shift, 0), 0.0)
        whole = jnp.broadcast_to(x[7:8], shape)
        parts = [jnp.where(lane >= 16 * k, roll(whole, 16 * k, 1), 0.0) for k in range(1, levels // 8)]
        while len(parts) > 1:
            parts = [sum(parts[k : k + 2]) for k in range(0, len(parts), 2)]
        return x + parts[0]

    lit = jnp.where(distance >= 0, edge_wet, halo_wet)
    gate = DT_TRACER * jnp.where(column == 7, edge_wet * halo_wet, 1.0)
    near_side = jnp.where(even_lane, lane, LANES - 1 - lane) < 4
    near_wet = jnp.concatenate([jnp.where(near_side, edge_wet, 0.0)] * 2, axis=0) > 0.5

    send_far.wait()
    state = []
    for t in range(tracers):
        part = from_far[8 * (t // 8) : 8 * (t // 8) + 8, :]
        came = roll(part, -2 * (t % 8) if t < 16 else -2 * HALO, 1)
        state.append(jnp.where(halo_two, came, pack_v[t]))
    fields = []
    for f in range(2):
        came = roll(from_far[16:24, :], -HALO * f, 1)
        fields.append(jnp.where(halo_three, came, pack_v[tracers + f]))
    velocity, buoyancy = fields
    for step in range(STEPS):
        attenuation = WATER_ATT + PIGMENT_ATT * state[0] * state[0]
        depth = total_from_top(attenuation)
        light = SURFACE_LIGHT * (jnp.exp(attenuation - depth) - jnp.exp(-depth))
        buoyancy = buoyancy + HEATING * lit * light
        horiz = roll(velocity, 1, 1) + roll(velocity, -1, 1) - 2.0 * velocity
        upper = jnp.where(level == 0, velocity, above(velocity))
        lower = jnp.where(level == levels - 1, velocity, below(velocity))
        press = roll(buoyancy, -1, 1) - buoyancy
        velocity = velocity + DT_OCEAN * (
            HORIZ_VISC * horiz + VERT_VISC * (upper + lower - 2.0 * velocity) - PRESSURE * press
        )
        shear, settled = velocity - below(velocity), buoyancy - below(buoyancy)
        spreading = jnp.where(level == levels - 1, 0.0, diffusivity(shear, settled))
        shear, settled = above(velocity) - velocity, above(buoyancy) - buoyancy
        spreading_up = jnp.where(level == 0, 0.0, diffusivity(shear, settled))
        forward = jnp.maximum(velocity, 0.0) * gate
        backward = jnp.minimum(velocity, 0.0) * gate
        stay = 1.0 - forward + roll(backward, 1, 1)
        from_left = roll(forward, 1, 1)
        keep = 1.0 - DT_MIX * (spreading + spreading_up)
        warm = KINETIC_DELTA * jnp.exp(THERMAL_GAIN * buoyancy)
        mixed = []
        for t in range(tracers):
            moved = stay * state[t] - backward * roll(state[t], -1, 1) + from_left * roll(state[t], 1, 1)
            mixed.append(
                keep * moved + DT_MIX * (spreading * below(moved) + spreading_up * above(moved))
            )
            thin_mix[8 * t : 8 * t + 8, :] = mixed[t]
        flat = thin_mix[...]
        high = flat.astype(jnp.bfloat16)
        low = (flat - high.astype(jnp.float32)).astype(jnp.bfloat16)
        drift = jnp.dot(
            matrix, jnp.concatenate([high, low, high], axis=0), preferred_element_type=jnp.float32
        )
        state = [mixed[t] + warm * drift[8 * t : 8 * t + 8] for t in range(tracers)]
        state[0] = state[0] + GROWTH * light

    for f, field in enumerate((velocity, buoyancy)):
        for g in range(groups):
            rows = slice(8 * g, 8 * g + 8)
            kept = ub_out[f, rows, far_edge]
            ub_out[f, rows, far_edge] = jnp.where(near_side, roll(field, -16 * g - 8, 1), kept)
    for t in range(tracers):
        for g in range(levels // 16):
            rows = slice(16 * g, 16 * g + 16)
            fresh = jnp.concatenate(
                [roll(state[t], -32 * g - 8, 1), roll(state[t], -32 * g - 24, 1)], axis=0
            )
            kept = out_v[t, rows, slot_edge].astype(jnp.float32)
            out_v[t, rows, slot_edge] = jnp.where(near_wet, fresh, kept).astype(jnp.bfloat16)


def finish(t_v, ub_v, t_out, u_out, b_out, sems):
    copies = [
        pltpu.make_async_copy(t_v, t_out, sems.at[0]),
        pltpu.make_async_copy(ub_v.at[0], u_out, sems.at[1]),
        pltpu.make_async_copy(ub_v.at[1], b_out, sems.at[2]),
    ]
    for copy in copies:
        copy.start()
    for copy in copies:
        copy.wait()


def on_device(ocean_u, ocean_b, tracers, wet_tiles, kinetic_matrix):
    levels, own = ocean_u.shape
    count, _, slots = tracers.shape
    padded = count + count % 2
    wide = slots + LANES
    domain = own + 2 * LANES
    f32, bf16 = jnp.float32, jnp.bfloat16
    hbm = pl.BlockSpec(memory_space=pltpu.HBM)
    vmem = pl.BlockSpec(memory_space=pltpu.VMEM)
    operands = [
        pltpu.with_memory_space_constraint(x, pltpu.HBM)
        for x in (ocean_u, ocean_b, tracers, wet_tiles, kinetic_matrix)
    ]
    rows = 8 * padded
    parts = pl.pallas_call(
        functools.partial(kernel, lax.axis_size("sec"), lax.axis_size("tile")),
        out_shape=(
            jax.ShapeDtypeStruct(tracers.shape, bf16),
            jax.ShapeDtypeStruct((2, levels, own), f32),
        ),
        in_specs=[hbm] * 5,
        out_specs=(vmem,) * 2,
        scratch_shapes=[
            pltpu.VMEM((levels, domain), f32),
            pltpu.VMEM((levels, domain), f32),
            pltpu.VMEM(tracers.shape, bf16),
            pltpu.VMEM(kinetic_matrix.shape, f32),
            pltpu.SMEM(wet_tiles.shape, jnp.int32),
            pltpu.VMEM((count, levels, LANES), bf16),
            pltpu.VMEM((2, levels, LANES), f32),
            pltpu.VMEM((levels, LANES), f32),
            pltpu.VMEM((24, LANES), f32),
            pltpu.VMEM((levels, LANES), f32),
            pltpu.VMEM((24, LANES), f32),
            pltpu.VMEM((2, levels, LANES), f32),
            pltpu.VMEM((2, levels, LANES), f32),
            pltpu.VMEM((count, levels, wide), f32),
            pltpu.VMEM((padded, levels, wide), f32),
            pltpu.VMEM((levels, wide), f32),
            pltpu.VMEM((7, levels, wide), f32),
            pltpu.VMEM((count + 2, 8, LANES), f32),
            pltpu.VMEM((rows, LANES), f32),
            pltpu.SemaphoreType.DMA((4,)),
            pltpu.SemaphoreType.DMA,
            pltpu.SemaphoreType.DMA((6,)),
            pltpu.SemaphoreType.DMA((6,)),
            pltpu.SemaphoreType.REGULAR,
            pltpu.SemaphoreType.REGULAR,
        ],
        compiler_params=pltpu.CompilerParams(
            collective_id=0, has_side_effects=True, vmem_limit_bytes=40 * 2**20
        ),
    )(*operands)
    return pl.pallas_call(
        finish,
        out_shape=(
            jax.ShapeDtypeStruct(tracers.shape, bf16),
            jax.ShapeDtypeStruct(ocean_u.shape, f32),
            jax.ShapeDtypeStruct(ocean_b.shape, f32),
        ),
        in_specs=[vmem] * 2,
        out_specs=(hbm, hbm, hbm),
        scratch_shapes=[pltpu.SemaphoreType.DMA((3,))],
        compiler_params=pltpu.CompilerParams(vmem_limit_bytes=2**20),
    )(*parts)


def solution(mesh):
    flat = ("sec", "tile")
    placed = (P(None, flat), P(None, flat), P(None, None, flat), P(), P())
    return jax.shard_map(
        on_device,
        mesh=mesh,
        in_specs=placed,
        out_specs=(P(None, None, flat), P(None, flat), P(None, flat)),
        check_vma=False,
    )
```

```python
import functools

import jax
import jax.numpy as jnp
from jax import lax
from jax.experimental import pallas as pl
from jax.experimental.pallas import tpu as pltpu
from jax.sharding import PartitionSpec as P

MESH = pl.DeviceIdType.MESH
LANES = 128
STEPS = 2
WET_DEV = 3
OCEAN_DEV = 4
HALO = 3

DT_OCEAN = 0.25
PRESSURE = 1.0
HORIZ_VISC = 0.2
VERT_VISC = 0.2
HEATING = 0.2
KAPPA_BASE = 0.05
KAPPA_SPAN = 0.35
DT_TRACER = 0.3
DT_MIX = 1.0
KINETIC_DELTA = 0.5
SURFACE_LIGHT = 10.0
WATER_ATT = 0.04
PIGMENT_ATT = 0.08
GROWTH = 0.05
THERMAL_GAIN = 0.1


def roll(x, shift, axis):
    size = x.shape[axis]
    shift = shift % size
    return x if shift == 0 else pltpu.roll(x, shift, axis)


def iota(shape, axis):
    return lax.broadcasted_iota(jnp.int32, shape, axis)


def pick(position, options):
    value = None
    for where, option in options:
        value = option if value is None else jnp.where(position == where, option, value)
    return value


def exact(a, b):
    return jnp.dot(a, b, precision=lax.Precision.HIGHEST, preferred_element_type=jnp.float32)


def absorbed_light(pigment, tri):
    attenuation = WATER_ATT + PIGMENT_ATT * pigment * pigment
    below = jnp.exp(-exact(tri, attenuation))
    above = jnp.where(iota(pigment.shape, 0) == 0, 1.0, roll(below, 1, 0))
    return SURFACE_LIGHT * (above - below)


def advance_velocity(velocity, buoyancy):
    level = iota(velocity.shape, 0)
    horiz = roll(velocity, 1, 1) + roll(velocity, -1, 1) - 2.0 * velocity
    press = roll(buoyancy, -1, 1) - buoyancy
    upper = jnp.where(level == 0, velocity, roll(velocity, 1, 0))
    lower = jnp.where(level == velocity.shape[0] - 1, velocity, roll(velocity, -1, 0))
    vert = upper + lower - 2.0 * velocity
    return velocity + DT_OCEAN * (HORIZ_VISC * horiz + VERT_VISC * vert - PRESSURE * press)


def diffusivity(shear, settled):
    steep = 4.0 * (shear * shear - settled)
    return KAPPA_BASE + KAPPA_SPAN / (1.0 + jnp.exp(-steep))


def set_coefficients(coef, face_u, warmth, gate):
    level = iota(face_u.shape, 0)
    shear = face_u - roll(face_u, -1, 0)
    stratified = warmth - roll(warmth, -1, 0)
    spreading = diffusivity(shear, stratified)
    spreading = jnp.where(level == face_u.shape[0] - 1, 0.0, spreading)
    spreading_up = jnp.where(level == 0, 0.0, roll(spreading, 1, 0))
    gate = DT_TRACER * gate
    forward = jnp.maximum(face_u, 0.0) * gate
    backward = jnp.minimum(face_u, 0.0) * gate
    coef[0] = 1.0 - forward + roll(backward, 1, 1)
    coef[1] = -backward
    coef[2] = roll(forward, 1, 1)
    coef[3] = 1.0 - DT_MIX * (spreading + spreading_up)
    coef[4] = DT_MIX * spreading
    coef[5] = DT_MIX * spreading_up
    coef[6] = KINETIC_DELTA * jnp.exp(THERMAL_GAIN * warmth)


def transport(state, coef, width):
    moved = (coef[0] * state + coef[1] * roll(state, -1, 1) + coef[2] * roll(state, 1, 1))[:, :width]
    return (
        coef[3][:, :width] * moved
        + coef[4][:, :width] * roll(moved, -1, 0)
        + coef[5][:, :width] * roll(moved, 1, 0)
    )


def react(mixed, warm, light, matrix, tracers):
    padded, rows, width = mixed.shape
    flat = mixed.reshape(padded * rows, width)
    high = flat.astype(jnp.bfloat16)
    low = (flat - high.astype(jnp.float32)).astype(jnp.bfloat16)
    drift = jnp.dot(
        matrix, jnp.concatenate([high, low, high], axis=0), preferred_element_type=jnp.float32
    ).reshape(padded, rows, width)
    grown = mixed + warm[None] * drift
    return jnp.concatenate([(grown[0] + GROWTH * light)[None], grown[1:tracers]], axis=0)


def kernel(
    secs, tiles, u_in, b_in, t_in, wet_in, k_in,
    out_v, ub_out,
    u_v, b_v, t_v, k_v, wet_s, edge_t, edge_ub, to_near, to_far, from_near, from_far, tile_in, tile_back,
    s_v, mix_v, abs_v, coef, pack_v, thin_mix,
    load_sem, wet_sem, send_sem, recv_sem, far_ready, near_ready,
):
    levels = u_in.shape[0]
    tracers = t_in.shape[0]
    padded = mix_v.shape[0]
    total_wet = WET_DEV * secs * tiles
    total_tiles = OCEAN_DEV * secs * tiles
    own = OCEAN_DEV * LANES
    slots = WET_DEV * LANES
    sec = lax.axis_index("sec")
    tile = lax.axis_index("tile")
    device = sec * tiles + tile
    odd = lax.rem(tile, 2)
    even_lane = odd == 0
    partner = (sec, tile + 1 - 2 * odd)
    far_flat = lax.rem(device + 2 * odd - 1 + secs * tiles, secs * tiles)
    far = (far_flat // tiles, lax.rem(far_flat, tiles))

    slot_edge = pl.ds(pl.multiple_of((slots - LANES) * odd, LANES), LANES)
    far_edge = pl.ds(pl.multiple_of((own - LANES) * odd, LANES), LANES)
    near_edge = pl.ds(pl.multiple_of((own - LANES) * (1 - odd), LANES), LANES)
    loads = [
        pltpu.make_async_copy(t_in.at[:, :, slot_edge], edge_t, load_sem.at[0]),
        pltpu.make_async_copy(u_in.at[:, far_edge], edge_ub.at[0], load_sem.at[1]),
        pltpu.make_async_copy(b_in.at[:, far_edge], edge_ub.at[1], load_sem.at[2]),
        pltpu.make_async_copy(t_in, t_v, load_sem.at[3]),
        pltpu.make_async_copy(u_in, u_v.at[:, pl.ds(0, own)], load_sem.at[4]),
        pltpu.make_async_copy(b_in, b_v.at[:, pl.ds(0, own)], load_sem.at[5]),
        pltpu.make_async_copy(k_in, k_v, load_sem.at[6]),
        pltpu.make_async_copy(wet_in, wet_s, wet_sem),
    ]
    for load in loads[:3]:
        load.start()

    barrier = pltpu.get_barrier_semaphore()
    greeted = (jnp.where(even_lane, far[0], partner[0]), jnp.where(even_lane, far[1], partner[1]))
    pl.semaphore_signal(barrier, inc=1, device_id=greeted, device_id_type=MESH)
    for load in loads[3:]:
        load.start()

    def remote(src, dst, index, target):
        return pltpu.make_async_remote_copy(
            src_ref=src, dst_ref=dst, send_sem=send_sem.at[index], recv_sem=recv_sem.at[index],
            device_id=target, device_id_type=MESH,
        )

    pl.semaphore_wait(barrier, 1)

    @pl.when(odd == 1)
    def _():
        pl.semaphore_signal(far_ready, inc=1, device_id=far, device_id_type=MESH)

    @pl.when(odd == 0)
    def _():
        pl.semaphore_signal(near_ready, inc=1, device_id=partner, device_id_type=MESH)

    lane = iota((levels, LANES), 1)
    base = 2 * tracers
    for load in loads[:3]:
        load.wait()
    thin = iota((8, LANES), 1)
    groups = levels // 8
    frame = (thin + (LANES - 8 + 2 * odd)) & (LANES - 1)
    last_frame = (thin + (LANES - 8 + HALO * odd)) & (LANES - 1)
    for part in range(3):
        spots = frame if part < 2 else last_frame
        within = spots & 15
        value = None
        for g in range(groups):
            level = slice(8 * g, 8 * g + 8)
            natural = 16 * g + 8
            if part < 2:
                chunk = None
                for k in range(8):
                    moved = roll(edge_t[8 * part + k, level, :].astype(jnp.float32), natural + 2 * k, 1)
                    chunk = moved if chunk is None else jnp.where(within >= 2 * k, moved, chunk)
            else:
                chunk = roll(edge_ub[0, level, :], natural, 1)
                chunk = jnp.where(within >= HALO, roll(edge_ub[1, level, :], natural + HALO, 1), chunk)
                moved = roll(edge_t[tracers - 1, level, :].astype(jnp.float32), natural + 2 * HALO, 1)
                chunk = jnp.where(within >= 2 * HALO, moved, chunk)
            value = chunk if value is None else jnp.where((spots >> 4) == g, chunk, value)
        to_far[8 * part : 8 * part + 8, :] = value

    send_far = remote(to_far, from_far, 0, far)

    @pl.when(odd == 1)
    def _():
        send_far.start()
        pl.semaphore_wait(near_ready, 1)

    tile_u = remote(u_in.at[:, near_edge], tile_in.at[0], 2, partner)
    tile_b = remote(b_in.at[:, near_edge], tile_in.at[1], 3, partner)
    tile_u.start()
    tile_b.start()

    for load in loads[3:6]:
        load.wait()
    message = jnp.zeros((levels, LANES), jnp.float32)
    for t in range(tracers):
        here = (lane >= 2 * t) & (lane < 2 * t + 2)
        near = jnp.where(even_lane, t_v[t, :, slots - LANES :], t_v[t, :, :LANES]).astype(jnp.float32)
        message = jnp.where(here, pltpu.roll(near, 2 * t + 2 - 2 * odd, 1), message)
    for field, offset in ((u_v, base), (b_v, base + HALO)):
        here = (lane >= offset) & (lane < offset + HALO)
        near = jnp.where(even_lane, field[:, 2 * LANES : 3 * LANES], field[:, LANES : 2 * LANES])
        message = jnp.where(here, pltpu.roll(near, offset + HALO - HALO * odd, 1), message)
    to_near[...] = message
    send_near = remote(to_near, from_near, 1, partner)
    send_near.start()

    loads[6].wait()
    rows = 8 * padded
    wide = 3 * rows
    spread = ((iota((rows, tracers), 0) >> 3) == iota((rows, tracers), 1)).astype(jnp.float32)
    column = iota((tracers, wide), 1)
    column = jnp.where(column >= 2 * rows, column - 2 * rows, jnp.where(column >= rows, column - rows, column))
    gather = ((column >> 3) == iota((tracers, wide), 0)).astype(jnp.float32)
    matrix = exact(exact(spread, k_v[...]), gather)
    same = (iota((rows, wide), 0) & 7) == (iota((rows, wide), 1) & 7)
    matrix = jnp.where(same, matrix, 0.0)
    coarse = matrix.astype(jnp.bfloat16).astype(jnp.float32)
    matrix = jnp.where(iota((rows, wide), 1) < 2 * rows, coarse, matrix - coarse).astype(jnp.bfloat16)
    mix_v[tracers, :, :] = jnp.zeros(mix_v.shape[1:], jnp.float32)
    thin_mix[8 * tracers :, :] = jnp.zeros((8, LANES), jnp.float32)

    for f in range(tracers + 2):
        value = None
        for g in range(groups):
            level = slice(8 * g, 8 * g + 8)
            part = edge_t[f, level, :].astype(jnp.float32) if f < tracers else edge_ub[f - tracers, level, :]
            moved = roll(part, 16 * g + 8, 1)
            value = moved if value is None else jnp.where((thin >> 4) == g, moved, value)
        pack_v[f] = value

    for t in range(tracers):
        s_v[t, :, :slots] = t_v[t].astype(jnp.float32)

    loads[7].wait()
    listed = [
        wet_s[lax.rem(device * WET_DEV + total_wet + j, total_wet)] for j in range(-1, WET_DEV + 1)
    ]
    ring = OCEAN_DEV + 2
    relative = [lax.rem(w - device * OCEAN_DEV + total_tiles + 2, total_tiles) - 2 for w in listed]
    position = [jnp.where(r < 0, r + ring, jnp.where(r < ring, r, ring)) for r in relative]
    is_open = [
        lax.rem(listed[j + 1] - listed[j] + total_tiles, total_tiles) == 1 for j in range(WET_DEV + 1)
    ]
    spot_left, spot, spot_right = position[0], position[1 : WET_DEV + 1], position[WET_DEV + 1]

    tri = (iota((levels, levels), 0) >= iota((levels, levels), 1)).astype(jnp.float32)
    abs_v[:, :slots] = absorbed_light(s_v[0, :, :slots], tri)

    send_near.wait_recv()
    halo_two = jnp.where(even_lane, lane, LANES - 1 - lane) < 2
    halo_three = jnp.where(even_lane, lane, LANES - 1 - lane) < HALO
    for t in range(tracers):
        came = pltpu.roll(from_near[...], 2 * LANES - 2 * t - 2 * odd, 1)
        s_v[t, :, slots:] = jnp.where(halo_two, came, 0.0)
    abs_v[:, slots:] = absorbed_light(s_v[0, :, slots:], tri)
    tile_u.wait_recv()
    tile_b.wait_recv()
    for field, offset, whole in ((u_v, base, tile_in[0]), (b_v, base + HALO, tile_in[1])):
        came = pltpu.roll(from_near[...], 2 * LANES - offset - HALO * odd, 1)
        near = jnp.where(halo_three, came, 0.0)
        field[:, own : own + LANES] = jnp.where(even_lane, whole, near)
        field[:, own + LANES :] = jnp.where(even_lane, near, whole)

    final = None
    for step in range(STEPS):
        width = slots + LANES if step < STEPS - 1 else slots
        light = [abs_v[:, j * LANES : (j + 1) * LANES] for j in range(WET_DEV + 1)]
        heat = []
        for q in range(ring):
            at_halo = jnp.where(lane < LANES // 2, spot_right, spot_left) == q
            term = jnp.where(at_halo, light[WET_DEV], 0.0)
            for j in range(WET_DEV):
                term = jnp.where(spot[j] == q, light[j], term)
            heat.append(term)
        buoyancy = b_v[...] + HEATING * jnp.concatenate(heat, axis=1)
        b_v[...] = buoyancy
        u_v[...] = advance_velocity(u_v[...], buoyancy)
        if step == STEPS - 1:
            place = pl.ds(pl.multiple_of(own + LANES * odd, LANES), LANES)
            final = (
                remote(u_v.at[:, place], tile_back.at[0], 4, partner),
                remote(b_v.at[:, place], tile_back.at[1], 5, partner),
            )
            for copy in final:
                copy.start()
        taken = []
        for field in (u_v, b_v):
            part = [field[:, q * LANES : (q + 1) * LANES] for q in range(ring)]
            chosen = [
                pick(spot[0], [(0, part[0]), (1, part[1]), (2, part[2]), (5, part[5])]),
                pick(spot[1], [(0, part[0]), (1, part[1]), (2, part[2]), (3, part[3])]),
                pick(spot[2], [(1, part[1]), (2, part[2]), (3, part[3]), (4, part[4])]),
            ]
            ahead = pick(spot_right, [(3, part[3]), (4, part[4]), (5, part[5])])
            behind = pick(spot_left, [(0, part[0]), (4, part[4]), (5, part[5])])
            chosen.append(jnp.where(lane < LANES // 2, ahead, behind))
            taken.append(jnp.concatenate(chosen, axis=1))
        gates = []
        for j in range(WET_DEV + 1):
            ends = is_open[(j + 1) % (WET_DEV + 1)].astype(jnp.float32)
            gates.append(jnp.where(lane == LANES - 1, ends, 1.0))
        set_coefficients(coef, taken[0], taken[1], jnp.concatenate(gates, axis=1))
        for t in range(tracers):
            mix_v[t, :, :width] = transport(s_v[t], coef, width)
        for group in range(levels // 16):
            halves = []
            for half in range(2):
                level = slice(group * 16 + half * 8, group * 16 + half * 8 + 8)
                grown = react(
                    mix_v[:, level, :width], coef[6, level, :width], abs_v[level, :width], matrix, tracers
                )
                if step < STEPS - 1:
                    s_v[:, level, :width] = grown
                halves.append(grown)
            if step == STEPS - 1:
                level = slice(group * 16, group * 16 + 16)
                out_v[:, level, :] = jnp.concatenate(halves, axis=1).astype(jnp.bfloat16)
        if step < STEPS - 1:
            abs_v[:, :width] = absorbed_light(s_v[0, :, :width], tri)

    @pl.when(odd == 0)
    def _():
        pl.semaphore_wait(far_ready, 1)
        send_far.start()

    for copy in final:
        copy.wait_recv()
    for field, index in ((u_v, 0), (b_v, 1)):
        back = tile_back[index]
        low_given = jnp.logical_and(odd == 1, spot_left == 0)
        high_given = jnp.logical_and(odd == 0, spot_right == OCEAN_DEV - 1)
        ub_out[index, :, :LANES] = jnp.where(low_given, back, field[:, :LANES])
        ub_out[index, :, LANES : own - LANES] = field[:, LANES : own - LANES]
        ub_out[index, :, own - LANES :] = jnp.where(high_given, back, field[:, own - LANES : own])

    edge_wet = jnp.where(even_lane, relative[1] == 0, relative[WET_DEV] == OCEAN_DEV - 1)
    halo_wet = jnp.where(even_lane, relative[0] == -1, relative[WET_DEV + 1] == OCEAN_DEV)
    column = thin & 15
    distance = jnp.where(even_lane, column - 8, 7 - column)
    edge_wet, halo_wet = edge_wet.astype(jnp.float32), halo_wet.astype(jnp.float32)
    shape = (8, LANES)
    lane = thin
    row = iota(shape, 0)
    level = 8 * (lane >> 4) + row
    inside = jnp.where(even_lane, 7 - column, column - 8)
    halo_two = (inside >= 0) & (inside < 2)
    halo_three = (inside >= 0) & (inside < HALO)

    def above(x):
        turned = roll(x, 1, 0)
        return jnp.where(row == 0, roll(turned, 16, 1), turned)

    def below(x):
        turned = roll(x, -1, 0)
        return jnp.where(row == 7, roll(turned, -16, 1), turned)

    def total_from_top(x):
        for shift in (1, 2, 4):
            x = x + jnp.where(row >= shift, roll(x, shift, 0), 0.0)
        whole = jnp.broadcast_to(x[7:8], shape)
        parts = [jnp.where(lane >= 16 * k, roll(whole, 16 * k, 1), 0.0) for k in range(1, levels // 8)]
        while len(parts) > 1:
            parts = [sum(parts[k : k + 2]) for k in range(0, len(parts), 2)]
        return x + parts[0]

    lit = jnp.where(distance >= 0, edge_wet, halo_wet)
    gate = DT_TRACER * jnp.where(column == 7, edge_wet * halo_wet, 1.0)
    near_side = jnp.where(even_lane, lane, LANES - 1 - lane) < 4
    near_wet = jnp.concatenate([jnp.where(near_side, edge_wet, 0.0)] * 2, axis=0) > 0.5

    send_far.wait_recv()
    state = []
    for t in range(tracers):
        part = from_far[8 * (t // 8) : 8 * (t // 8) + 8, :]
        came = roll(part, -2 * (t % 8) if t < 16 else -2 * HALO, 1)
        state.append(jnp.where(halo_two, came, pack_v[t]))
    fields = []
    for f in range(2):
        came = roll(from_far[16:24, :], -HALO * f, 1)
        fields.append(jnp.where(halo_three, came, pack_v[tracers + f]))
    velocity, buoyancy = fields
    for step in range(STEPS):
        attenuation = WATER_ATT + PIGMENT_ATT * state[0] * state[0]
        depth = total_from_top(attenuation)
        light = SURFACE_LIGHT * (jnp.exp(attenuation - depth) - jnp.exp(-depth))
        buoyancy = buoyancy + HEATING * lit * light
        horiz = roll(velocity, 1, 1) + roll(velocity, -1, 1) - 2.0 * velocity
        upper = jnp.where(level == 0, velocity, above(velocity))
        lower = jnp.where(level == levels - 1, velocity, below(velocity))
        press = roll(buoyancy, -1, 1) - buoyancy
        velocity = velocity + DT_OCEAN * (
            HORIZ_VISC * horiz + VERT_VISC * (upper + lower - 2.0 * velocity) - PRESSURE * press
        )
        shear, settled = velocity - below(velocity), buoyancy - below(buoyancy)
        spreading = jnp.where(level == levels - 1, 0.0, diffusivity(shear, settled))
        shear, settled = above(velocity) - velocity, above(buoyancy) - buoyancy
        spreading_up = jnp.where(level == 0, 0.0, diffusivity(shear, settled))
        forward = jnp.maximum(velocity, 0.0) * gate
        backward = jnp.minimum(velocity, 0.0) * gate
        stay = 1.0 - forward + roll(backward, 1, 1)
        from_left = roll(forward, 1, 1)
        keep = 1.0 - DT_MIX * (spreading + spreading_up)
        warm = KINETIC_DELTA * jnp.exp(THERMAL_GAIN * buoyancy)
        mixed = []
        for t in range(tracers):
            moved = stay * state[t] - backward * roll(state[t], -1, 1) + from_left * roll(state[t], 1, 1)
            mixed.append(
                keep * moved + DT_MIX * (spreading * below(moved) + spreading_up * above(moved))
            )
            thin_mix[8 * t : 8 * t + 8, :] = mixed[t]
        flat = thin_mix[...]
        high = flat.astype(jnp.bfloat16)
        low = (flat - high.astype(jnp.float32)).astype(jnp.bfloat16)
        drift = jnp.dot(
            matrix, jnp.concatenate([high, low, high], axis=0), preferred_element_type=jnp.float32
        )
        state = [mixed[t] + warm * drift[8 * t : 8 * t + 8] for t in range(tracers)]
        state[0] = state[0] + GROWTH * light

    for f, field in enumerate((velocity, buoyancy)):
        for g in range(groups):
            rows = slice(8 * g, 8 * g + 8)
            kept = ub_out[f, rows, far_edge]
            ub_out[f, rows, far_edge] = jnp.where(near_side, roll(field, -16 * g - 8, 1), kept)
    for t in range(tracers):
        for g in range(levels // 16):
            rows = slice(16 * g, 16 * g + 16)
            fresh = jnp.concatenate(
                [roll(state[t], -32 * g - 8, 1), roll(state[t], -32 * g - 24, 1)], axis=0
            )
            kept = out_v[t, rows, slot_edge].astype(jnp.float32)
            out_v[t, rows, slot_edge] = jnp.where(near_wet, fresh, kept).astype(jnp.bfloat16)
    for copy in (send_near, tile_u, tile_b, *final, send_far):
        copy.wait_send()


def finish(t_v, ub_v, t_out, u_out, b_out, sems):
    copies = [
        pltpu.make_async_copy(t_v, t_out, sems.at[0]),
        pltpu.make_async_copy(ub_v.at[0], u_out, sems.at[1]),
        pltpu.make_async_copy(ub_v.at[1], b_out, sems.at[2]),
    ]
    for copy in copies:
        copy.start()
    for copy in copies:
        copy.wait()


def on_device(ocean_u, ocean_b, tracers, wet_tiles, kinetic_matrix):
    levels, own = ocean_u.shape
    count, _, slots = tracers.shape
    padded = count + count % 2
    wide = slots + LANES
    domain = own + 2 * LANES
    f32, bf16 = jnp.float32, jnp.bfloat16
    hbm = pl.BlockSpec(memory_space=pltpu.HBM)
    vmem = pl.BlockSpec(memory_space=pltpu.VMEM)
    operands = [
        pltpu.with_memory_space_constraint(x, pltpu.HBM)
        for x in (ocean_u, ocean_b, tracers, wet_tiles, kinetic_matrix)
    ]
    rows = 8 * padded
    parts = pl.pallas_call(
        functools.partial(kernel, lax.axis_size("sec"), lax.axis_size("tile")),
        out_shape=(
            jax.ShapeDtypeStruct(tracers.shape, bf16),
            jax.ShapeDtypeStruct((2, levels, own), f32),
        ),
        in_specs=[hbm] * 5,
        out_specs=(vmem,) * 2,
        scratch_shapes=[
            pltpu.VMEM((levels, domain), f32),
            pltpu.VMEM((levels, domain), f32),
            pltpu.VMEM(tracers.shape, bf16),
            pltpu.VMEM(kinetic_matrix.shape, f32),
            pltpu.SMEM(wet_tiles.shape, jnp.int32),
            pltpu.VMEM((count, levels, LANES), bf16),
            pltpu.VMEM((2, levels, LANES), f32),
            pltpu.VMEM((levels, LANES), f32),
            pltpu.VMEM((24, LANES), f32),
            pltpu.VMEM((levels, LANES), f32),
            pltpu.VMEM((24, LANES), f32),
            pltpu.VMEM((2, levels, LANES), f32),
            pltpu.VMEM((2, levels, LANES), f32),
            pltpu.VMEM((count, levels, wide), f32),
            pltpu.VMEM((padded, levels, wide), f32),
            pltpu.VMEM((levels, wide), f32),
            pltpu.VMEM((7, levels, wide), f32),
            pltpu.VMEM((count + 2, 8, LANES), f32),
            pltpu.VMEM((rows, LANES), f32),
            pltpu.SemaphoreType.DMA((7,)),
            pltpu.SemaphoreType.DMA,
            pltpu.SemaphoreType.DMA((6,)),
            pltpu.SemaphoreType.DMA((6,)),
            pltpu.SemaphoreType.REGULAR,
            pltpu.SemaphoreType.REGULAR,
        ],
        compiler_params=pltpu.CompilerParams(
            collective_id=0, has_side_effects=True, vmem_limit_bytes=40 * 2**20
        ),
    )(*operands)
    return pl.pallas_call(
        finish,
        out_shape=(
            jax.ShapeDtypeStruct(tracers.shape, bf16),
            jax.ShapeDtypeStruct(ocean_u.shape, f32),
            jax.ShapeDtypeStruct(ocean_b.shape, f32),
        ),
        in_specs=[vmem] * 2,
        out_specs=(hbm, hbm, hbm),
        scratch_shapes=[pltpu.SemaphoreType.DMA((3,))],
        compiler_params=pltpu.CompilerParams(vmem_limit_bytes=2**20),
    )(*parts)


def solution(mesh):
    flat = ("sec", "tile")
    placed = (P(None, flat), P(None, flat), P(None, None, flat), P(), P())
    return jax.shard_map(
        on_device,
        mesh=mesh,
        in_specs=placed,
        out_specs=(P(None, None, flat), P(None, flat), P(None, flat)),
        check_vma=False,
    )
```

```python
import functools

import jax
import jax.numpy as jnp
from jax import lax
from jax.experimental import pallas as pl
from jax.experimental.pallas import tpu as pltpu
from jax.sharding import PartitionSpec as P

MESH = pl.DeviceIdType.MESH
LANES = 128
STEPS = 2
WET_DEV = 3
OCEAN_DEV = 4
HALO = 3

DT_OCEAN = 0.25
PRESSURE = 1.0
HORIZ_VISC = 0.2
VERT_VISC = 0.2
HEATING = 0.2
KAPPA_BASE = 0.05
KAPPA_SPAN = 0.35
DT_TRACER = 0.3
DT_MIX = 1.0
KINETIC_DELTA = 0.5
SURFACE_LIGHT = 10.0
WATER_ATT = 0.04
PIGMENT_ATT = 0.08
GROWTH = 0.05
THERMAL_GAIN = 0.1


def roll(x, shift, axis):
    size = x.shape[axis]
    shift = shift % size
    return x if shift == 0 else pltpu.roll(x, shift, axis)


def iota(shape, axis):
    return lax.broadcasted_iota(jnp.int32, shape, axis)


def pick(position, options):
    value = None
    for where, option in options:
        value = option if value is None else jnp.where(position == where, option, value)
    return value


def exact(a, b):
    return jnp.dot(a, b, precision=lax.Precision.HIGHEST, preferred_element_type=jnp.float32)


def absorbed_light(pigment, tri):
    attenuation = WATER_ATT + PIGMENT_ATT * pigment * pigment
    below = jnp.exp(-exact(tri, attenuation))
    above = jnp.where(iota(pigment.shape, 0) == 0, 1.0, roll(below, 1, 0))
    return SURFACE_LIGHT * (above - below)


def advance_velocity(velocity, buoyancy):
    level = iota(velocity.shape, 0)
    horiz = roll(velocity, 1, 1) + roll(velocity, -1, 1) - 2.0 * velocity
    press = roll(buoyancy, -1, 1) - buoyancy
    upper = jnp.where(level == 0, velocity, roll(velocity, 1, 0))
    lower = jnp.where(level == velocity.shape[0] - 1, velocity, roll(velocity, -1, 0))
    vert = upper + lower - 2.0 * velocity
    return velocity + DT_OCEAN * (HORIZ_VISC * horiz + VERT_VISC * vert - PRESSURE * press)


def diffusivity(shear, settled):
    steep = 4.0 * (shear * shear - settled)
    return KAPPA_BASE + KAPPA_SPAN / (1.0 + jnp.exp(-steep))


def set_coefficients(coef, face_u, warmth, gate):
    level = iota(face_u.shape, 0)
    shear = face_u - roll(face_u, -1, 0)
    stratified = warmth - roll(warmth, -1, 0)
    spreading = diffusivity(shear, stratified)
    spreading = jnp.where(level == face_u.shape[0] - 1, 0.0, spreading)
    spreading_up = jnp.where(level == 0, 0.0, roll(spreading, 1, 0))
    gate = DT_TRACER * gate
    forward = jnp.maximum(face_u, 0.0) * gate
    backward = jnp.minimum(face_u, 0.0) * gate
    coef[0] = 1.0 - forward + roll(backward, 1, 1)
    coef[1] = -backward
    coef[2] = roll(forward, 1, 1)
    coef[3] = 1.0 - DT_MIX * (spreading + spreading_up)
    coef[4] = DT_MIX * spreading
    coef[5] = DT_MIX * spreading_up
    coef[6] = KINETIC_DELTA * jnp.exp(THERMAL_GAIN * warmth)


def transport(state, coef, width):
    moved = (coef[0] * state + coef[1] * roll(state, -1, 1) + coef[2] * roll(state, 1, 1))[:, :width]
    return (
        coef[3][:, :width] * moved
        + coef[4][:, :width] * roll(moved, -1, 0)
        + coef[5][:, :width] * roll(moved, 1, 0)
    )


def react(mixed, warm, light, matrix, tracers):
    padded, rows, width = mixed.shape
    flat = mixed.reshape(padded * rows, width)
    high = flat.astype(jnp.bfloat16)
    low = (flat - high.astype(jnp.float32)).astype(jnp.bfloat16)
    drift = jnp.dot(
        matrix, jnp.concatenate([high, low, high], axis=0), preferred_element_type=jnp.float32
    ).reshape(padded, rows, width)
    grown = mixed + warm[None] * drift
    return jnp.concatenate([(grown[0] + GROWTH * light)[None], grown[1:tracers]], axis=0)


def kernel(
    secs, tiles, u_in, b_in, t_in, wet_in, k_in,
    out_v, ub_out,
    u_v, b_v, t_v, k_v, wet_s, edge_t, edge_ub, to_near, to_far, from_near, from_far, tile_in, tile_back,
    s_v, mix_v, abs_v, coef, pack_v, splat_v,
    load_sem, wet_sem, send_sem, recv_sem, far_ready, near_ready,
):
    levels = u_in.shape[0]
    tracers = t_in.shape[0]
    padded = mix_v.shape[0]
    total_wet = WET_DEV * secs * tiles
    total_tiles = OCEAN_DEV * secs * tiles
    own = OCEAN_DEV * LANES
    slots = WET_DEV * LANES
    sec = lax.axis_index("sec")
    tile = lax.axis_index("tile")
    device = sec * tiles + tile
    odd = lax.rem(tile, 2)
    even_lane = odd == 0
    partner = (sec, tile + 1 - 2 * odd)
    far_flat = lax.rem(device + 2 * odd - 1 + secs * tiles, secs * tiles)
    far = (far_flat // tiles, lax.rem(far_flat, tiles))

    slot_edge = pl.ds(pl.multiple_of((slots - LANES) * odd, LANES), LANES)
    far_edge = pl.ds(pl.multiple_of((own - LANES) * odd, LANES), LANES)
    near_edge = pl.ds(pl.multiple_of((own - LANES) * (1 - odd), LANES), LANES)
    loads = [
        pltpu.make_async_copy(u_in.at[:, far_edge], edge_ub.at[0], load_sem.at[0]),
        pltpu.make_async_copy(b_in.at[:, far_edge], edge_ub.at[1], load_sem.at[1]),
        pltpu.make_async_copy(t_in.at[16:, :, slot_edge], edge_t.at[16:], load_sem.at[2]),
        pltpu.make_async_copy(t_in.at[:8, :, slot_edge], edge_t.at[:8], load_sem.at[7]),
        pltpu.make_async_copy(t_in.at[8:16, :, slot_edge], edge_t.at[8:16], load_sem.at[8]),
        pltpu.make_async_copy(t_in, t_v, load_sem.at[3]),
        pltpu.make_async_copy(u_in, u_v.at[:, pl.ds(0, own)], load_sem.at[4]),
        pltpu.make_async_copy(b_in, b_v.at[:, pl.ds(0, own)], load_sem.at[5]),
        pltpu.make_async_copy(k_in, k_v, load_sem.at[6]),
        pltpu.make_async_copy(wet_in, wet_s, wet_sem),
    ]
    for load in loads[:5]:
        load.start()

    barrier = pltpu.get_barrier_semaphore()
    greeted = (jnp.where(even_lane, far[0], partner[0]), jnp.where(even_lane, far[1], partner[1]))
    pl.semaphore_signal(barrier, inc=1, device_id=greeted, device_id_type=MESH)
    for load in loads[5:]:
        load.start()

    def remote(src, dst, index, target):
        return pltpu.make_async_remote_copy(
            src_ref=src, dst_ref=dst, send_sem=send_sem.at[index], recv_sem=recv_sem.at[index],
            device_id=target, device_id_type=MESH,
        )

    pl.semaphore_wait(barrier, 1)

    @pl.when(odd == 1)
    def _():
        pl.semaphore_signal(far_ready, inc=1, device_id=far, device_id_type=MESH)

    @pl.when(odd == 0)
    def _():
        pl.semaphore_signal(near_ready, inc=1, device_id=partner, device_id_type=MESH)

    lane = iota((levels, LANES), 1)
    base = 2 * tracers
    thin = iota((8, LANES), 1)
    groups = levels // 8
    frame = (thin + (LANES - 8 + 2 * odd)) & (LANES - 1)
    last_frame = (thin + (LANES - 8 + HALO * odd)) & (LANES - 1)
    for part in (2, 0, 1):
        for load in loads[3 + part : 4 + part] if part < 2 else loads[:3]:
            load.wait()
        spots = frame if part < 2 else last_frame
        within = spots & 15
        value = None
        for g in range(groups):
            level = slice(8 * g, 8 * g + 8)
            natural = 16 * g + 8
            if part < 2:
                chunk = None
                for k in range(8):
                    moved = roll(edge_t[8 * part + k, level, :].astype(jnp.float32), natural + 2 * k, 1)
                    chunk = moved if chunk is None else jnp.where(within >= 2 * k, moved, chunk)
            else:
                chunk = roll(edge_ub[0, level, :], natural, 1)
                chunk = jnp.where(within >= HALO, roll(edge_ub[1, level, :], natural + HALO, 1), chunk)
                moved = roll(edge_t[tracers - 1, level, :].astype(jnp.float32), natural + 2 * HALO, 1)
                chunk = jnp.where(within >= 2 * HALO, moved, chunk)
            value = chunk if value is None else jnp.where((spots >> 4) == g, chunk, value)
        to_far[8 * part : 8 * part + 8, :] = value

    send_far = remote(to_far, from_far, 0, far)

    @pl.when(odd == 1)
    def _():
        send_far.start()
        pl.semaphore_wait(near_ready, 1)

    tile_u = remote(u_in.at[:, near_edge], tile_in.at[0], 2, partner)
    tile_b = remote(b_in.at[:, near_edge], tile_in.at[1], 3, partner)
    tile_u.start()
    tile_b.start()

    for load in loads[5:8]:
        load.wait()
    message = jnp.zeros((levels, LANES), jnp.float32)
    for t in range(tracers):
        here = (lane >= 2 * t) & (lane < 2 * t + 2)
        near = jnp.where(even_lane, t_v[t, :, slots - LANES :], t_v[t, :, :LANES]).astype(jnp.float32)
        message = jnp.where(here, pltpu.roll(near, 2 * t + 2 - 2 * odd, 1), message)
    for field, offset in ((u_v, base), (b_v, base + HALO)):
        here = (lane >= offset) & (lane < offset + HALO)
        near = jnp.where(even_lane, field[:, 2 * LANES : 3 * LANES], field[:, LANES : 2 * LANES])
        message = jnp.where(here, pltpu.roll(near, offset + HALO - HALO * odd, 1), message)
    to_near[...] = message
    send_near = remote(to_near, from_near, 1, partner)
    send_near.start()

    loads[8].wait()
    rows = 8 * padded
    wide = 3 * rows
    spread = ((iota((rows, tracers), 0) >> 3) == iota((rows, tracers), 1)).astype(jnp.float32)
    column = iota((tracers, wide), 1)
    column = jnp.where(column >= 2 * rows, column - 2 * rows, jnp.where(column >= rows, column - rows, column))
    gather = ((column >> 3) == iota((tracers, wide), 0)).astype(jnp.float32)
    matrix = exact(exact(spread, k_v[...]), gather)
    same = (iota((rows, wide), 0) & 7) == (iota((rows, wide), 1) & 7)
    matrix = jnp.where(same, matrix, 0.0)
    coarse = matrix.astype(jnp.bfloat16).astype(jnp.float32)
    matrix = jnp.where(iota((rows, wide), 1) < 2 * rows, coarse, matrix - coarse).astype(jnp.bfloat16)
    mix_v[tracers, :, :] = jnp.zeros(mix_v.shape[1:], jnp.float32)
    for i in range(tracers):
        for k in range(tracers):
            splat_v[tracers * i + k] = jnp.broadcast_to(k_v[i : i + 1, k : k + 1], (8, LANES))

    for f in range(tracers + 2):
        value = None
        for g in range(groups):
            level = slice(8 * g, 8 * g + 8)
            part = edge_t[f, level, :].astype(jnp.float32) if f < tracers else edge_ub[f - tracers, level, :]
            moved = roll(part, 16 * g + 8, 1)
            value = moved if value is None else jnp.where((thin >> 4) == g, moved, value)
        pack_v[f] = value

    for t in range(tracers):
        s_v[t, :, :slots] = t_v[t].astype(jnp.float32)

    loads[9].wait()
    listed = [
        wet_s[lax.rem(device * WET_DEV + total_wet + j, total_wet)] for j in range(-1, WET_DEV + 1)
    ]
    ring = OCEAN_DEV + 2
    relative = [lax.rem(w - device * OCEAN_DEV + total_tiles + 2, total_tiles) - 2 for w in listed]
    position = [jnp.where(r < 0, r + ring, jnp.where(r < ring, r, ring)) for r in relative]
    is_open = [
        lax.rem(listed[j + 1] - listed[j] + total_tiles, total_tiles) == 1 for j in range(WET_DEV + 1)
    ]
    spot_left, spot, spot_right = position[0], position[1 : WET_DEV + 1], position[WET_DEV + 1]

    tri = (iota((levels, levels), 0) >= iota((levels, levels), 1)).astype(jnp.float32)
    abs_v[:, :slots] = absorbed_light(s_v[0, :, :slots], tri)

    send_near.wait_recv()
    halo_two = jnp.where(even_lane, lane, LANES - 1 - lane) < 2
    halo_three = jnp.where(even_lane, lane, LANES - 1 - lane) < HALO
    for t in range(tracers):
        came = pltpu.roll(from_near[...], 2 * LANES - 2 * t - 2 * odd, 1)
        s_v[t, :, slots:] = jnp.where(halo_two, came, 0.0)
    abs_v[:, slots:] = absorbed_light(s_v[0, :, slots:], tri)
    tile_u.wait_recv()
    tile_b.wait_recv()
    for field, offset, whole in ((u_v, base, tile_in[0]), (b_v, base + HALO, tile_in[1])):
        came = pltpu.roll(from_near[...], 2 * LANES - offset - HALO * odd, 1)
        near = jnp.where(halo_three, came, 0.0)
        field[:, own : own + LANES] = jnp.where(even_lane, whole, near)
        field[:, own + LANES :] = jnp.where(even_lane, near, whole)

    final = None
    for step in range(STEPS):
        width = slots + LANES if step < STEPS - 1 else slots
        light = [abs_v[:, j * LANES : (j + 1) * LANES] for j in range(WET_DEV + 1)]
        heat = []
        for q in range(ring):
            at_halo = jnp.where(lane < LANES // 2, spot_right, spot_left) == q
            term = jnp.where(at_halo, light[WET_DEV], 0.0)
            for j in range(WET_DEV):
                term = jnp.where(spot[j] == q, light[j], term)
            heat.append(term)
        buoyancy = b_v[...] + HEATING * jnp.concatenate(heat, axis=1)
        b_v[...] = buoyancy
        u_v[...] = advance_velocity(u_v[...], buoyancy)
        if step == STEPS - 1:
            place = pl.ds(pl.multiple_of(own + LANES * odd, LANES), LANES)
            final = (
                remote(u_v.at[:, place], tile_back.at[0], 4, partner),
                remote(b_v.at[:, place], tile_back.at[1], 5, partner),
            )
            for copy in final:
                copy.start()
        taken = []
        for field in (u_v, b_v):
            part = [field[:, q * LANES : (q + 1) * LANES] for q in range(ring)]
            chosen = [
                pick(spot[0], [(0, part[0]), (1, part[1]), (2, part[2]), (5, part[5])]),
                pick(spot[1], [(0, part[0]), (1, part[1]), (2, part[2]), (3, part[3])]),
                pick(spot[2], [(1, part[1]), (2, part[2]), (3, part[3]), (4, part[4])]),
            ]
            ahead = pick(spot_right, [(3, part[3]), (4, part[4]), (5, part[5])])
            behind = pick(spot_left, [(0, part[0]), (4, part[4]), (5, part[5])])
            chosen.append(jnp.where(lane < LANES // 2, ahead, behind))
            taken.append(jnp.concatenate(chosen, axis=1))
        gates = []
        for j in range(WET_DEV + 1):
            ends = is_open[(j + 1) % (WET_DEV + 1)].astype(jnp.float32)
            gates.append(jnp.where(lane == LANES - 1, ends, 1.0))
        set_coefficients(coef, taken[0], taken[1], jnp.concatenate(gates, axis=1))
        for t in range(tracers):
            mix_v[t, :, :width] = transport(s_v[t], coef, width)
        for group in range(levels // 16):
            halves = []
            for half in range(2):
                level = slice(group * 16 + half * 8, group * 16 + half * 8 + 8)
                grown = react(
                    mix_v[:, level, :width], coef[6, level, :width], abs_v[level, :width], matrix, tracers
                )
                if step < STEPS - 1:
                    s_v[:, level, :width] = grown
                halves.append(grown)
            if step == STEPS - 1:
                level = slice(group * 16, group * 16 + 16)
                out_v[:, level, :] = jnp.concatenate(halves, axis=1).astype(jnp.bfloat16)
        if step < STEPS - 1:
            abs_v[:, :width] = absorbed_light(s_v[0, :, :width], tri)

    @pl.when(odd == 0)
    def _():
        pl.semaphore_wait(far_ready, 1)
        send_far.start()

    for copy in final:
        copy.wait_recv()
    for field, index in ((u_v, 0), (b_v, 1)):
        back = tile_back[index]
        low_given = jnp.logical_and(odd == 1, spot_left == 0)
        high_given = jnp.logical_and(odd == 0, spot_right == OCEAN_DEV - 1)
        ub_out[index, :, :LANES] = jnp.where(low_given, back, field[:, :LANES])
        ub_out[index, :, LANES : own - LANES] = field[:, LANES : own - LANES]
        ub_out[index, :, own - LANES :] = jnp.where(high_given, back, field[:, own - LANES : own])

    edge_wet = jnp.where(even_lane, relative[1] == 0, relative[WET_DEV] == OCEAN_DEV - 1)
    halo_wet = jnp.where(even_lane, relative[0] == -1, relative[WET_DEV + 1] == OCEAN_DEV)
    column = thin & 15
    distance = jnp.where(even_lane, column - 8, 7 - column)
    edge_wet, halo_wet = edge_wet.astype(jnp.float32), halo_wet.astype(jnp.float32)
    shape = (8, LANES)
    lane = thin
    row = iota(shape, 0)
    level = 8 * (lane >> 4) + row
    inside = jnp.where(even_lane, 7 - column, column - 8)
    halo_two = (inside >= 0) & (inside < 2)
    halo_three = (inside >= 0) & (inside < HALO)

    def above(x):
        turned = roll(x, 1, 0)
        return jnp.where(row == 0, roll(turned, 16, 1), turned)

    def below(x):
        turned = roll(x, -1, 0)
        return jnp.where(row == 7, roll(turned, -16, 1), turned)

    def total_from_top(x):
        for shift in (1, 2, 4):
            x = x + jnp.where(row >= shift, roll(x, shift, 0), 0.0)
        whole = jnp.broadcast_to(x[7:8], shape)
        parts = [jnp.where(lane >= 16 * k, roll(whole, 16 * k, 1), 0.0) for k in range(1, levels // 8)]
        while len(parts) > 1:
            parts = [sum(parts[k : k + 2]) for k in range(0, len(parts), 2)]
        return x + parts[0]

    lit = jnp.where(distance >= 0, edge_wet, halo_wet)
    gate = DT_TRACER * jnp.where(column == 7, edge_wet * halo_wet, 1.0)
    near_side = jnp.where(even_lane, lane, LANES - 1 - lane) < 4
    near_wet = jnp.concatenate([jnp.where(near_side, edge_wet, 0.0)] * 2, axis=0) > 0.5

    send_far.wait_recv()
    state = []
    for t in range(tracers):
        part = from_far[8 * (t // 8) : 8 * (t // 8) + 8, :]
        came = roll(part, -2 * (t % 8) if t < 16 else -2 * HALO, 1)
        state.append(jnp.where(halo_two, came, pack_v[t]))
    fields = []
    for f in range(2):
        came = roll(from_far[16:24, :], -HALO * f, 1)
        fields.append(jnp.where(halo_three, came, pack_v[tracers + f]))
    velocity, buoyancy = fields
    for step in range(STEPS):
        attenuation = WATER_ATT + PIGMENT_ATT * state[0] * state[0]
        depth = total_from_top(attenuation)
        light = SURFACE_LIGHT * (jnp.exp(attenuation - depth) - jnp.exp(-depth))
        buoyancy = buoyancy + HEATING * lit * light
        horiz = roll(velocity, 1, 1) + roll(velocity, -1, 1) - 2.0 * velocity
        upper = jnp.where(level == 0, velocity, above(velocity))
        lower = jnp.where(level == levels - 1, velocity, below(velocity))
        press = roll(buoyancy, -1, 1) - buoyancy
        velocity = velocity + DT_OCEAN * (
            HORIZ_VISC * horiz + VERT_VISC * (upper + lower - 2.0 * velocity) - PRESSURE * press
        )
        shear, settled = velocity - below(velocity), buoyancy - below(buoyancy)
        spreading = jnp.where(level == levels - 1, 0.0, diffusivity(shear, settled))
        shear, settled = above(velocity) - velocity, above(buoyancy) - buoyancy
        spreading_up = jnp.where(level == 0, 0.0, diffusivity(shear, settled))
        forward = jnp.maximum(velocity, 0.0) * gate
        backward = jnp.minimum(velocity, 0.0) * gate
        stay = 1.0 - forward + roll(backward, 1, 1)
        from_left = roll(forward, 1, 1)
        keep = 1.0 - DT_MIX * (spreading + spreading_up)
        warm = KINETIC_DELTA * jnp.exp(THERMAL_GAIN * buoyancy)
        mixed = []
        for t in range(tracers):
            moved = stay * state[t] - backward * roll(state[t], -1, 1) + from_left * roll(state[t], 1, 1)
            mixed.append(
                keep * moved + DT_MIX * (spreading * below(moved) + spreading_up * above(moved))
            )
        state = []
        for t in range(tracers):
            sums = [splat_v[tracers * t + k] * mixed[k] for k in range(2)]
            for k in range(2, tracers):
                sums[k % 2] = sums[k % 2] + splat_v[tracers * t + k] * mixed[k]
            state.append(mixed[t] + warm * (sums[0] + sums[1]))
        state[0] = state[0] + GROWTH * light

    for f, field in enumerate((velocity, buoyancy)):
        for g in range(groups):
            rows = slice(8 * g, 8 * g + 8)
            kept = ub_out[f, rows, far_edge]
            ub_out[f, rows, far_edge] = jnp.where(near_side, roll(field, -16 * g - 8, 1), kept)
    for t in range(tracers):
        for g in range(levels // 16):
            rows = slice(16 * g, 16 * g + 16)
            fresh = jnp.concatenate(
                [roll(state[t], -32 * g - 8, 1), roll(state[t], -32 * g - 24, 1)], axis=0
            )
            kept = out_v[t, rows, slot_edge].astype(jnp.float32)
            out_v[t, rows, slot_edge] = jnp.where(near_wet, fresh, kept).astype(jnp.bfloat16)
    for copy in (send_near, tile_u, tile_b, *final, send_far):
        copy.wait_send()


def finish(t_v, ub_v, t_out, u_out, b_out, sems):
    copies = [
        pltpu.make_async_copy(t_v, t_out, sems.at[0]),
        pltpu.make_async_copy(ub_v.at[0], u_out, sems.at[1]),
        pltpu.make_async_copy(ub_v.at[1], b_out, sems.at[2]),
    ]
    for copy in copies:
        copy.start()
    for copy in copies:
        copy.wait()


def on_device(ocean_u, ocean_b, tracers, wet_tiles, kinetic_matrix):
    levels, own = ocean_u.shape
    count, _, slots = tracers.shape
    padded = count + count % 2
    wide = slots + LANES
    domain = own + 2 * LANES
    f32, bf16 = jnp.float32, jnp.bfloat16
    hbm = pl.BlockSpec(memory_space=pltpu.HBM)
    vmem = pl.BlockSpec(memory_space=pltpu.VMEM)
    operands = [
        pltpu.with_memory_space_constraint(x, pltpu.HBM)
        for x in (ocean_u, ocean_b, tracers, wet_tiles, kinetic_matrix)
    ]
    parts = pl.pallas_call(
        functools.partial(kernel, lax.axis_size("sec"), lax.axis_size("tile")),
        out_shape=(
            jax.ShapeDtypeStruct(tracers.shape, bf16),
            jax.ShapeDtypeStruct((2, levels, own), f32),
        ),
        in_specs=[hbm] * 5,
        out_specs=(vmem,) * 2,
        scratch_shapes=[
            pltpu.VMEM((levels, domain), f32),
            pltpu.VMEM((levels, domain), f32),
            pltpu.VMEM(tracers.shape, bf16),
            pltpu.VMEM(kinetic_matrix.shape, f32),
            pltpu.SMEM(wet_tiles.shape, jnp.int32),
            pltpu.VMEM((count, levels, LANES), bf16),
            pltpu.VMEM((2, levels, LANES), f32),
            pltpu.VMEM((levels, LANES), f32),
            pltpu.VMEM((24, LANES), f32),
            pltpu.VMEM((levels, LANES), f32),
            pltpu.VMEM((24, LANES), f32),
            pltpu.VMEM((2, levels, LANES), f32),
            pltpu.VMEM((2, levels, LANES), f32),
            pltpu.VMEM((count, levels, wide), f32),
            pltpu.VMEM((padded, levels, wide), f32),
            pltpu.VMEM((levels, wide), f32),
            pltpu.VMEM((7, levels, wide), f32),
            pltpu.VMEM((count + 2, 8, LANES), f32),
            pltpu.VMEM((count * count, 8, LANES), f32),
            pltpu.SemaphoreType.DMA((9,)),
            pltpu.SemaphoreType.DMA,
            pltpu.SemaphoreType.DMA((6,)),
            pltpu.SemaphoreType.DMA((6,)),
            pltpu.SemaphoreType.REGULAR,
            pltpu.SemaphoreType.REGULAR,
        ],
        compiler_params=pltpu.CompilerParams(
            collective_id=0, has_side_effects=True, vmem_limit_bytes=40 * 2**20
        ),
    )(*operands)
    return pl.pallas_call(
        finish,
        out_shape=(
            jax.ShapeDtypeStruct(tracers.shape, bf16),
            jax.ShapeDtypeStruct(ocean_u.shape, f32),
            jax.ShapeDtypeStruct(ocean_b.shape, f32),
        ),
        in_specs=[vmem] * 2,
        out_specs=(hbm, hbm, hbm),
        scratch_shapes=[pltpu.SemaphoreType.DMA((3,))],
        compiler_params=pltpu.CompilerParams(vmem_limit_bytes=2**20),
    )(*parts)


def solution(mesh):
    flat = ("sec", "tile")
    placed = (P(None, flat), P(None, flat), P(None, None, flat), P(), P())
    return jax.shard_map(
        on_device,
        mesh=mesh,
        in_specs=placed,
        out_specs=(P(None, None, flat), P(None, flat), P(None, flat)),
        check_vma=False,
    )
```

```python
import functools

import jax
import jax.numpy as jnp
from jax import lax
from jax.experimental import pallas as pl
from jax.experimental.pallas import tpu as pltpu
from jax.sharding import PartitionSpec as P

MESH = pl.DeviceIdType.MESH
LANES = 128
STEPS = 2
WET_DEV = 3
OCEAN_DEV = 4
HALO = 3

DT_OCEAN = 0.25
PRESSURE = 1.0
HORIZ_VISC = 0.2
VERT_VISC = 0.2
HEATING = 0.2
KAPPA_BASE = 0.05
KAPPA_SPAN = 0.35
DT_TRACER = 0.3
DT_MIX = 1.0
KINETIC_DELTA = 0.5
SURFACE_LIGHT = 10.0
WATER_ATT = 0.04
PIGMENT_ATT = 0.08
GROWTH = 0.05
THERMAL_GAIN = 0.1


def roll(x, shift, axis):
    size = x.shape[axis]
    shift = shift % size
    return x if shift == 0 else pltpu.roll(x, shift, axis)


def iota(shape, axis):
    return lax.broadcasted_iota(jnp.int32, shape, axis)


def pick(position, options):
    value = None
    for where, option in options:
        value = option if value is None else jnp.where(position == where, option, value)
    return value


def exact(a, b):
    return jnp.dot(a, b, precision=lax.Precision.HIGHEST, preferred_element_type=jnp.float32)


def absorbed_light(pigment, tri):
    attenuation = WATER_ATT + PIGMENT_ATT * pigment * pigment
    below = jnp.exp(-exact(tri, attenuation))
    above = jnp.where(iota(pigment.shape, 0) == 0, 1.0, roll(below, 1, 0))
    return SURFACE_LIGHT * (above - below)


def advance_velocity(velocity, buoyancy):
    level = iota(velocity.shape, 0)
    horiz = roll(velocity, 1, 1) + roll(velocity, -1, 1) - 2.0 * velocity
    press = roll(buoyancy, -1, 1) - buoyancy
    upper = jnp.where(level == 0, velocity, roll(velocity, 1, 0))
    lower = jnp.where(level == velocity.shape[0] - 1, velocity, roll(velocity, -1, 0))
    vert = upper + lower - 2.0 * velocity
    return velocity + DT_OCEAN * (HORIZ_VISC * horiz + VERT_VISC * vert - PRESSURE * press)


def diffusivity(shear, settled):
    steep = 4.0 * (shear * shear - settled)
    return KAPPA_BASE + KAPPA_SPAN / (1.0 + jnp.exp(-steep))


def set_coefficients(coef, face_u, warmth, gate):
    level = iota(face_u.shape, 0)
    shear = face_u - roll(face_u, -1, 0)
    stratified = warmth - roll(warmth, -1, 0)
    spreading = diffusivity(shear, stratified)
    spreading = jnp.where(level == face_u.shape[0] - 1, 0.0, spreading)
    spreading_up = jnp.where(level == 0, 0.0, roll(spreading, 1, 0))
    gate = DT_TRACER * gate
    forward = jnp.maximum(face_u, 0.0) * gate
    backward = jnp.minimum(face_u, 0.0) * gate
    coef[0] = 1.0 - forward + roll(backward, 1, 1)
    coef[1] = -backward
    coef[2] = roll(forward, 1, 1)
    coef[3] = 1.0 - DT_MIX * (spreading + spreading_up)
    coef[4] = DT_MIX * spreading
    coef[5] = DT_MIX * spreading_up
    coef[6] = KINETIC_DELTA * jnp.exp(THERMAL_GAIN * warmth)


def transport(state, coef, width):
    moved = (coef[0] * state + coef[1] * roll(state, -1, 1) + coef[2] * roll(state, 1, 1))[:, :width]
    return (
        coef[3][:, :width] * moved
        + coef[4][:, :width] * roll(moved, -1, 0)
        + coef[5][:, :width] * roll(moved, 1, 0)
    )


def react(mixed, warm, light, matrix, tracers):
    padded, rows, width = mixed.shape
    flat = mixed.reshape(padded * rows, width)
    high = flat.astype(jnp.bfloat16)
    low = (flat - high.astype(jnp.float32)).astype(jnp.bfloat16)
    drift = jnp.dot(
        matrix, jnp.concatenate([high, low, high], axis=0), preferred_element_type=jnp.float32
    ).reshape(padded, rows, width)
    grown = mixed + warm[None] * drift
    return jnp.concatenate([(grown[0] + GROWTH * light)[None], grown[1:tracers]], axis=0)


def kernel(
    secs, tiles, u_in, b_in, t_in, wet_in, k_in,
    out_v, ub_out,
    u_v, b_v, t_v, k_v, wet_s, edge_t, edge_ub, to_near, to_far, from_near, from_far, tile_in, tile_back,
    s_v, mix_v, abs_v, coef, pack_v, splat_v,
    load_sem, wet_sem, send_sem, recv_sem, far_ready, near_ready,
):
    levels = u_in.shape[0]
    tracers = t_in.shape[0]
    padded = mix_v.shape[0]
    total_wet = WET_DEV * secs * tiles
    total_tiles = OCEAN_DEV * secs * tiles
    own = OCEAN_DEV * LANES
    slots = WET_DEV * LANES
    sec = lax.axis_index("sec")
    tile = lax.axis_index("tile")
    device = sec * tiles + tile
    odd = lax.rem(tile, 2)
    even_lane = odd == 0
    partner = (sec, tile + 1 - 2 * odd)
    far_flat = lax.rem(device + 2 * odd - 1 + secs * tiles, secs * tiles)
    far = (far_flat // tiles, lax.rem(far_flat, tiles))

    slot_edge = pl.ds(pl.multiple_of((slots - LANES) * odd, LANES), LANES)
    far_edge = pl.ds(pl.multiple_of((own - LANES) * odd, LANES), LANES)
    near_edge = pl.ds(pl.multiple_of((own - LANES) * (1 - odd), LANES), LANES)
    loads = [
        pltpu.make_async_copy(u_in.at[:, far_edge], edge_ub.at[0], load_sem.at[0]),
        pltpu.make_async_copy(b_in.at[:, far_edge], edge_ub.at[1], load_sem.at[1]),
        pltpu.make_async_copy(t_in.at[16:, :, slot_edge], edge_t.at[16:], load_sem.at[2]),
        pltpu.make_async_copy(t_in.at[:8, :, slot_edge], edge_t.at[:8], load_sem.at[7]),
        pltpu.make_async_copy(t_in.at[8:16, :, slot_edge], edge_t.at[8:16], load_sem.at[8]),
        pltpu.make_async_copy(t_in, t_v, load_sem.at[3]),
        pltpu.make_async_copy(u_in, u_v.at[:, pl.ds(0, own)], load_sem.at[4]),
        pltpu.make_async_copy(b_in, b_v.at[:, pl.ds(0, own)], load_sem.at[5]),
        pltpu.make_async_copy(k_in, k_v, load_sem.at[6]),
        pltpu.make_async_copy(wet_in, wet_s, wet_sem),
    ]
    for load in loads[:5]:
        load.start()

    barrier = pltpu.get_barrier_semaphore()
    greeted = (jnp.where(even_lane, far[0], partner[0]), jnp.where(even_lane, far[1], partner[1]))
    pl.semaphore_signal(barrier, inc=1, device_id=greeted, device_id_type=MESH)
    for load in loads[5:]:
        load.start()

    def remote(src, dst, index, target):
        return pltpu.make_async_remote_copy(
            src_ref=src, dst_ref=dst, send_sem=send_sem.at[index], recv_sem=recv_sem.at[index],
            device_id=target, device_id_type=MESH,
        )

    pl.semaphore_wait(barrier, 1)

    @pl.when(odd == 1)
    def _():
        pl.semaphore_signal(far_ready, inc=1, device_id=far, device_id_type=MESH)

    @pl.when(odd == 0)
    def _():
        pl.semaphore_signal(near_ready, inc=1, device_id=partner, device_id_type=MESH)

    lane = iota((levels, LANES), 1)
    base = 2 * tracers
    thin = iota((8, LANES), 1)
    groups = levels // 8
    frame = (thin + (LANES - 8 + 2 * odd)) & (LANES - 1)
    last_frame = (thin + (LANES - 8 + HALO * odd)) & (LANES - 1)
    send_far = [
        remote(to_far.at[pl.ds(8 * p, 8), :], from_far.at[pl.ds(8 * p, 8), :], (0, 6, 7)[p], far) for p in range(3)
    ]
    for part in (2, 0, 1):
        for load in loads[3 + part : 4 + part] if part < 2 else loads[:3]:
            load.wait()
        spots = frame if part < 2 else last_frame
        within = spots & 15
        value = None
        for g in range(groups):
            level = slice(8 * g, 8 * g + 8)
            natural = 16 * g + 8
            if part < 2:
                chunk = None
                for k in range(8):
                    moved = roll(edge_t[8 * part + k, level, :].astype(jnp.float32), natural + 2 * k, 1)
                    chunk = moved if chunk is None else jnp.where(within >= 2 * k, moved, chunk)
            else:
                chunk = roll(edge_ub[0, level, :], natural, 1)
                chunk = jnp.where(within >= HALO, roll(edge_ub[1, level, :], natural + HALO, 1), chunk)
                moved = roll(edge_t[tracers - 1, level, :].astype(jnp.float32), natural + 2 * HALO, 1)
                chunk = jnp.where(within >= 2 * HALO, moved, chunk)
            value = chunk if value is None else jnp.where((spots >> 4) == g, chunk, value)
        to_far[8 * part : 8 * part + 8, :] = value

        @pl.when(odd == 1)
        def _(copy=send_far[part]):
            copy.start()

    @pl.when(odd == 1)
    def _():
        pl.semaphore_wait(near_ready, 1)

    tile_u = remote(u_in.at[:, near_edge], tile_in.at[0], 2, partner)
    tile_b = remote(b_in.at[:, near_edge], tile_in.at[1], 3, partner)
    tile_u.start()
    tile_b.start()

    for load in loads[5:8]:
        load.wait()
    message = jnp.zeros((levels, LANES), jnp.float32)
    for t in range(tracers):
        here = (lane >= 2 * t) & (lane < 2 * t + 2)
        near = jnp.where(even_lane, t_v[t, :, slots - LANES :], t_v[t, :, :LANES]).astype(jnp.float32)
        message = jnp.where(here, pltpu.roll(near, 2 * t + 2 - 2 * odd, 1), message)
    for field, offset in ((u_v, base), (b_v, base + HALO)):
        here = (lane >= offset) & (lane < offset + HALO)
        near = jnp.where(even_lane, field[:, 2 * LANES : 3 * LANES], field[:, LANES : 2 * LANES])
        message = jnp.where(here, pltpu.roll(near, offset + HALO - HALO * odd, 1), message)
    to_near[...] = message
    send_near = remote(to_near, from_near, 1, partner)
    send_near.start()

    loads[8].wait()
    rows = 8 * padded
    wide = 3 * rows
    spread = ((iota((rows, tracers), 0) >> 3) == iota((rows, tracers), 1)).astype(jnp.float32)
    column = iota((tracers, wide), 1)
    column = jnp.where(column >= 2 * rows, column - 2 * rows, jnp.where(column >= rows, column - rows, column))
    gather = ((column >> 3) == iota((tracers, wide), 0)).astype(jnp.float32)
    matrix = exact(exact(spread, k_v[...]), gather)
    same = (iota((rows, wide), 0) & 7) == (iota((rows, wide), 1) & 7)
    matrix = jnp.where(same, matrix, 0.0)
    coarse = matrix.astype(jnp.bfloat16).astype(jnp.float32)
    matrix = jnp.where(iota((rows, wide), 1) < 2 * rows, coarse, matrix - coarse).astype(jnp.bfloat16)
    mix_v[tracers, :, :] = jnp.zeros(mix_v.shape[1:], jnp.float32)
    for i in range(tracers):
        for k in range(tracers):
            splat_v[tracers * i + k] = jnp.broadcast_to(k_v[i : i + 1, k : k + 1], (8, LANES))

    for f in range(tracers + 2):
        value = None
        for g in range(groups):
            level = slice(8 * g, 8 * g + 8)
            part = edge_t[f, level, :].astype(jnp.float32) if f < tracers else edge_ub[f - tracers, level, :]
            moved = roll(part, 16 * g + 8, 1)
            value = moved if value is None else jnp.where((thin >> 4) == g, moved, value)
        pack_v[f] = value

    for t in range(tracers):
        s_v[t, :, :slots] = t_v[t].astype(jnp.float32)

    loads[9].wait()
    listed = [
        wet_s[lax.rem(device * WET_DEV + total_wet + j, total_wet)] for j in range(-1, WET_DEV + 1)
    ]
    ring = OCEAN_DEV + 2
    relative = [lax.rem(w - device * OCEAN_DEV + total_tiles + 2, total_tiles) - 2 for w in listed]
    position = [jnp.where(r < 0, r + ring, jnp.where(r < ring, r, ring)) for r in relative]
    is_open = [
        lax.rem(listed[j + 1] - listed[j] + total_tiles, total_tiles) == 1 for j in range(WET_DEV + 1)
    ]
    spot_left, spot, spot_right = position[0], position[1 : WET_DEV + 1], position[WET_DEV + 1]

    tri = (iota((levels, levels), 0) >= iota((levels, levels), 1)).astype(jnp.float32)
    abs_v[:, :slots] = absorbed_light(s_v[0, :, :slots], tri)

    send_near.wait_recv()
    halo_two = jnp.where(even_lane, lane, LANES - 1 - lane) < 2
    halo_three = jnp.where(even_lane, lane, LANES - 1 - lane) < HALO
    for t in range(tracers):
        came = pltpu.roll(from_near[...], 2 * LANES - 2 * t - 2 * odd, 1)
        s_v[t, :, slots:] = jnp.where(halo_two, came, 0.0)
    abs_v[:, slots:] = absorbed_light(s_v[0, :, slots:], tri)
    tile_u.wait_recv()
    tile_b.wait_recv()
    for field, offset, whole in ((u_v, base, tile_in[0]), (b_v, base + HALO, tile_in[1])):
        came = pltpu.roll(from_near[...], 2 * LANES - offset - HALO * odd, 1)
        near = jnp.where(halo_three, came, 0.0)
        field[:, own : own + LANES] = jnp.where(even_lane, whole, near)
        field[:, own + LANES :] = jnp.where(even_lane, near, whole)

    final = None
    for step in range(STEPS):
        width = slots + LANES if step < STEPS - 1 else slots
        light = [abs_v[:, j * LANES : (j + 1) * LANES] for j in range(WET_DEV + 1)]
        heat = []
        for q in range(ring):
            at_halo = jnp.where(lane < LANES // 2, spot_right, spot_left) == q
            term = jnp.where(at_halo, light[WET_DEV], 0.0)
            for j in range(WET_DEV):
                term = jnp.where(spot[j] == q, light[j], term)
            heat.append(term)
        buoyancy = b_v[...] + HEATING * jnp.concatenate(heat, axis=1)
        b_v[...] = buoyancy
        u_v[...] = advance_velocity(u_v[...], buoyancy)
        if step == STEPS - 1:
            place = pl.ds(pl.multiple_of(own + LANES * odd, LANES), LANES)
            final = (
                remote(u_v.at[:, place], tile_back.at[0], 4, partner),
                remote(b_v.at[:, place], tile_back.at[1], 5, partner),
            )
            for copy in final:
                copy.start()
        taken = []
        for field in (u_v, b_v):
            part = [field[:, q * LANES : (q + 1) * LANES] for q in range(ring)]
            chosen = [
                pick(spot[0], [(0, part[0]), (1, part[1]), (2, part[2]), (5, part[5])]),
                pick(spot[1], [(0, part[0]), (1, part[1]), (2, part[2]), (3, part[3])]),
                pick(spot[2], [(1, part[1]), (2, part[2]), (3, part[3]), (4, part[4])]),
            ]
            ahead = pick(spot_right, [(3, part[3]), (4, part[4]), (5, part[5])])
            behind = pick(spot_left, [(0, part[0]), (4, part[4]), (5, part[5])])
            chosen.append(jnp.where(lane < LANES // 2, ahead, behind))
            taken.append(jnp.concatenate(chosen, axis=1))
        gates = []
        for j in range(WET_DEV + 1):
            ends = is_open[(j + 1) % (WET_DEV + 1)].astype(jnp.float32)
            gates.append(jnp.where(lane == LANES - 1, ends, 1.0))
        set_coefficients(coef, taken[0], taken[1], jnp.concatenate(gates, axis=1))
        for t in range(tracers):
            mix_v[t, :, :width] = transport(s_v[t], coef, width)
        for group in range(levels // 16):
            halves = []
            for half in range(2):
                level = slice(group * 16 + half * 8, group * 16 + half * 8 + 8)
                grown = react(
                    mix_v[:, level, :width], coef[6, level, :width], abs_v[level, :width], matrix, tracers
                )
                if step < STEPS - 1:
                    s_v[:, level, :width] = grown
                halves.append(grown)
            if step == STEPS - 1:
                level = slice(group * 16, group * 16 + 16)
                out_v[:, level, :] = jnp.concatenate(halves, axis=1).astype(jnp.bfloat16)
        if step < STEPS - 1:
            abs_v[:, :width] = absorbed_light(s_v[0, :, :width], tri)

    @pl.when(odd == 0)
    def _():
        pl.semaphore_wait(far_ready, 1)
        for copy in send_far:
            copy.start()

    for copy in final:
        copy.wait_recv()
    for field, index in ((u_v, 0), (b_v, 1)):
        back = tile_back[index]
        low_given = jnp.logical_and(odd == 1, spot_left == 0)
        high_given = jnp.logical_and(odd == 0, spot_right == OCEAN_DEV - 1)
        ub_out[index, :, :LANES] = jnp.where(low_given, back, field[:, :LANES])
        ub_out[index, :, LANES : own - LANES] = field[:, LANES : own - LANES]
        ub_out[index, :, own - LANES :] = jnp.where(high_given, back, field[:, own - LANES : own])

    edge_wet = jnp.where(even_lane, relative[1] == 0, relative[WET_DEV] == OCEAN_DEV - 1)
    halo_wet = jnp.where(even_lane, relative[0] == -1, relative[WET_DEV + 1] == OCEAN_DEV)
    column = thin & 15
    distance = jnp.where(even_lane, column - 8, 7 - column)
    edge_wet, halo_wet = edge_wet.astype(jnp.float32), halo_wet.astype(jnp.float32)
    shape = (8, LANES)
    lane = thin
    row = iota(shape, 0)
    level = 8 * (lane >> 4) + row
    inside = jnp.where(even_lane, 7 - column, column - 8)
    halo_two = (inside >= 0) & (inside < 2)
    halo_three = (inside >= 0) & (inside < HALO)

    def above(x):
        turned = roll(x, 1, 0)
        return jnp.where(row == 0, roll(turned, 16, 1), turned)

    def below(x):
        turned = roll(x, -1, 0)
        return jnp.where(row == 7, roll(turned, -16, 1), turned)

    def total_from_top(x):
        for shift in (1, 2, 4):
            x = x + jnp.where(row >= shift, roll(x, shift, 0), 0.0)
        whole = jnp.broadcast_to(x[7:8], shape)
        parts = [jnp.where(lane >= 16 * k, roll(whole, 16 * k, 1), 0.0) for k in range(1, levels // 8)]
        while len(parts) > 1:
            parts = [sum(parts[k : k + 2]) for k in range(0, len(parts), 2)]
        return x + parts[0]

    lit = jnp.where(distance >= 0, edge_wet, halo_wet)
    gate = DT_TRACER * jnp.where(column == 7, edge_wet * halo_wet, 1.0)
    near_side = jnp.where(even_lane, lane, LANES - 1 - lane) < 4
    near_wet = jnp.concatenate([jnp.where(near_side, edge_wet, 0.0)] * 2, axis=0) > 0.5

    for copy in send_far:
        copy.wait_recv()
    state = []
    for t in range(tracers):
        part = from_far[8 * (t // 8) : 8 * (t // 8) + 8, :]
        came = roll(part, -2 * (t % 8) if t < 16 else -2 * HALO, 1)
        state.append(jnp.where(halo_two, came, pack_v[t]))
    fields = []
    for f in range(2):
        came = roll(from_far[16:24, :], -HALO * f, 1)
        fields.append(jnp.where(halo_three, came, pack_v[tracers + f]))
    velocity, buoyancy = fields
    for step in range(STEPS):
        attenuation = WATER_ATT + PIGMENT_ATT * state[0] * state[0]
        depth = total_from_top(attenuation)
        light = SURFACE_LIGHT * (jnp.exp(attenuation - depth) - jnp.exp(-depth))
        buoyancy = buoyancy + HEATING * lit * light
        horiz = roll(velocity, 1, 1) + roll(velocity, -1, 1) - 2.0 * velocity
        upper = jnp.where(level == 0, velocity, above(velocity))
        lower = jnp.where(level == levels - 1, velocity, below(velocity))
        press = roll(buoyancy, -1, 1) - buoyancy
        velocity = velocity + DT_OCEAN * (
            HORIZ_VISC * horiz + VERT_VISC * (upper + lower - 2.0 * velocity) - PRESSURE * press
        )
        shear, settled = velocity - below(velocity), buoyancy - below(buoyancy)
        spreading = jnp.where(level == levels - 1, 0.0, diffusivity(shear, settled))
        shear, settled = above(velocity) - velocity, above(buoyancy) - buoyancy
        spreading_up = jnp.where(level == 0, 0.0, diffusivity(shear, settled))
        forward = jnp.maximum(velocity, 0.0) * gate
        backward = jnp.minimum(velocity, 0.0) * gate
        stay = 1.0 - forward + roll(backward, 1, 1)
        from_left = roll(forward, 1, 1)
        keep = 1.0 - DT_MIX * (spreading + spreading_up)
        warm = KINETIC_DELTA * jnp.exp(THERMAL_GAIN * buoyancy)
        mixed = []
        for t in range(tracers):
            moved = stay * state[t] - backward * roll(state[t], -1, 1) + from_left * roll(state[t], 1, 1)
            mixed.append(
                keep * moved + DT_MIX * (spreading * below(moved) + spreading_up * above(moved))
            )
        state = []
        for t in range(tracers):
            sums = [splat_v[tracers * t + k] * mixed[k] for k in range(2)]
            for k in range(2, tracers):
                sums[k % 2] = sums[k % 2] + splat_v[tracers * t + k] * mixed[k]
            state.append(mixed[t] + warm * (sums[0] + sums[1]))
        state[0] = state[0] + GROWTH * light

    for f, field in enumerate((velocity, buoyancy)):
        for g in range(groups):
            rows = slice(8 * g, 8 * g + 8)
            kept = ub_out[f, rows, far_edge]
            ub_out[f, rows, far_edge] = jnp.where(near_side, roll(field, -16 * g - 8, 1), kept)
    for t in range(tracers):
        for g in range(levels // 16):
            rows = slice(16 * g, 16 * g + 16)
            fresh = jnp.concatenate(
                [roll(state[t], -32 * g - 8, 1), roll(state[t], -32 * g - 24, 1)], axis=0
            )
            kept = out_v[t, rows, slot_edge].astype(jnp.float32)
            out_v[t, rows, slot_edge] = jnp.where(near_wet, fresh, kept).astype(jnp.bfloat16)
    for copy in (send_near, tile_u, tile_b, *final, *send_far):
        copy.wait_send()


def finish(t_v, ub_v, t_out, u_out, b_out, sems):
    copies = [
        pltpu.make_async_copy(t_v, t_out, sems.at[0]),
        pltpu.make_async_copy(ub_v.at[0], u_out, sems.at[1]),
        pltpu.make_async_copy(ub_v.at[1], b_out, sems.at[2]),
    ]
    for copy in copies:
        copy.start()
    for copy in copies:
        copy.wait()


def on_device(ocean_u, ocean_b, tracers, wet_tiles, kinetic_matrix):
    levels, own = ocean_u.shape
    count, _, slots = tracers.shape
    padded = count + count % 2
    wide = slots + LANES
    domain = own + 2 * LANES
    f32, bf16 = jnp.float32, jnp.bfloat16
    hbm = pl.BlockSpec(memory_space=pltpu.HBM)
    vmem = pl.BlockSpec(memory_space=pltpu.VMEM)
    operands = [
        pltpu.with_memory_space_constraint(x, pltpu.HBM)
        for x in (ocean_u, ocean_b, tracers, wet_tiles, kinetic_matrix)
    ]
    parts = pl.pallas_call(
        functools.partial(kernel, lax.axis_size("sec"), lax.axis_size("tile")),
        out_shape=(
            jax.ShapeDtypeStruct(tracers.shape, bf16),
            jax.ShapeDtypeStruct((2, levels, own), f32),
        ),
        in_specs=[hbm] * 5,
        out_specs=(vmem,) * 2,
        scratch_shapes=[
            pltpu.VMEM((levels, domain), f32),
            pltpu.VMEM((levels, domain), f32),
            pltpu.VMEM(tracers.shape, bf16),
            pltpu.VMEM(kinetic_matrix.shape, f32),
            pltpu.SMEM(wet_tiles.shape, jnp.int32),
            pltpu.VMEM((count, levels, LANES), bf16),
            pltpu.VMEM((2, levels, LANES), f32),
            pltpu.VMEM((levels, LANES), f32),
            pltpu.VMEM((24, LANES), f32),
            pltpu.VMEM((levels, LANES), f32),
            pltpu.VMEM((24, LANES), f32),
            pltpu.VMEM((2, levels, LANES), f32),
            pltpu.VMEM((2, levels, LANES), f32),
            pltpu.VMEM((count, levels, wide), f32),
            pltpu.VMEM((padded, levels, wide), f32),
            pltpu.VMEM((levels, wide), f32),
            pltpu.VMEM((7, levels, wide), f32),
            pltpu.VMEM((count + 2, 8, LANES), f32),
            pltpu.VMEM((count * count, 8, LANES), f32),
            pltpu.SemaphoreType.DMA((9,)),
            pltpu.SemaphoreType.DMA,
            pltpu.SemaphoreType.DMA((8,)),
            pltpu.SemaphoreType.DMA((8,)),
            pltpu.SemaphoreType.REGULAR,
            pltpu.SemaphoreType.REGULAR,
        ],
        compiler_params=pltpu.CompilerParams(
            collective_id=0, has_side_effects=True, vmem_limit_bytes=40 * 2**20
        ),
    )(*operands)
    return pl.pallas_call(
        finish,
        out_shape=(
            jax.ShapeDtypeStruct(tracers.shape, bf16),
            jax.ShapeDtypeStruct(ocean_u.shape, f32),
            jax.ShapeDtypeStruct(ocean_b.shape, f32),
        ),
        in_specs=[vmem] * 2,
        out_specs=(hbm, hbm, hbm),
        scratch_shapes=[pltpu.SemaphoreType.DMA((3,))],
        compiler_params=pltpu.CompilerParams(vmem_limit_bytes=2**20),
    )(*parts)


def solution(mesh):
    flat = ("sec", "tile")
    placed = (P(None, flat), P(None, flat), P(None, None, flat), P(), P())
    return jax.shard_map(
        on_device,
        mesh=mesh,
        in_specs=placed,
        out_specs=(P(None, None, flat), P(None, flat), P(None, flat)),
        check_vma=False,
    )
```

```python
import functools

import jax
import jax.numpy as jnp
from jax import lax
from jax.experimental import pallas as pl
from jax.experimental.pallas import tpu as pltpu
from jax.sharding import PartitionSpec as P

MESH = pl.DeviceIdType.MESH
LANES = 128
STEPS = 2
WET_DEV = 3
OCEAN_DEV = 4
HALO = 3

DT_OCEAN = 0.25
PRESSURE = 1.0
HORIZ_VISC = 0.2
VERT_VISC = 0.2
HEATING = 0.2
KAPPA_BASE = 0.05
KAPPA_SPAN = 0.35
DT_TRACER = 0.3
DT_MIX = 1.0
KINETIC_DELTA = 0.5
SURFACE_LIGHT = 10.0
WATER_ATT = 0.04
PIGMENT_ATT = 0.08
GROWTH = 0.05
THERMAL_GAIN = 0.1


def roll(x, shift, axis):
    size = x.shape[axis]
    shift = shift % size
    return x if shift == 0 else pltpu.roll(x, shift, axis)


def iota(shape, axis):
    return lax.broadcasted_iota(jnp.int32, shape, axis)


def pick(position, options):
    value = None
    for where, option in options:
        value = option if value is None else jnp.where(position == where, option, value)
    return value


def exact(a, b):
    return jnp.dot(a, b, precision=lax.Precision.HIGHEST, preferred_element_type=jnp.float32)


def absorbed_light(pigment, tri):
    attenuation = WATER_ATT + PIGMENT_ATT * pigment * pigment
    below = jnp.exp(-exact(tri, attenuation))
    above = jnp.where(iota(pigment.shape, 0) == 0, 1.0, roll(below, 1, 0))
    return SURFACE_LIGHT * (above - below)


def advance_velocity(velocity, buoyancy):
    level = iota(velocity.shape, 0)
    horiz = roll(velocity, 1, 1) + roll(velocity, -1, 1) - 2.0 * velocity
    press = roll(buoyancy, -1, 1) - buoyancy
    upper = jnp.where(level == 0, velocity, roll(velocity, 1, 0))
    lower = jnp.where(level == velocity.shape[0] - 1, velocity, roll(velocity, -1, 0))
    vert = upper + lower - 2.0 * velocity
    return velocity + DT_OCEAN * (HORIZ_VISC * horiz + VERT_VISC * vert - PRESSURE * press)


def diffusivity(shear, settled):
    steep = 4.0 * (shear * shear - settled)
    return KAPPA_BASE + KAPPA_SPAN / (1.0 + jnp.exp(-steep))


def set_coefficients(coef, face_u, warmth, gate):
    level = iota(face_u.shape, 0)
    shear = face_u - roll(face_u, -1, 0)
    stratified = warmth - roll(warmth, -1, 0)
    spreading = diffusivity(shear, stratified)
    spreading = jnp.where(level == face_u.shape[0] - 1, 0.0, spreading)
    spreading_up = jnp.where(level == 0, 0.0, roll(spreading, 1, 0))
    gate = DT_TRACER * gate
    forward = jnp.maximum(face_u, 0.0) * gate
    backward = jnp.minimum(face_u, 0.0) * gate
    coef[0] = 1.0 - forward + roll(backward, 1, 1)
    coef[1] = -backward
    coef[2] = roll(forward, 1, 1)
    coef[3] = 1.0 - DT_MIX * (spreading + spreading_up)
    coef[4] = DT_MIX * spreading
    coef[5] = DT_MIX * spreading_up
    coef[6] = KINETIC_DELTA * jnp.exp(THERMAL_GAIN * warmth)


def transport(state, coef, width):
    moved = (coef[0] * state + coef[1] * roll(state, -1, 1) + coef[2] * roll(state, 1, 1))[:, :width]
    return (
        coef[3][:, :width] * moved
        + coef[4][:, :width] * roll(moved, -1, 0)
        + coef[5][:, :width] * roll(moved, 1, 0)
    )


def react(mixed, warm, light, matrix, tracers):
    padded, rows, width = mixed.shape
    flat = mixed.reshape(padded * rows, width)
    high = flat.astype(jnp.bfloat16)
    low = (flat - high.astype(jnp.float32)).astype(jnp.bfloat16)
    drift = jnp.dot(
        matrix, jnp.concatenate([high, low, high], axis=0), preferred_element_type=jnp.float32
    ).reshape(padded, rows, width)
    grown = mixed + warm[None] * drift
    return jnp.concatenate([(grown[0] + GROWTH * light)[None], grown[1:tracers]], axis=0)


def kernel(
    secs, tiles, u_in, b_in, t_in, wet_in, k_in,
    out_v, ub_out,
    u_v, b_v, t_v, k_v, wet_s, edge_t, edge_ub, to_near, to_far, from_near, from_far, tile_in, tile_back,
    s_v, mix_v, abs_v, coef, pack_v, splat_v,
    load_sem, wet_sem, send_sem, recv_sem, far_ready, near_ready,
):
    levels = u_in.shape[0]
    tracers = t_in.shape[0]
    padded = mix_v.shape[0]
    total_wet = WET_DEV * secs * tiles
    total_tiles = OCEAN_DEV * secs * tiles
    own = OCEAN_DEV * LANES
    slots = WET_DEV * LANES
    sec = lax.axis_index("sec")
    tile = lax.axis_index("tile")
    device = sec * tiles + tile
    odd = lax.rem(tile, 2)
    even_lane = odd == 0
    partner = (sec, tile + 1 - 2 * odd)
    far_flat = lax.rem(device + 2 * odd - 1 + secs * tiles, secs * tiles)
    far = (far_flat // tiles, lax.rem(far_flat, tiles))

    slot_edge = pl.ds(pl.multiple_of((slots - LANES) * odd, LANES), LANES)
    far_edge = pl.ds(pl.multiple_of((own - LANES) * odd, LANES), LANES)
    near_edge = pl.ds(pl.multiple_of((own - LANES) * (1 - odd), LANES), LANES)
    loads = [
        pltpu.make_async_copy(u_in.at[:, far_edge], edge_ub.at[0], load_sem.at[0]),
        pltpu.make_async_copy(b_in.at[:, far_edge], edge_ub.at[1], load_sem.at[1]),
        pltpu.make_async_copy(t_in.at[16:, :, slot_edge], edge_t.at[16:], load_sem.at[2]),
        pltpu.make_async_copy(t_in.at[:8, :, slot_edge], edge_t.at[:8], load_sem.at[7]),
        pltpu.make_async_copy(t_in.at[8:16, :, slot_edge], edge_t.at[8:16], load_sem.at[8]),
        pltpu.make_async_copy(t_in, t_v, load_sem.at[3]),
        pltpu.make_async_copy(u_in, u_v.at[:, pl.ds(0, own)], load_sem.at[4]),
        pltpu.make_async_copy(b_in, b_v.at[:, pl.ds(0, own)], load_sem.at[5]),
        pltpu.make_async_copy(k_in, k_v, load_sem.at[6]),
        pltpu.make_async_copy(wet_in, wet_s, wet_sem),
    ]
    for load in loads[:5]:
        load.start()

    barrier = pltpu.get_barrier_semaphore()
    greeted = (jnp.where(even_lane, far[0], partner[0]), jnp.where(even_lane, far[1], partner[1]))
    pl.semaphore_signal(barrier, inc=1, device_id=greeted, device_id_type=MESH)
    for load in loads[5:]:
        load.start()

    def remote(src, dst, index, target):
        return pltpu.make_async_remote_copy(
            src_ref=src, dst_ref=dst, send_sem=send_sem.at[index], recv_sem=recv_sem.at[index],
            device_id=target, device_id_type=MESH,
        )

    pl.semaphore_wait(barrier, 1)

    @pl.when(odd == 1)
    def _():
        pl.semaphore_signal(far_ready, inc=1, device_id=far, device_id_type=MESH)

    @pl.when(odd == 0)
    def _():
        pl.semaphore_signal(near_ready, inc=1, device_id=partner, device_id_type=MESH)

    lane = iota((levels, LANES), 1)
    base = 2 * tracers
    thin = iota((8, LANES), 1)
    groups = levels // 8
    frame = (thin + (LANES - 8 + 2 * odd)) & (LANES - 1)
    last_frame = (thin + (LANES - 8 + HALO * odd)) & (LANES - 1)
    send_far = [
        remote(to_far.at[pl.ds(8 * p, 8), :], from_far.at[pl.ds(8 * p, 8), :], (0, 6, 7)[p], far) for p in range(3)
    ]
    for part in (2, 0, 1):
        for load in loads[3 + part : 4 + part] if part < 2 else loads[:3]:
            load.wait()
        spots = frame if part < 2 else last_frame
        within = spots & 15
        value = None
        for g in range(groups):
            level = slice(8 * g, 8 * g + 8)
            natural = 16 * g + 8
            if part < 2:
                chunk = None
                for k in range(8):
                    moved = roll(edge_t[8 * part + k, level, :].astype(jnp.float32), natural + 2 * k, 1)
                    chunk = moved if chunk is None else jnp.where(within >= 2 * k, moved, chunk)
            else:
                chunk = roll(edge_ub[0, level, :], natural, 1)
                chunk = jnp.where(within >= HALO, roll(edge_ub[1, level, :], natural + HALO, 1), chunk)
                moved = roll(edge_t[tracers - 1, level, :].astype(jnp.float32), natural + 2 * HALO, 1)
                chunk = jnp.where(within >= 2 * HALO, moved, chunk)
            value = chunk if value is None else jnp.where((spots >> 4) == g, chunk, value)
        to_far[8 * part : 8 * part + 8, :] = value

        @pl.when(odd == 1)
        def _(copy=send_far[part]):
            copy.start()

    @pl.when(odd == 1)
    def _():
        pl.semaphore_wait(near_ready, 1)

    tile_u = remote(u_in.at[:, near_edge], tile_in.at[0], 2, partner)
    tile_b = remote(b_in.at[:, near_edge], tile_in.at[1], 3, partner)
    tile_u.start()
    tile_b.start()

    for load in loads[5:8]:
        load.wait()
    message = jnp.zeros((levels, LANES), jnp.float32)
    for t in range(tracers):
        here = (lane >= 2 * t) & (lane < 2 * t + 2)
        near = jnp.where(even_lane, t_v[t, :, slots - LANES :], t_v[t, :, :LANES]).astype(jnp.float32)
        message = jnp.where(here, pltpu.roll(near, 2 * t + 2 - 2 * odd, 1), message)
    for field, offset in ((u_v, base), (b_v, base + HALO)):
        here = (lane >= offset) & (lane < offset + HALO)
        near = jnp.where(even_lane, field[:, 2 * LANES : 3 * LANES], field[:, LANES : 2 * LANES])
        message = jnp.where(here, pltpu.roll(near, offset + HALO - HALO * odd, 1), message)
    to_near[...] = message
    send_near = remote(to_near, from_near, 1, partner)
    send_near.start()

    loads[8].wait()
    rows = 8 * padded
    wide = 3 * rows
    spread = ((iota((rows, tracers), 0) >> 3) == iota((rows, tracers), 1)).astype(jnp.float32)
    column = iota((tracers, wide), 1)
    column = jnp.where(column >= 2 * rows, column - 2 * rows, jnp.where(column >= rows, column - rows, column))
    gather = ((column >> 3) == iota((tracers, wide), 0)).astype(jnp.float32)
    matrix = exact(exact(spread, k_v[...]), gather)
    same = (iota((rows, wide), 0) & 7) == (iota((rows, wide), 1) & 7)
    matrix = jnp.where(same, matrix, 0.0)
    coarse = matrix.astype(jnp.bfloat16).astype(jnp.float32)
    matrix = jnp.where(iota((rows, wide), 1) < 2 * rows, coarse, matrix - coarse).astype(jnp.bfloat16)
    mix_v[tracers, :, :] = jnp.zeros(mix_v.shape[1:], jnp.float32)
    for i in range(tracers):
        for k in range(tracers):
            splat_v[tracers * i + k] = jnp.broadcast_to(k_v[i : i + 1, k : k + 1], (8, LANES))

    for f in range(tracers + 2):
        value = None
        for g in range(groups):
            level = slice(8 * g, 8 * g + 8)
            part = edge_t[f, level, :].astype(jnp.float32) if f < tracers else edge_ub[f - tracers, level, :]
            moved = roll(part, 16 * g + 8, 1)
            value = moved if value is None else jnp.where((thin >> 4) == g, moved, value)
        pack_v[f] = value

    for t in range(tracers):
        s_v[t, :, :slots] = t_v[t].astype(jnp.float32)

    loads[9].wait()
    listed = [
        wet_s[lax.rem(device * WET_DEV + total_wet + j, total_wet)] for j in range(-1, WET_DEV + 1)
    ]
    ring = OCEAN_DEV + 2
    relative = [lax.rem(w - device * OCEAN_DEV + total_tiles + 2, total_tiles) - 2 for w in listed]
    position = [jnp.where(r < 0, r + ring, jnp.where(r < ring, r, ring)) for r in relative]
    is_open = [
        lax.rem(listed[j + 1] - listed[j] + total_tiles, total_tiles) == 1 for j in range(WET_DEV + 1)
    ]
    spot_left, spot, spot_right = position[0], position[1 : WET_DEV + 1], position[WET_DEV + 1]

    tri = (iota((levels, levels), 0) >= iota((levels, levels), 1)).astype(jnp.float32)
    abs_v[:, :slots] = absorbed_light(s_v[0, :, :slots], tri)

    send_near.wait_recv()
    halo_two = jnp.where(even_lane, lane, LANES - 1 - lane) < 2
    halo_three = jnp.where(even_lane, lane, LANES - 1 - lane) < HALO
    for t in range(tracers):
        came = pltpu.roll(from_near[...], 2 * LANES - 2 * t - 2 * odd, 1)
        s_v[t, :, slots:] = jnp.where(halo_two, came, 0.0)
    abs_v[:, slots:] = absorbed_light(s_v[0, :, slots:], tri)
    tile_u.wait_recv()
    tile_b.wait_recv()
    for field, offset, whole in ((u_v, base, tile_in[0]), (b_v, base + HALO, tile_in[1])):
        came = pltpu.roll(from_near[...], 2 * LANES - offset - HALO * odd, 1)
        near = jnp.where(halo_three, came, 0.0)
        field[:, own : own + LANES] = jnp.where(even_lane, whole, near)
        field[:, own + LANES :] = jnp.where(even_lane, near, whole)

    final = None
    for step in range(STEPS):
        width = slots + LANES if step < STEPS - 1 else slots
        light = [abs_v[:, j * LANES : (j + 1) * LANES] for j in range(WET_DEV + 1)]
        heat = []
        for q in range(ring):
            at_halo = jnp.where(lane < LANES // 2, spot_right, spot_left) == q
            term = jnp.where(at_halo, light[WET_DEV], 0.0)
            for j in range(WET_DEV):
                term = jnp.where(spot[j] == q, light[j], term)
            heat.append(term)
        buoyancy = b_v[...] + HEATING * jnp.concatenate(heat, axis=1)
        b_v[...] = buoyancy
        u_v[...] = advance_velocity(u_v[...], buoyancy)
        if step == STEPS - 1:
            place = pl.ds(pl.multiple_of(own + LANES * odd, LANES), LANES)
            final = (
                remote(u_v.at[:, place], tile_back.at[0], 4, partner),
                remote(b_v.at[:, place], tile_back.at[1], 5, partner),
            )
            for copy in final:
                copy.start()
        taken = []
        for field in (u_v, b_v):
            part = [field[:, q * LANES : (q + 1) * LANES] for q in range(ring)]
            chosen = [
                pick(spot[0], [(0, part[0]), (1, part[1]), (2, part[2]), (5, part[5])]),
                pick(spot[1], [(0, part[0]), (1, part[1]), (2, part[2]), (3, part[3])]),
                pick(spot[2], [(1, part[1]), (2, part[2]), (3, part[3]), (4, part[4])]),
            ]
            ahead = pick(spot_right, [(3, part[3]), (4, part[4]), (5, part[5])])
            behind = pick(spot_left, [(0, part[0]), (4, part[4]), (5, part[5])])
            chosen.append(jnp.where(lane < LANES // 2, ahead, behind))
            taken.append(jnp.concatenate(chosen, axis=1))
        gates = []
        for j in range(WET_DEV + 1):
            ends = is_open[(j + 1) % (WET_DEV + 1)].astype(jnp.float32)
            gates.append(jnp.where(lane == LANES - 1, ends, 1.0))
        set_coefficients(coef, taken[0], taken[1], jnp.concatenate(gates, axis=1))
        for t in range(tracers):
            mix_v[t, :, :width] = transport(s_v[t], coef, width)
        for group in range(levels // 16):
            halves = []
            for half in range(2):
                level = slice(group * 16 + half * 8, group * 16 + half * 8 + 8)
                grown = react(
                    mix_v[:, level, :width], coef[6, level, :width], abs_v[level, :width], matrix, tracers
                )
                if step < STEPS - 1:
                    s_v[:, level, :width] = grown
                halves.append(grown)
            if step == STEPS - 1:
                level = slice(group * 16, group * 16 + 16)
                out_v[:, level, :] = jnp.concatenate(halves, axis=1).astype(jnp.bfloat16)
        if step < STEPS - 1:
            abs_v[:, :width] = absorbed_light(s_v[0, :, :width], tri)

    @pl.when(odd == 0)
    def _():
        pl.semaphore_wait(far_ready, 1)
        for copy in send_far:
            copy.start()

    for copy in final:
        copy.wait_recv()
    for field, index in ((u_v, 0), (b_v, 1)):
        back = tile_back[index]
        low_given = jnp.logical_and(odd == 1, spot_left == 0)
        high_given = jnp.logical_and(odd == 0, spot_right == OCEAN_DEV - 1)
        ub_out[index, :, :LANES] = jnp.where(low_given, back, field[:, :LANES])
        ub_out[index, :, LANES : own - LANES] = field[:, LANES : own - LANES]
        ub_out[index, :, own - LANES :] = jnp.where(high_given, back, field[:, own - LANES : own])

    edge_wet = jnp.where(even_lane, relative[1] == 0, relative[WET_DEV] == OCEAN_DEV - 1)
    halo_wet = jnp.where(even_lane, relative[0] == -1, relative[WET_DEV + 1] == OCEAN_DEV)
    column = thin & 15
    distance = jnp.where(even_lane, column - 8, 7 - column)
    edge_wet, halo_wet = edge_wet.astype(jnp.float32), halo_wet.astype(jnp.float32)
    shape = (8, LANES)
    lane = thin
    row = iota(shape, 0)
    level = 8 * (lane >> 4) + row
    inside = jnp.where(even_lane, 7 - column, column - 8)
    halo_two = (inside >= 0) & (inside < 2)
    halo_three = (inside >= 0) & (inside < HALO)

    def above(x):
        turned = roll(x, 1, 0)
        return jnp.where(row == 0, roll(turned, 16, 1), turned)

    def below(x):
        turned = roll(x, -1, 0)
        return jnp.where(row == 7, roll(turned, -16, 1), turned)

    def total_from_top(x):
        for shift in (1, 2, 4):
            x = x + jnp.where(row >= shift, roll(x, shift, 0), 0.0)
        whole = jnp.broadcast_to(x[7:8], shape)
        parts = [jnp.where(lane >= 16 * k, roll(whole, 16 * k, 1), 0.0) for k in range(1, levels // 8)]
        while len(parts) > 1:
            parts = [sum(parts[k : k + 2]) for k in range(0, len(parts), 2)]
        return x + parts[0]

    lit = jnp.where(distance >= 0, edge_wet, halo_wet)
    gate = DT_TRACER * jnp.where(column == 7, edge_wet * halo_wet, 1.0)
    near_side = jnp.where(even_lane, lane, LANES - 1 - lane) < 4
    near_wet = jnp.concatenate([jnp.where(near_side, edge_wet, 0.0)] * 2, axis=0) > 0.5

    def arrived(t):
        part = from_far[8 * (t // 8) : 8 * (t // 8) + 8, :]
        came = roll(part, -2 * (t % 8) if t < 16 else -2 * HALO, 1)
        return jnp.where(halo_two, came, pack_v[t])

    send_far[2].wait_recv()
    send_far[0].wait_recv()
    state = [arrived(t) for t in range(8)]
    fields = []
    for f in range(2):
        came = roll(from_far[16:24, :], -HALO * f, 1)
        fields.append(jnp.where(halo_three, came, pack_v[tracers + f]))
    velocity, buoyancy = fields
    for step in range(STEPS):
        attenuation = WATER_ATT + PIGMENT_ATT * state[0] * state[0]
        depth = total_from_top(attenuation)
        light = SURFACE_LIGHT * (jnp.exp(attenuation - depth) - jnp.exp(-depth))
        buoyancy = buoyancy + HEATING * lit * light
        horiz = roll(velocity, 1, 1) + roll(velocity, -1, 1) - 2.0 * velocity
        upper = jnp.where(level == 0, velocity, above(velocity))
        lower = jnp.where(level == levels - 1, velocity, below(velocity))
        press = roll(buoyancy, -1, 1) - buoyancy
        velocity = velocity + DT_OCEAN * (
            HORIZ_VISC * horiz + VERT_VISC * (upper + lower - 2.0 * velocity) - PRESSURE * press
        )
        shear, settled = velocity - below(velocity), buoyancy - below(buoyancy)
        spreading = jnp.where(level == levels - 1, 0.0, diffusivity(shear, settled))
        shear, settled = above(velocity) - velocity, above(buoyancy) - buoyancy
        spreading_up = jnp.where(level == 0, 0.0, diffusivity(shear, settled))
        forward = jnp.maximum(velocity, 0.0) * gate
        backward = jnp.minimum(velocity, 0.0) * gate
        stay = 1.0 - forward + roll(backward, 1, 1)
        from_left = roll(forward, 1, 1)
        keep = 1.0 - DT_MIX * (spreading + spreading_up)
        warm = KINETIC_DELTA * jnp.exp(THERMAL_GAIN * buoyancy)
        if step == 0:
            send_far[1].wait_recv()
            state += [arrived(t) for t in range(8, tracers)]
        mixed = []
        for t in range(tracers):
            moved = stay * state[t] - backward * roll(state[t], -1, 1) + from_left * roll(state[t], 1, 1)
            mixed.append(
                keep * moved + DT_MIX * (spreading * below(moved) + spreading_up * above(moved))
            )
        state = []
        for t in range(tracers):
            sums = [splat_v[tracers * t + k] * mixed[k] for k in range(2)]
            for k in range(2, tracers):
                sums[k % 2] = sums[k % 2] + splat_v[tracers * t + k] * mixed[k]
            state.append(mixed[t] + warm * (sums[0] + sums[1]))
        state[0] = state[0] + GROWTH * light

    for f, field in enumerate((velocity, buoyancy)):
        for g in range(groups):
            rows = slice(8 * g, 8 * g + 8)
            kept = ub_out[f, rows, far_edge]
            ub_out[f, rows, far_edge] = jnp.where(near_side, roll(field, -16 * g - 8, 1), kept)
    for t in range(tracers):
        for g in range(levels // 16):
            rows = slice(16 * g, 16 * g + 16)
            fresh = jnp.concatenate(
                [roll(state[t], -32 * g - 8, 1), roll(state[t], -32 * g - 24, 1)], axis=0
            )
            kept = out_v[t, rows, slot_edge].astype(jnp.float32)
            out_v[t, rows, slot_edge] = jnp.where(near_wet, fresh, kept).astype(jnp.bfloat16)
    for copy in (send_near, tile_u, tile_b, *final, *send_far):
        copy.wait_send()


def finish(t_v, ub_v, t_out, u_out, b_out, sems):
    copies = [
        pltpu.make_async_copy(t_v, t_out, sems.at[0]),
        pltpu.make_async_copy(ub_v.at[0], u_out, sems.at[1]),
        pltpu.make_async_copy(ub_v.at[1], b_out, sems.at[2]),
    ]
    for copy in copies:
        copy.start()
    for copy in copies:
        copy.wait()


def on_device(ocean_u, ocean_b, tracers, wet_tiles, kinetic_matrix):
    levels, own = ocean_u.shape
    count, _, slots = tracers.shape
    padded = count + count % 2
    wide = slots + LANES
    domain = own + 2 * LANES
    f32, bf16 = jnp.float32, jnp.bfloat16
    hbm = pl.BlockSpec(memory_space=pltpu.HBM)
    vmem = pl.BlockSpec(memory_space=pltpu.VMEM)
    operands = [
        pltpu.with_memory_space_constraint(x, pltpu.HBM)
        for x in (ocean_u, ocean_b, tracers, wet_tiles, kinetic_matrix)
    ]
    parts = pl.pallas_call(
        functools.partial(kernel, lax.axis_size("sec"), lax.axis_size("tile")),
        out_shape=(
            jax.ShapeDtypeStruct(tracers.shape, bf16),
            jax.ShapeDtypeStruct((2, levels, own), f32),
        ),
        in_specs=[hbm] * 5,
        out_specs=(vmem,) * 2,
        scratch_shapes=[
            pltpu.VMEM((levels, domain), f32),
            pltpu.VMEM((levels, domain), f32),
            pltpu.VMEM(tracers.shape, bf16),
            pltpu.VMEM(kinetic_matrix.shape, f32),
            pltpu.SMEM(wet_tiles.shape, jnp.int32),
            pltpu.VMEM((count, levels, LANES), bf16),
            pltpu.VMEM((2, levels, LANES), f32),
            pltpu.VMEM((levels, LANES), f32),
            pltpu.VMEM((24, LANES), f32),
            pltpu.VMEM((levels, LANES), f32),
            pltpu.VMEM((24, LANES), f32),
            pltpu.VMEM((2, levels, LANES), f32),
            pltpu.VMEM((2, levels, LANES), f32),
            pltpu.VMEM((count, levels, wide), f32),
            pltpu.VMEM((padded, levels, wide), f32),
            pltpu.VMEM((levels, wide), f32),
            pltpu.VMEM((7, levels, wide), f32),
            pltpu.VMEM((count + 2, 8, LANES), f32),
            pltpu.VMEM((count * count, 8, LANES), f32),
            pltpu.SemaphoreType.DMA((9,)),
            pltpu.SemaphoreType.DMA,
            pltpu.SemaphoreType.DMA((8,)),
            pltpu.SemaphoreType.DMA((8,)),
            pltpu.SemaphoreType.REGULAR,
            pltpu.SemaphoreType.REGULAR,
        ],
        compiler_params=pltpu.CompilerParams(
            collective_id=0, has_side_effects=True, vmem_limit_bytes=40 * 2**20
        ),
    )(*operands)
    return pl.pallas_call(
        finish,
        out_shape=(
            jax.ShapeDtypeStruct(tracers.shape, bf16),
            jax.ShapeDtypeStruct(ocean_u.shape, f32),
            jax.ShapeDtypeStruct(ocean_b.shape, f32),
        ),
        in_specs=[vmem] * 2,
        out_specs=(hbm, hbm, hbm),
        scratch_shapes=[pltpu.SemaphoreType.DMA((3,))],
        compiler_params=pltpu.CompilerParams(vmem_limit_bytes=2**20),
    )(*parts)


def solution(mesh):
    flat = ("sec", "tile")
    placed = (P(None, flat), P(None, flat), P(None, None, flat), P(), P())
    return jax.shard_map(
        on_device,
        mesh=mesh,
        in_specs=placed,
        out_specs=(P(None, None, flat), P(None, flat), P(None, flat)),
        check_vma=False,
    )
```
